32 devices in a mesh: dp: 8 (over z, x), seq: 4 (over y, core).
Axes of the slice: x: 2, y: 2, z: 4, core: 2. Of those that a mesh axis runs over, the one named last changes fastest.
Arguments:
- stream_in: bfloat16 [8, 1024, 512], P('dp', 'seq'), may hold values from -6 to 6
- residue_in: float32 [8, 1024, 512], P('dp', 'seq'), may hold values from -6 to 6
- segments: int32 [8, 1024], P('dp', 'seq'), may hold values from 0 to 7, never falling along the last dimension, each value on 1 to 512 neighbouring positions
- out_cot: float32 [8, 1024, 512], P('dp', 'seq'), may hold values from -6 to 6
- qkv_weight: bfloat16 [2, 512, 1536], P(None, ('dp', 'seq')), may hold values from -0.375 to 0.375
- out_weight: bfloat16 [2, 512, 512], P(None, ('dp', 'seq')), may hold values from -0.75 to 0.75
- ff_in_weight: bfloat16 [2, 512, 2048], P(None, ('dp', 'seq')), may hold values from -0.25 to 0.25
- ff_out_weight: bfloat16 [2, 2048, 512], P(None, ('dp', 'seq')), may hold values from -0.1875 to 0.1875
- att_bias: bfloat16 [2, 3, 512], P(None, None, ('dp', 'seq')), may hold values from -1.796875 to 1.796875
- ff_in_bias: bfloat16 [2, 2048], P(None, ('dp', 'seq')), may hold values from -1.796875 to 1.796875
- ff_out_bias: bfloat16 [2, 512], P(None, ('dp', 'seq')), may hold values from -1.796875 to 1.796875
- norm_gain: bfloat16 [2, 2, 512], P(None, None, ('dp', 'seq')), may hold values from 0.5 to 1.5
- norm_shift: bfloat16 [2, 2, 512], P(None, None, ('dp', 'seq')), may hold values from -1.796875 to 1.796875
- final_gain: bfloat16 [512], P(('dp', 'seq')), may hold values from 0.099609375 to 1.8984375
- final_shift: bfloat16 [512], P(('dp', 'seq')), may hold values from -1.796875 to 1.796875
Outputs:
- output: float32 [8, 1024, 512], P('dp', 'seq')
- stream_grad: float32 [8, 1024, 512], P('dp', 'seq')
- residue_grad: float32 [8, 1024, 512], P('dp', 'seq')
- qkv_weight_grad: float32 [2, 512, 1536], P(None, ('dp', 'seq'))
- out_weight_grad: float32 [2, 512, 512], P(None, ('dp', 'seq'))
- ff_in_weight_grad: float32 [2, 512, 2048], P(None, ('dp', 'seq'))
- ff_out_weight_grad: float32 [2, 2048, 512], P(None, ('dp', 'seq'))
- att_bias_grad: float32 [2, 3, 512], P(None, None, ('dp', 'seq'))
- ff_in_bias_grad: float32 [2, 2048], P(None, ('dp', 'seq'))
- ff_out_bias_grad: float32 [2, 512], P(None, ('dp', 'seq'))
- norm_gain_grad: float32 [2, 2, 512], P(None, None, ('dp', 'seq'))
- norm_shift_grad: float32 [2, 2, 512], P(None, None, ('dp', 'seq'))
- final_gain_grad: float32 [512], P(('dp', 'seq'))
- final_shift_grad: float32 [512], P(('dp', 'seq'))
The draws below stay inside these ranges and needn't reach their ends.
Inputs may be any that keep to these rules, and one draw needn't show every extreme that they name: `segments`: within each sequence the document numbers never fall; each of the 8 documents holds 1 to 512 consecutive tokens, and one holds exactly 512.
All inputs are finite; a program needn't handle non-finite values.
Results may differ from the reference program's by a relative error of at most 0.025.
Values may be sent and summed in bfloat16 or wider, within the bound.
A program may use at most 192 MiB of HBM per device.

```python
import math
import jax
import jax.numpy as jnp
import numpy as np
from jax import lax

D = 512
HEADS = 8
FF = 2048
LAYERS = 2
DOCS = 8
LENGTH = 1024
SEQS = 8
MOST_DOC = 512


def shard_levels(key, dims, cuts, low, largest):
    level, own = 1.0, jax.random.fold_in(key, 6)
    for position, blocks in cuts:
        draws = jnp.exp(jax.random.uniform(jax.random.fold_in(own, position), (blocks,), jnp.float32, low / len(cuts), largest / len(cuts)))
        level = level * jnp.repeat(draws, dims[position] // blocks).reshape([-1 if axis == position else 1 for axis in range(len(dims))])
    return level


def split_up(number_of, total, bound, slope):
    portions = [(1 << 20) // math.isqrt(grade ** slope) + 1 for grade in range(2, number_of + 1)]
    surplus, given = total - bound - (number_of - 1), [1] * (number_of - 1)
    while surplus > 0:
        movable = [i for i in range(number_of - 1) if given[i] < bound]
        pool, remaining = sum([portions[i] for i in movable]), surplus
        for i in movable:
            more = min(bound - given[i], max(1, remaining * portions[i] // pool), surplus)
            given[i] = given[i] + more
            surplus = surplus - more
    return np.array([bound] + given)


def ragged(stream_key, number_of, total, bound, lean):
    if number_of == 2:
        one = jax.random.randint(stream_key, (), max(1, total - bound), min(bound, total - 1) + 1)
        return jnp.stack([one, total - one])
    sizes = jnp.asarray(split_up(number_of, total, bound, lean), jnp.int32)
    couples = (number_of - 1) // 2
    giver, taker = sizes[1:1 + 2 * couples:2], sizes[2:2 + 2 * couples:2]
    margin = jnp.minimum(giver - 1, bound - taker)
    moved = jax.random.randint(jax.random.fold_in(stream_key, 1), (couples,), 0, 1 << 20) % (margin + 1)
    sizes = sizes.at[1:1 + 2 * couples:2].set(giver - moved).at[2:2 + 2 * couples:2].set(taker + moved)
    return sizes[jax.random.permutation(jax.random.fold_in(stream_key, 2), number_of)]


def bell_draw(stream_key, shape, scale, most, cuts=(), kind=jnp.bfloat16):
    entries = scale * jax.random.normal(stream_key, shape, jnp.float32)
    if cuts:
        entries = entries * shard_levels(stream_key, shape, cuts, -0.22, 0.18)
    return jnp.clip(entries, -most, most).astype(kind)


def setup_inputs(seed: int = 0) -> dict:
    keys = jax.random.split(jax.random.key(seed), 16)
    stream_in = bell_draw(keys[0], (SEQS, LENGTH, D), 1.0, 6.0, ((0, 8), (1, 4)))
    residue_in = bell_draw(keys[1], (SEQS, LENGTH, D), 1.0, 6.0, ((0, 8), (1, 4)), jnp.float32)
    segments = jax.vmap(lambda own: jnp.searchsorted(jnp.cumsum(ragged(own, DOCS, LENGTH, MOST_DOC, 2)), jnp.arange(LENGTH), side="right"))(jax.random.split(keys[2], SEQS)).reshape((SEQS, LENGTH)).astype(jnp.int32)
    out_cot = bell_draw(keys[3], (SEQS, LENGTH, D), 1.0, 6.0, ((0, 8), (1, 4)), jnp.float32)
    qkv_weight = bell_draw(keys[4], (LAYERS, D, 3 * D), (D // 2) ** -0.5, 0.375, ((1, 32),))
    out_weight = bell_draw(keys[5], (LAYERS, D, D), (D // 8) ** -0.5, 0.75, ((1, 32),))
    ff_in_weight = bell_draw(keys[6], (LAYERS, D, FF), D ** -0.5, 0.25, ((1, 32),))
    ff_out_weight = bell_draw(keys[7], (LAYERS, FF, D), (FF // 2) ** -0.5, 0.1875, ((1, 32),))
    att_bias = bell_draw(keys[8], (LAYERS, 3, D), 0.3, 1.796875, ((2, 32),))
    ff_in_bias = bell_draw(keys[9], (LAYERS, FF), 0.3, 1.796875, ((1, 32),))
    ff_out_bias = bell_draw(keys[10], (LAYERS, D), 0.3, 1.796875, ((1, 32),))
    norm_gain = jnp.clip(1.0 + 0.1 * jax.random.normal(keys[11], (LAYERS, 2, D), jnp.float32), 0.5, 1.5).astype(jnp.bfloat16)
    norm_shift = bell_draw(keys[12], (LAYERS, 2, D), 0.3, 1.796875, ((2, 32),))
    final_gain = jnp.clip(1.0 + 0.18 * jax.random.normal(keys[13], (D,), jnp.float32), 0.099609375, 1.8984375).astype(jnp.bfloat16)
    final_shift = bell_draw(keys[14], (D,), 0.3, 1.796875, ((0, 32),))
    return {"stream_in": stream_in, "residue_in": residue_in, "segments": segments, "out_cot": out_cot, "qkv_weight": qkv_weight, "out_weight": out_weight, "ff_in_weight": ff_in_weight, "ff_out_weight": ff_out_weight, "att_bias": att_bias, "ff_in_bias": ff_in_bias, "ff_out_bias": ff_out_bias, "norm_gain": norm_gain, "norm_shift": norm_shift, "final_gain": final_gain, "final_shift": final_shift}


@jax.custom_vjp
def low(v):
    return lax.optimization_barrier(v.astype(jnp.bfloat16)).astype(jnp.float32)

@jax.custom_vjp
def low_back(v):
    return v

def low_keep(v):
    return (low(v), None)

def low_pass(kept, grad):
    return (grad,)

def back_keep(v):
    return (v, None)

def back_low(kept, grad):
    return (low(grad),)
low.defvjp(low_keep, low_pass)
low_back.defvjp(back_keep, back_low)
precise = lax.Precision.HIGHEST
epsilon = 1e-05
masked_value = -1e+30

def product(left, right):
    return jnp.dot(left, right, precision=precise, preferred_element_type=jnp.float32)

def smooth_gate(values):
    return jax.nn.gelu(values, approximate=True)

def layer_norm(values, norm_gain, norm_shift):
    average = lax.optimization_barrier(jnp.mean(values, axis=-1, keepdims=True))
    centred = values - average
    variance = lax.optimization_barrier(jnp.mean(centred * centred, axis=-1, keepdims=True))
    return centred * lax.rsqrt(variance + epsilon) * norm_gain + norm_shift

def attend_rows(query_rows, query_pos, query_seg, keys_all, values_all, key_seg, key_pos):
    scaling = 1.0 / math.sqrt(query_rows.shape[-1])
    scores = jnp.einsum('qhd,khd->hqk', query_rows, keys_all, precision=precise) * scaling
    scores = low_back(scores)
    allowed = (query_seg[:, None] == key_seg[None, :]) & (key_pos[None, :] <= query_pos[:, None])
    scores = jnp.where(allowed[None], scores, masked_value)
    weights = low(jax.nn.softmax(scores, axis=-1))
    return jnp.einsum('hqk,khd->qhd', weights, values_all, precision=precise)

def sequence_forward(stream, residue, params, seg_row):
    qkv_weight, out_weight, ff_in_weight, ff_out_weight, att_bias, ff_in_bias, ff_out_bias, norm_gain, norm_shift, final_gain, final_shift = params
    length = stream.shape[0]
    features = stream.shape[1]
    head_size = features // HEADS
    positions = jnp.arange(length, dtype=jnp.int32)
    block_rows = math.gcd(length, 512)
    block_count = length // block_rows
    attend = jax.checkpoint(attend_rows)
    for number in range(qkv_weight.shape[0]):
        joined = product(low(stream), qkv_weight[number])
        queries = joined[:, :features] + att_bias[number, 0]
        keys_part = joined[:, features:2 * features]
        values_part = joined[:, 2 * features:] + att_bias[number, 1]
        joined = low(low_back(jnp.concatenate([queries, keys_part, values_part], axis=1)))
        split_heads = joined.reshape(length, 3, HEADS, head_size)
        queries3 = split_heads[:, 0]
        keys3 = split_heads[:, 1]
        values3 = split_heads[:, 2]

        def one_block(pieces):
            return attend(pieces[0], pieces[1], pieces[2], keys3, values3, seg_row, positions)
        mixed_heads = lax.map(one_block, (queries3.reshape(block_count, block_rows, HEADS, head_size), positions.reshape(block_count, block_rows), seg_row.reshape(block_count, block_rows)))
        attended = low(low_back(mixed_heads.reshape(length, features)))
        branch = low_back(product(attended, out_weight[number]) + att_bias[number, 2])
        middle = layer_norm(stream + branch, norm_gain[number, 0], norm_shift[number, 0])
        residue = residue + branch
        hidden = low_back(product(low(middle), ff_in_weight[number]) + ff_in_bias[number])
        active = low(smooth_gate(hidden))
        branch = low_back(product(active, ff_out_weight[number]) + ff_out_bias[number])
        stream = layer_norm(middle + branch, norm_gain[number, 1], norm_shift[number, 1])
        residue = residue + branch
    return stream + layer_norm(residue, final_gain, final_shift)

def add_pair(first_term, second_term):
    return first_term + second_term

def reference(stream_in, residue_in, segments, out_cot, qkv_weight, out_weight, ff_in_weight, ff_out_weight, att_bias, ff_in_bias, ff_out_bias, norm_gain, norm_shift, final_gain, final_shift):
    params = tuple((weight.astype(jnp.float32) for weight in (qkv_weight, out_weight, ff_in_weight, ff_out_weight, att_bias, ff_in_bias, ff_out_bias, norm_gain, norm_shift, final_gain, final_shift)))

    def one_sequence(totals, block_items):
        stream, residue, seg_row, cotangent = block_items

        def forward(stream_f, residue_f, params_f):
            return sequence_forward(stream_f, residue_f, params_f, seg_row)
        result, pullback = jax.vjp(forward, stream.astype(jnp.float32), residue, params)
        grad_stream, grad_residue, grad_params = pullback(cotangent)
        totals = jax.tree.map(add_pair, totals, grad_params)
        return (totals, (result, grad_stream, grad_residue))
    zero_sums = jax.tree.map(jnp.zeros_like, params)
    totals, (output, stream_grad, residue_grad) = lax.scan(one_sequence, zero_sums, (stream_in, residue_in, segments, out_cot))
    return (output, stream_grad, residue_grad, totals[0], totals[1], totals[2], totals[3], totals[4], totals[5], totals[6], totals[7], totals[8], totals[9], totals[10])
```

```python
import functools
import math

import jax
import jax.numpy as jnp
from jax import lax
from jax.experimental import pallas as pl
from jax.experimental.pallas import tpu as pltpu
from jax.sharding import PartitionSpec as P

HEADS = 8
MESH = pl.DeviceIdType.MESH


class Geometry:
    def __init__(self, mesh):
        self.dp, self.seq = mesh.shape["dp"], mesh.shape["seq"]
        self.ny = self.seq // 2
        self.nx = self.ny
        self.nz = self.dp // self.nx
        self.shards = self.dp * self.seq

    def here(self):
        dp, seq = lax.axis_index("dp"), lax.axis_index("seq")
        return lax.div(dp, self.nx), lax.rem(dp, self.nx), lax.div(seq, 2), lax.rem(seq, 2)

    def device(self, z, x, y, c):
        return (z * self.nx + x, y * 2 + c)

    def peers(self):
        z, x, y, c = self.here()
        found = [self.device(lax.rem(z + k, self.nz), x, y, c) for k in range(1, self.nz)]
        found += [self.device(z, lax.rem(x + k, self.nx), y, c) for k in range(1, self.nx)]
        found += [self.device(z, x, lax.rem(y + k, self.ny), c) for k in range(1, self.ny)]
        return found + [self.device(z, x, y, 1 - c)]


def greet(devices):
    barrier = pltpu.get_barrier_semaphore()
    for device in devices:
        pl.semaphore_signal(barrier, inc=1, device_id=device, device_id_type=MESH)
    pl.semaphore_wait(barrier, len(devices))


def remote(src, dst, send_sem, recv_sem, device):
    return pltpu.make_async_remote_copy(
        src_ref=src,
        dst_ref=dst,
        send_sem=send_sem,
        recv_sem=recv_sem,
        device_id=device,
        device_id_type=MESH,
    )


def gather_kernel(geo, cut, src, out, own_sem, *sems):
    z_send, z_recv, x_send, x_recv, y_send, y_recv, xd_send, xd_recv, yd_send, yd_recv, c_send, c_recv = sems
    z, x, y, c = geo.here()
    nz, nx, ny = geo.nz, geo.nx, geo.ny
    rows = src.shape[1]
    top, low = pl.ds(0, cut), pl.ds(cut, rows - cut)
    levels = src.shape[0]
    greet(geo.peers())

    def slot(l, zi, xi, yi):
        return out.at[l, zi, xi, yi, c]

    def z_copy(l, k):
        return remote(
            src.at[l], slot(l, z, x, y), z_send.at[l, k], z_recv.at[l, k],
            geo.device(lax.rem(z + k, nz), x, y, c),
        )

    def fan_copies(l, k, piece):
        zi = lax.rem(z + nz - k, nz)
        copies = []
        for j in range(1, nx):
            copies.append(remote(
                piece, slot(l, zi, x, y), x_send.at[l, k, j], x_recv.at[l, k, j],
                geo.device(z, lax.rem(x + j, nx), y, c),
            ))
        for j in range(1, ny):
            copies.append(remote(
                piece, slot(l, zi, x, y), y_send.at[l, k, j], y_recv.at[l, k, j],
                geo.device(z, x, lax.rem(y + j, ny), c),
            ))
        copies.append(remote(
            piece, slot(l, zi, x, y), c_send.at[l, k, 0, 0], c_recv.at[l, k, 0, 0],
            geo.device(z, x, y, 1 - c),
        ))
        return copies

    def to_sibling(l, k, i, j):
        zi, xi, yi = lax.rem(z + nz - k, nz), lax.rem(x + nx - i, nx), lax.rem(y + ny - j, ny)
        piece = slot(l, zi, xi, yi)
        return remote(
            piece, piece, c_send.at[l, k, i, j], c_recv.at[l, k, i, j], geo.device(z, x, y, 1 - c)
        )

    def x_forward(l, k, i, j):
        piece = out.at[l, lax.rem(z + nz - k, nz), x, lax.rem(y + ny - j, ny), c, low]
        return remote(
            piece, piece, xd_send.at[l, k, i, j], xd_recv.at[l, k, i, j],
            geo.device(z, lax.rem(x + i, nx), y, c),
        )

    def y_forward(l, k, i, j):
        piece = out.at[l, lax.rem(z + nz - k, nz), lax.rem(x + nx - i, nx), y, c, top]
        return remote(
            piece, piece, yd_send.at[l, k, i, j], yd_recv.at[l, k, i, j],
            geo.device(z, x, lax.rem(y + j, ny), c),
        )

    def first(l):
        pltpu.make_async_copy(src.at[l], slot(l, z, x, y), own_sem.at[l]).start()
        for k in range(1, nz):
            z_copy(l, k).start()
        for copy in fan_copies(l, 0, src.at[l]):
            copy.start()

    def second(l):
        for k in range(1, nz):
            z_copy(l, k).wait_recv()
            for copy in fan_copies(l, k, slot(l, lax.rem(z + nz - k, nz), x, y)):
                copy.start()

    def third(l):
        for k in range(nz):
            copies = fan_copies(l, k, slot(l, lax.rem(z + nz - k, nz), x, y))
            for j in range(1, ny):
                copies[nx - 1 + j - 1].wait_recv()
                for i in range(1, nx):
                    x_forward(l, k, i, j).start()
                to_sibling(l, k, 0, j).start()
            for i in range(1, nx):
                copies[i - 1].wait_recv()
                for j in range(1, ny):
                    y_forward(l, k, i, j).start()
                to_sibling(l, k, i, 0).start()

    def fourth(l):
        for k in range(nz):
            for i in range(1, nx):
                for j in range(1, ny):
                    x_forward(l, k, i, j).wait_recv()
                    y_forward(l, k, i, j).wait_recv()
                    to_sibling(l, k, i, j).start()

    def last(l):
        pltpu.make_async_copy(src.at[l], slot(l, z, x, y), own_sem.at[l]).wait()
        for k in range(1, nz):
            z_copy(l, k).wait_send()
        for k in range(nz):
            copies = fan_copies(l, k, slot(l, z, x, y))
            for copy in copies:
                copy.wait_send()
            copies[-1].wait_recv()
            for i in range(nx):
                for j in range(ny):
                    if i or j:
                        to_sibling(l, k, i, j).wait()
                    if i and j:
                        x_forward(l, k, i, j).wait_send()
                        y_forward(l, k, i, j).wait_send()

    first(0)
    second(0)
    for l in range(1, levels):
        first(l)
        third(l - 1)
        second(l)
        fourth(l - 1)
    third(levels - 1)
    fourth(levels - 1)
    for l in range(levels):
        last(l)


def gather_all(geo, packed, cut):
    levels, rows, columns = packed.shape
    nz, nx, ny = geo.nz, geo.nx, geo.ny
    dma = pltpu.SemaphoreType.DMA
    out = pl.pallas_call(
        functools.partial(gather_kernel, geo, cut),
        out_shape=jax.ShapeDtypeStruct((levels, nz, nx, ny, 2, rows, columns), packed.dtype),
        in_specs=[pl.BlockSpec(memory_space=pl.ANY)],
        out_specs=pl.BlockSpec(memory_space=pl.ANY),
        scratch_shapes=[dma((levels,))]
        + [dma((levels, nz))] * 2
        + [dma((levels, nz, nx))] * 2
        + [dma((levels, nz, ny))] * 2
        + [dma((levels, nz, nx, ny))] * 6,
        compiler_params=pltpu.CompilerParams(collective_id=0, has_side_effects=True),
        name="gather_all",
    )(packed)
    return out.reshape(levels, geo.shards, rows, columns)


def scatter_kernel(geo, half, g, small, out, small_out, own, r0, r1h, r1l, r2h, r2l, zin, sbuf, sin, *sems):
    own_sem, s0, d0, s1h, d1h, s1l, d1l, s2h, d2h, s2l, d2l, zs, zd, ss, sd = sems
    z, x, y, c = geo.here()
    nz, nx, ny = geo.nz, geo.nx, geo.ny
    levels = g.shape[0]
    rows = g.shape[5]
    top, low = pl.ds(0, half), pl.ds(half, rows - half)
    sibling = geo.device(z, x, y, 1 - c)
    greet(geo.peers())
    groups = [(l, k) for l in reversed(range(levels)) for k in list(range(1, nz)) + [0]]

    def wide(ref):
        return ref.astype(jnp.float32)

    def load(l, k):
        return pltpu.make_async_copy(g.at[l, lax.rem(z + k, nz), :, :, c], own.at[l, k], own_sem.at[l, k])

    def cross(l, k):
        return remote(
            g.at[l, lax.rem(z + k, nz), :, :, 1 - c], r0.at[l, k], s0.at[l, k], d0.at[l, k], sibling
        )

    def one(l, k):
        copies = []
        for j in range(1, ny):
            other = lax.rem(y + j, ny)
            copies.append(remote(
                own.at[l, k, :, other, top], r1h.at[l, k, j - 1], s1h.at[l, k, j - 1], d1h.at[l, k, j - 1],
                geo.device(z, x, other, c),
            ))
        for i in range(1, nx):
            other = lax.rem(x + i, nx)
            copies.append(remote(
                own.at[l, k, other, :, low], r1l.at[l, k, i - 1], s1l.at[l, k, i - 1], d1l.at[l, k, i - 1],
                geo.device(z, other, y, c),
            ))
        return copies

    def two(l, k):
        copies = []
        for i in range(1, nx):
            other = lax.rem(x + i, nx)
            copies.append(remote(
                own.at[l, k, other, y, top], r2h.at[l, k, i - 1], s2h.at[l, k, i - 1], d2h.at[l, k, i - 1],
                geo.device(z, other, y, c),
            ))
        for j in range(1, ny):
            other = lax.rem(y + j, ny)
            copies.append(remote(
                own.at[l, k, x, other, low], r2l.at[l, k, j - 1], s2l.at[l, k, j - 1], d2l.at[l, k, j - 1],
                geo.device(z, x, other, c),
            ))
        return copies

    def three(l, k):
        return remote(
            own.at[l, k, x, y], zin.at[l, k - 1], zs.at[l, k - 1], zd.at[l, k - 1],
            geo.device(lax.rem(z + k, nz), x, y, c),
        )

    def step_one(l, k):
        load(l, k).wait()
        cross(l, k).wait_recv()
        for i in range(nx):
            for j in range(ny):
                own[l, k, i, j] = (wide(own[l, k, i, j]) + wide(r0[l, k, i, j])).astype(own.dtype)
        for copy in one(l, k):
            copy.start()

    def step_two(l, k):
        for copy in one(l, k):
            copy.wait_recv()
        for i in range(nx):
            total = wide(own[l, k, i, y, top])
            for j in range(1, ny):
                total = total + wide(r1h[l, k, j - 1, i])
            own[l, k, i, y, top] = total.astype(own.dtype)
        for j in range(ny):
            total = wide(own[l, k, x, j, low])
            for i in range(1, nx):
                total = total + wide(r1l[l, k, i - 1, j])
            own[l, k, x, j, low] = total.astype(own.dtype)
        for copy in two(l, k):
            copy.start()

    def step_three(l, k):
        for copy in two(l, k):
            copy.wait_recv()
        total = wide(own[l, k, x, y, top])
        for i in range(1, nx):
            total = total + wide(r2h[l, k, i - 1])
        other = wide(own[l, k, x, y, low])
        for j in range(1, ny):
            other = other + wide(r2l[l, k, j - 1])
        if k:
            own[l, k, x, y, top] = total.astype(own.dtype)
            own[l, k, x, y, low] = other.astype(own.dtype)
            three(l, k).start()
        else:
            out[l, top] = total
            out[l, low] = other

    def finish(l):
        total = out[l]
        for k in range(1, nz):
            three(l, k).wait_recv()
            total = total + wide(zin[l, k - 1])
        out[l] = total

    lines = [
        [sibling],
        [geo.device(z, lax.rem(x + i, nx), y, c) for i in range(1, nx)],
        [geo.device(z, x, lax.rem(y + j, ny), c) for j in range(1, ny)],
        [geo.device(lax.rem(z + k, nz), x, y, c) for k in range(1, nz)],
    ]
    widest = max(len(line) for line in lines)

    def small_copies(p):
        return [
            remote(sbuf.at[p], sin.at[p, n], ss.at[p, n], sd.at[p, n], device)
            for n, device in enumerate(lines[p])
        ]

    def small_start(p, value):
        sbuf[p] = value
        for copy in small_copies(p):
            copy.start()

    def small_sum(p):
        total = sbuf[p]
        for n, copy in enumerate(small_copies(p)):
            copy.wait_recv()
            total = total + sin[p, n]
        return total

    for l, k in groups:
        load(l, k).start()
        cross(l, k).start()
    small_start(0, small[...])
    for t in range(len(groups) + 2):
        if t < len(groups):
            step_one(*groups[t])
        if 1 <= t <= len(groups):
            step_two(*groups[t - 1])
        if t >= 2:
            step_three(*groups[t - 2])
        if t < 3:
            small_start(t + 1, small_sum(t))
        elif t == 3:
            small_out[...] = small_sum(3)
    for l in reversed(range(levels)):
        finish(l)
    for l, k in groups:
        cross(l, k).wait_send()
        for copy in one(l, k) + two(l, k):
            copy.wait_send()
        if k:
            three(l, k).wait_send()
    for p in range(4):
        for copy in small_copies(p):
            copy.wait_send()


def scatter_all(geo, grads, small, half):
    levels, shards, rows, columns = grads.shape
    nz, nx, ny = geo.nz, geo.nx, geo.ny
    dma, vmem = pltpu.SemaphoreType.DMA, pltpu.VMEM
    kind = grads.dtype
    widest = max(1, nx - 1, ny - 1, nz - 1)
    return pl.pallas_call(
        functools.partial(scatter_kernel, geo, half),
        out_shape=(
            jax.ShapeDtypeStruct((levels, rows, columns), jnp.float32),
            jax.ShapeDtypeStruct(small.shape, jnp.float32),
        ),
        in_specs=[pl.BlockSpec(memory_space=pl.ANY), pl.BlockSpec(memory_space=pltpu.VMEM)],
        out_specs=(pl.BlockSpec(memory_space=pltpu.VMEM), pl.BlockSpec(memory_space=pltpu.VMEM)),
        scratch_shapes=[
            vmem((levels, nz, nx, ny, rows, columns), kind),
            vmem((levels, nz, nx, ny, rows, columns), kind),
            vmem((levels, nz, ny - 1, nx, half, columns), kind),
            vmem((levels, nz, nx - 1, ny, rows - half, columns), kind),
            vmem((levels, nz, nx - 1, half, columns), kind),
            vmem((levels, nz, ny - 1, rows - half, columns), kind),
            vmem((levels, nz - 1, rows, columns), kind),
            vmem((4,) + small.shape, jnp.float32),
            vmem((4, widest) + small.shape, jnp.float32),
            dma((levels, nz)),
        ]
        + [dma((levels, nz))] * 2
        + [dma((levels, nz, ny - 1))] * 2
        + [dma((levels, nz, nx - 1))] * 2
        + [dma((levels, nz, nx - 1))] * 2
        + [dma((levels, nz, ny - 1))] * 2
        + [dma((levels, nz - 1))] * 2
        + [dma((4, widest))] * 2,
        compiler_params=pltpu.CompilerParams(
            collective_id=1, has_side_effects=True, vmem_limit_bytes=60 << 20
        ),
        name="scatter_all",
    )(grads.reshape(levels, nz, nx, ny, 2, rows, columns), small)


epsilon = 1e-05
masked_value = -1e30


def smooth_gate(values):
    return jax.nn.gelu(values, approximate=True)


def layer_norm(values, norm_gain, norm_shift):
    average = jnp.mean(values, axis=-1, keepdims=True)
    centred = values - average
    variance = jnp.mean(centred * centred, axis=-1, keepdims=True)
    return centred * lax.rsqrt(variance + epsilon) * norm_gain + norm_shift


def keep_state(carried):
    return carried


def allowed_pairs(query_pos, query_seg, key_pos, key_seg):
    return (query_seg[:, None] == key_seg[None, :]) & (key_pos[None, :] <= query_pos[:, None])


def block_needed(query_pos, query_seg, key_pos, key_seg):
    return (key_pos[0] <= query_pos[-1]) & (key_seg[-1] >= query_seg[0])


def key_blocks(keys_values, key_seg):
    length = keys_values.shape[0]
    features = keys_values.shape[1] // 2
    head_size = features // HEADS
    block_rows = math.gcd(length, 512)
    block_count = length // block_rows
    split_kv = keys_values.reshape(block_count, block_rows, 2, HEADS, head_size)
    key_pos = jnp.arange(length, dtype=jnp.int32).reshape(block_count, block_rows)
    return (split_kv[:, :, 0], split_kv[:, :, 1], key_pos, key_seg.reshape(block_count, block_rows))


def block_scores(queries3, key_block, query_pos, query_seg, key_pos, key_seg):
    scaling = 1.0 / math.sqrt(queries3.shape[-1])
    raw_scores = (
        jnp.einsum("qhd,khd->hqk", queries3, key_block, preferred_element_type=jnp.float32)
        * scaling
    )
    return (raw_scores, allowed_pairs(query_pos, query_seg, key_pos, key_seg)[None])


def attention_forward(queries3, blocks, query_pos, query_seg):
    tokens, head_count, head_size = queries3.shape

    def statistics(carried, block_items):
        key_block, value_block, key_pos, key_seg = block_items

        def statistics_compute(running):
            run_max, run_sum = running
            raw_scores, allowed = block_scores(
                queries3, key_block, query_pos, query_seg, key_pos, key_seg
            )
            new_max = jnp.maximum(
                run_max, jnp.max(jnp.where(allowed, raw_scores, masked_value), axis=-1)
            )
            exp_terms = jnp.exp(jnp.where(allowed, raw_scores - new_max[..., None], masked_value))
            return (new_max, run_sum * jnp.exp(run_max - new_max) + jnp.sum(exp_terms, axis=-1))

        needed = block_needed(query_pos, query_seg, key_pos, key_seg)
        return (lax.cond(needed, statistics_compute, keep_state, carried), None)

    initial = (
        jnp.full((head_count, tokens), masked_value, jnp.float32),
        jnp.zeros((head_count, tokens), jnp.float32),
    )
    (run_max, run_sum), unused = lax.scan(statistics, initial, blocks)
    log_total = run_max + jnp.log(run_sum)

    def accumulate(carried, block_items):
        key_block, value_block, key_pos, key_seg = block_items

        def accumulate_compute(running):
            raw_scores, allowed = block_scores(
                queries3, key_block, query_pos, query_seg, key_pos, key_seg
            )
            weights = jnp.exp(jnp.where(allowed, raw_scores - log_total[..., None], masked_value))
            weights = weights.astype(jnp.bfloat16)
            return running + jnp.einsum(
                "hqk,khd->qhd", weights, value_block, preferred_element_type=jnp.float32
            )

        needed = block_needed(query_pos, query_seg, key_pos, key_seg)
        return (lax.cond(needed, accumulate_compute, keep_state, carried), None)

    mixed_heads, unused = lax.scan(
        accumulate, jnp.zeros((tokens, head_count, head_size), jnp.float32), blocks
    )
    return (mixed_heads, log_total)


def attention_backward(queries3, blocks, query_pos, query_seg, log_total, mixed_heads, grad_heads):
    tokens, head_count, head_size = queries3.shape
    scaling = 1.0 / math.sqrt(head_size)
    row_dots = jnp.sum(mixed_heads * grad_heads.astype(jnp.float32), axis=-1).T
    block_rows = blocks[0].shape[1]
    block_count = blocks[0].shape[0]

    def backward_step(grad_queries, block_items):
        key_block, value_block, key_pos, key_seg = block_items

        def backward_compute(running):
            raw_scores, allowed = block_scores(
                queries3, key_block, query_pos, query_seg, key_pos, key_seg
            )
            prob_values = jnp.exp(
                jnp.where(allowed, raw_scores - log_total[..., None], masked_value)
            )
            grad_values = jnp.einsum(
                "hqk,qhd->khd",
                prob_values.astype(jnp.bfloat16),
                grad_heads,
                preferred_element_type=jnp.float32,
            )
            grad_probs = jnp.einsum(
                "qhd,khd->hqk", grad_heads, value_block, preferred_element_type=jnp.float32
            )
            grad_scores = (prob_values * (grad_probs - row_dots[..., None])).astype(jnp.bfloat16)
            running = (
                running
                + jnp.einsum(
                    "hqk,khd->qhd", grad_scores, key_block, preferred_element_type=jnp.float32
                )
                * scaling
            )
            grad_keys = (
                jnp.einsum(
                    "hqk,qhd->khd", grad_scores, queries3, preferred_element_type=jnp.float32
                )
                * scaling
            )
            return (running, grad_keys, grad_values)

        def skip_block(running):
            empty_rows = jnp.zeros((block_rows, head_count, head_size), jnp.float32)
            return (running, empty_rows, empty_rows)

        needed = block_needed(query_pos, query_seg, key_pos, key_seg)
        grad_queries, grad_keys, grad_values = lax.cond(
            needed, backward_compute, skip_block, grad_queries
        )
        return (grad_queries, (grad_keys, grad_values))

    initial = jnp.zeros((tokens, head_count, head_size), jnp.float32)
    grad_queries, (grad_keys, grad_values) = lax.scan(backward_step, initial, blocks)
    length = block_count * block_rows
    return (
        grad_queries.reshape(tokens, head_count * head_size),
        grad_keys.reshape(length, head_count * head_size),
        grad_values.reshape(length, head_count * head_size),
    )


def layer_forward(stream, residue, weights, query_pos, query_seg, key_seg):
    (
        qkv_weight,
        out_weight,
        ff_in_weight,
        ff_out_weight,
        att_bias,
        ff_in_bias,
        ff_out_bias,
        norm_gain,
        norm_shift,
    ) = weights[:9]
    tokens, features = stream.shape
    stream_low = stream.astype(jnp.bfloat16)
    bias_row = jnp.concatenate([att_bias[0], jnp.zeros_like(att_bias[0]), att_bias[1]]).astype(
        jnp.float32
    )
    joined = (
        jnp.dot(stream_low, qkv_weight, preferred_element_type=jnp.float32) + bias_row
    ).astype(jnp.bfloat16)
    queries3 = joined[:, :features].reshape(tokens, HEADS, features // HEADS)
    keys_values = lax.all_gather(joined[:, features:], "seq", axis=0, tiled=True)
    blocks = key_blocks(keys_values, key_seg)
    mixed_heads, log_total = attention_forward(queries3, blocks, query_pos, query_seg)
    attended = mixed_heads.reshape(tokens, features).astype(jnp.bfloat16)
    branch_att = jnp.dot(attended, out_weight, preferred_element_type=jnp.float32) + att_bias[
        2
    ].astype(jnp.float32)
    middle, pull_first = jax.vjp(
        layer_norm,
        stream + branch_att,
        norm_gain[0].astype(jnp.float32),
        norm_shift[0].astype(jnp.float32),
    )
    residue_mid = residue + branch_att
    middle_low = middle.astype(jnp.bfloat16)
    hidden = jnp.dot(
        middle_low, ff_in_weight, preferred_element_type=jnp.float32
    ) + ff_in_bias.astype(jnp.float32)
    active = smooth_gate(hidden).astype(jnp.bfloat16)
    branch_ff = jnp.dot(
        active, ff_out_weight, preferred_element_type=jnp.float32
    ) + ff_out_bias.astype(jnp.float32)
    stream_next, pull_second = jax.vjp(
        layer_norm,
        middle + branch_ff,
        norm_gain[1].astype(jnp.float32),
        norm_shift[1].astype(jnp.float32),
    )
    saved_state = (
        stream_low,
        queries3,
        blocks,
        mixed_heads,
        log_total,
        attended,
        pull_first,
        middle_low,
        hidden,
        active,
        pull_second,
    )
    return (stream_next, residue_mid + branch_ff, saved_state)


def layer_backward(saved_state, weights, grad_stream, grad_residue, query_pos, query_seg):
    (
        stream_low,
        queries3,
        blocks,
        mixed_heads,
        log_total,
        attended,
        pull_first,
        middle_low,
        hidden,
        active,
        pull_second,
    ) = saved_state
    qkv_weight, out_weight, ff_in_weight, ff_out_weight = weights[:4]
    grad_second, gain_second, shift_second = pull_second(grad_stream)
    grad_ff = (grad_second + grad_residue).astype(jnp.bfloat16)
    grad_ff_out = jnp.einsum("tf,td->fd", active, grad_ff, preferred_element_type=jnp.float32)
    bias_ff_out = jnp.sum(grad_ff.astype(jnp.float32), axis=0)
    grad_active = jnp.einsum(
        "td,fd->tf", grad_ff, ff_out_weight, preferred_element_type=jnp.float32
    )
    unused_gate, pull_gate = jax.vjp(smooth_gate, hidden)
    grad_hidden = pull_gate(grad_active)[0].astype(jnp.bfloat16)
    grad_ff_in = jnp.einsum(
        "td,tf->df", middle_low, grad_hidden, preferred_element_type=jnp.float32
    )
    bias_ff_in = jnp.sum(grad_hidden.astype(jnp.float32), axis=0)
    grad_middle = grad_second + jnp.einsum(
        "tf,df->td", grad_hidden, ff_in_weight, preferred_element_type=jnp.float32
    )
    grad_first, gain_first, shift_first = pull_first(grad_middle)
    grad_att = (grad_first + grad_residue).astype(jnp.bfloat16)
    grad_out = jnp.einsum("te,td->ed", attended, grad_att, preferred_element_type=jnp.float32)
    bias_att_out = jnp.sum(grad_att.astype(jnp.float32), axis=0)
    grad_attended = jnp.einsum(
        "td,ed->te", grad_att, out_weight, preferred_element_type=jnp.float32
    )
    grad_attended = grad_attended.astype(jnp.bfloat16)
    tokens, features = grad_attended.shape
    grad_queries, grad_keys, grad_values = attention_backward(
        queries3,
        blocks,
        query_pos,
        query_seg,
        log_total,
        mixed_heads,
        grad_attended.reshape(tokens, HEADS, features // HEADS),
    )
    key_grads, value_grads = (
        lax.psum_scatter(
            grad_keys.astype(jnp.bfloat16), "seq", scatter_dimension=0, tiled=True
        ).astype(jnp.float32),
        lax.psum_scatter(
            grad_values.astype(jnp.bfloat16), "seq", scatter_dimension=0, tiled=True
        ).astype(jnp.float32),
    )
    grad_joined = jnp.concatenate([grad_queries, key_grads, value_grads], axis=1).astype(
        jnp.bfloat16
    )
    grad_qkv = jnp.einsum("td,te->de", stream_low, grad_joined, preferred_element_type=jnp.float32)
    column_sums = jnp.sum(grad_joined.astype(jnp.float32), axis=0)
    bias_att = jnp.stack([column_sums[:features], column_sums[2 * features :], bias_att_out])
    grad_stream_in = grad_first + jnp.einsum(
        "te,de->td", grad_joined, qkv_weight, preferred_element_type=jnp.float32
    )
    layer_grads = (
        grad_qkv,
        grad_out,
        grad_ff_in,
        grad_ff_out,
        bias_att,
        bias_ff_in,
        bias_ff_out,
        jnp.stack([gain_first, gain_second]),
        jnp.stack([shift_first, shift_second]),
    )
    return (grad_stream_in, layer_grads)


def pack_shards(shards):
    qkv, out_w, ff_in, ff_out, att_bias, ff_in_bias, ff_out_bias, gain, shift, final_gain, final_shift = shards
    levels, width, columns = out_w.shape

    def blocks(weight):
        count = weight.shape[2] // columns
        return weight.reshape(levels, width, count, columns).transpose(0, 2, 1, 3).reshape(levels, width * count, columns)

    small = jnp.concatenate(
        [
            att_bias.reshape(levels, -1),
            ff_in_bias,
            ff_out_bias,
            gain.reshape(levels, -1),
            shift.reshape(levels, -1),
            jnp.broadcast_to(final_gain, (levels, width)),
            jnp.broadcast_to(final_shift, (levels, width)),
        ],
        axis=1,
    )
    small = jnp.pad(small[:, None, :], ((0, 0), (0, 15), (0, columns - small.shape[1])))
    return jnp.concatenate([blocks(qkv), out_w, blocks(ff_in), ff_out, small], axis=1)


def unpack_weights(gathered, width, ff_width):
    shards, rows, columns = gathered.shape

    def whole(start, count):
        block = gathered[:, start : start + count * width]
        block = block.reshape(shards, count, width, columns).transpose(0, 2, 1, 3)
        return block.reshape(shards * width, count * columns)

    small = gathered[:, rows - 16]

    def vectors(start, count):
        block = small[:, start : start + count * width].reshape(shards, count, width)
        return block.transpose(1, 0, 2).reshape(count, shards * width)

    ff_count = ff_width // width
    at = 3 * width
    ff_bias = small[:, at : at + ff_width].reshape(shards * ff_width)
    at += ff_width
    return (
        whole(0, 3),
        whole(3 * width, 1),
        whole(4 * width, ff_count),
        gathered[:, (4 + ff_count) * width : (4 + ff_count) * width + ff_width].reshape(shards * ff_width, columns),
        vectors(0, 3),
        ff_bias,
        vectors(at, 1)[0],
        vectors(at + width, 2),
        vectors(at + 3 * width, 2),
        vectors(at + 5 * width, 1)[0],
        vectors(at + 6 * width, 1)[0],
    )


def pack_grads(grads, shards):
    columns = grads[1].shape[1]

    def blocks(grad):
        width, count = grad.shape[0] // shards, grad.shape[1] // columns
        return grad.reshape(shards, width, count, columns).transpose(0, 2, 1, 3).reshape(shards, width * count, columns)

    return jnp.concatenate(
        [blocks(grads[0]), blocks(grads[1]), blocks(grads[2]), grads[3].reshape(shards, -1, columns)], axis=1
    ).astype(jnp.bfloat16)


def gather_plain(shards, number):
    gathered = [
        lax.all_gather(shards[member][number], ("dp", "seq"), axis=axis, tiled=True)
        for member, axis in enumerate((0, 0, 0, 0, 1, 0, 0, 1, 1))
    ]
    return tuple(gathered) + tuple(
        lax.all_gather(shards[member], ("dp", "seq"), axis=0, tiled=True) for member in (9, 10)
    )


def body(geo, *args):
    stream_in, residue_in, segments, out_cot = args[:4]
    shards = args[4:]
    levels, width, _ = shards[1].shape
    ff_width = shards[3].shape[1]
    stream = stream_in[0].astype(jnp.float32)
    residue = residue_in[0]
    cotangent = out_cot[0]
    tokens = stream.shape[0]
    query_seg = segments[0]
    whole_seg = lax.all_gather(query_seg, "seq", axis=0, tiled=True)
    seq_index = lax.axis_index("seq")
    query_pos = seq_index * tokens + jnp.arange(tokens, dtype=jnp.int32)
    kernels = geo.shards <= 32
    if kernels:
        packed = pack_shards(shards)
        gathered = gather_all(geo, packed, 96)
        weights = [unpack_weights(gathered[number], width, ff_width) for number in range(levels)]
    else:
        weights = [gather_plain(shards, number) for number in range(levels)]
    states = []
    for number in range(levels):
        stream, residue, state = layer_forward(stream, residue, weights[number], query_pos, query_seg, whole_seg)
        states.append(state)
    final_norm, pull_final = jax.vjp(
        layer_norm,
        residue,
        weights[-1][9].astype(jnp.float32),
        weights[-1][10].astype(jnp.float32),
    )
    output = stream + final_norm
    grad_residue, final_gain_grad, final_shift_grad = pull_final(cotangent)
    grad_stream = cotangent
    grads = [None] * levels
    for number in reversed(range(levels)):
        grad_stream, grads[number] = layer_backward(
            states[number], weights[number], grad_stream, grad_residue, query_pos, query_seg
        )
    if kernels:
        packed = jnp.stack([pack_grads(grads[number], geo.shards) for number in range(levels)])
        features = stream.shape[1]
        rows = [
            jnp.stack([grads[number][member] for number in range(levels)]).reshape(-1, features)
            for member in (4, 5, 6, 7, 8)
        ]
        small = jnp.concatenate(rows + [final_gain_grad[None], final_shift_grad[None]])
        small = jnp.pad(small, ((0, -small.shape[0] % 8), (0, 0)))
        big, small = scatter_all(geo, packed, small, 96)
        shard = lax.axis_index("dp") * geo.seq + seq_index
        mine = lax.dynamic_slice_in_dim(small, shard * width, width, axis=1)

        def whole(start, count):
            block = big[:, start : start + count * width].reshape(levels, count, width, features)
            return block.transpose(0, 2, 1, 3).reshape(levels, width, count * features)

        ff_count = ff_width // width
        ff_rows = levels * ff_count
        ff_bias = small[3 * levels : 3 * levels + ff_rows].reshape(levels, -1)
        at = 3 * levels + ff_rows
        summed = [
            whole(0, 3),
            whole(3 * width, 1),
            whole(4 * width, ff_count),
            big[:, (4 + ff_count) * width :],
            mine[: 3 * levels].reshape(levels, 3, width),
            lax.dynamic_slice_in_dim(ff_bias, shard * ff_width, ff_width, axis=1),
            mine[at : at + levels],
            mine[at + levels : at + 3 * levels].reshape(levels, 2, width),
            mine[at + 3 * levels : at + 5 * levels].reshape(levels, 2, width),
            mine[at + 5 * levels],
            mine[at + 5 * levels + 1],
        ]
    else:
        summed = [
            jnp.stack(
                [
                    lax.psum_scatter(grads[number][member], ("dp", "seq"), scatter_dimension=axis, tiled=True)
                    for number in range(levels)
                ]
            )
            for member, axis in enumerate((0, 0, 0, 0, 1, 0, 0, 1, 1))
        ] + [
            lax.psum_scatter(final_gain_grad, ("dp", "seq"), scatter_dimension=0, tiled=True),
            lax.psum_scatter(final_shift_grad, ("dp", "seq"), scatter_dimension=0, tiled=True),
        ]
    return (output[None], grad_stream[None], grad_residue[None]) + tuple(summed)


def solution(mesh):
    return jax.shard_map(
        functools.partial(body, Geometry(mesh)),
        mesh=mesh,
        in_specs=(
            P("dp", "seq", None),
            P("dp", "seq", None),
            P("dp", "seq"),
            P("dp", "seq", None),
            P(None, ("dp", "seq"), None),
            P(None, ("dp", "seq"), None),
            P(None, ("dp", "seq"), None),
            P(None, ("dp", "seq"), None),
            P(None, None, ("dp", "seq")),
            P(None, ("dp", "seq")),
            P(None, ("dp", "seq")),
            P(None, None, ("dp", "seq")),
            P(None, None, ("dp", "seq")),
            P(("dp", "seq")),
            P(("dp", "seq")),
        ),
        out_specs=(
            P("dp", "seq", None),
            P("dp", "seq", None),
            P("dp", "seq", None),
            P(None, ("dp", "seq"), None),
            P(None, ("dp", "seq"), None),
            P(None, ("dp", "seq"), None),
            P(None, ("dp", "seq"), None),
            P(None, None, ("dp", "seq")),
            P(None, ("dp", "seq")),
            P(None, ("dp", "seq")),
            P(None, None, ("dp", "seq")),
            P(None, None, ("dp", "seq")),
            P(("dp", "seq")),
            P(("dp", "seq")),
        ),
        check_vma=False,
    )
```

```python
import functools
import math

import jax
import jax.numpy as jnp
from jax import lax
from jax.experimental import pallas as pl
from jax.experimental.pallas import tpu as pltpu
from jax.sharding import PartitionSpec as P

HEADS = 8
MESH = pl.DeviceIdType.MESH


class Geometry:
    def __init__(self, mesh):
        self.dp, self.seq = mesh.shape["dp"], mesh.shape["seq"]
        self.ny = self.seq // 2
        self.nx = self.ny
        self.nz = self.dp // self.nx
        self.shards = self.dp * self.seq

    def here(self):
        dp, seq = lax.axis_index("dp"), lax.axis_index("seq")
        return lax.div(dp, self.nx), lax.rem(dp, self.nx), lax.div(seq, 2), lax.rem(seq, 2)

    def device(self, z, x, y, c):
        return (z * self.nx + x, y * 2 + c)

    def peers(self):
        z, x, y, c = self.here()
        found = [self.device(lax.rem(z + k, self.nz), x, y, c) for k in range(1, self.nz)]
        found += [self.device(z, lax.rem(x + k, self.nx), y, c) for k in range(1, self.nx)]
        found += [self.device(z, x, lax.rem(y + k, self.ny), c) for k in range(1, self.ny)]
        return found + [self.device(z, x, y, 1 - c)]


def greet(devices):
    barrier = pltpu.get_barrier_semaphore()
    for device in devices:
        pl.semaphore_signal(barrier, inc=1, device_id=device, device_id_type=MESH)
    pl.semaphore_wait(barrier, len(devices))


def remote(src, dst, send_sem, recv_sem, device):
    return pltpu.make_async_remote_copy(
        src_ref=src,
        dst_ref=dst,
        send_sem=send_sem,
        recv_sem=recv_sem,
        device_id=device,
        device_id_type=MESH,
    )


epsilon = 1e-05
masked_value = -1e30


def smooth_gate(values):
    return jax.nn.gelu(values, approximate=True)


def layer_norm(values, norm_gain, norm_shift):
    average = jnp.mean(values, axis=-1, keepdims=True)
    centred = values - average
    variance = jnp.mean(centred * centred, axis=-1, keepdims=True)
    return centred * lax.rsqrt(variance + epsilon) * norm_gain + norm_shift


def keep_state(carried):
    return carried


def allowed_pairs(query_pos, query_seg, key_pos, key_seg):
    return (query_seg[:, None] == key_seg[None, :]) & (key_pos[None, :] <= query_pos[:, None])


def block_needed(query_pos, query_seg, key_pos, key_seg):
    return (key_pos[0] <= query_pos[-1]) & (key_seg[-1] >= query_seg[0])


def key_blocks(keys_values, key_seg):
    length = keys_values.shape[0]
    features = keys_values.shape[1] // 2
    head_size = features // HEADS
    block_rows = math.gcd(length, 512)
    block_count = length // block_rows
    split_kv = keys_values.reshape(block_count, block_rows, 2, HEADS, head_size)
    key_pos = jnp.arange(length, dtype=jnp.int32).reshape(block_count, block_rows)
    return (split_kv[:, :, 0], split_kv[:, :, 1], key_pos, key_seg.reshape(block_count, block_rows))


def block_scores(queries3, key_block, query_pos, query_seg, key_pos, key_seg):
    scaling = 1.0 / math.sqrt(queries3.shape[-1])
    raw_scores = (
        jnp.einsum("qhd,khd->hqk", queries3, key_block, preferred_element_type=jnp.float32)
        * scaling
    )
    return (raw_scores, allowed_pairs(query_pos, query_seg, key_pos, key_seg)[None])


def attention_forward(queries3, blocks, query_pos, query_seg):
    tokens, head_count, head_size = queries3.shape

    def statistics(carried, block_items):
        key_block, value_block, key_pos, key_seg = block_items

        def statistics_compute(running):
            run_max, run_sum = running
            raw_scores, allowed = block_scores(
                queries3, key_block, query_pos, query_seg, key_pos, key_seg
            )
            new_max = jnp.maximum(
                run_max, jnp.max(jnp.where(allowed, raw_scores, masked_value), axis=-1)
            )
            exp_terms = jnp.exp(jnp.where(allowed, raw_scores - new_max[..., None], masked_value))
            return (new_max, run_sum * jnp.exp(run_max - new_max) + jnp.sum(exp_terms, axis=-1))

        needed = block_needed(query_pos, query_seg, key_pos, key_seg)
        return (lax.cond(needed, statistics_compute, keep_state, carried), None)

    initial = (
        jnp.full((head_count, tokens), masked_value, jnp.float32),
        jnp.zeros((head_count, tokens), jnp.float32),
    )
    (run_max, run_sum), unused = lax.scan(statistics, initial, blocks)
    log_total = run_max + jnp.log(run_sum)

    def accumulate(carried, block_items):
        key_block, value_block, key_pos, key_seg = block_items

        def accumulate_compute(running):
            raw_scores, allowed = block_scores(
                queries3, key_block, query_pos, query_seg, key_pos, key_seg
            )
            weights = jnp.exp(jnp.where(allowed, raw_scores - log_total[..., None], masked_value))
            weights = weights.astype(jnp.bfloat16)
            return running + jnp.einsum(
                "hqk,khd->qhd", weights, value_block, preferred_element_type=jnp.float32
            )

        needed = block_needed(query_pos, query_seg, key_pos, key_seg)
        return (lax.cond(needed, accumulate_compute, keep_state, carried), None)

    mixed_heads, unused = lax.scan(
        accumulate, jnp.zeros((tokens, head_count, head_size), jnp.float32), blocks
    )
    return (mixed_heads, log_total)


def attention_backward(queries3, blocks, query_pos, query_seg, log_total, mixed_heads, grad_heads):
    tokens, head_count, head_size = queries3.shape
    scaling = 1.0 / math.sqrt(head_size)
    row_dots = jnp.sum(mixed_heads * grad_heads.astype(jnp.float32), axis=-1).T
    block_rows = blocks[0].shape[1]
    block_count = blocks[0].shape[0]

    def backward_step(grad_queries, block_items):
        key_block, value_block, key_pos, key_seg = block_items

        def backward_compute(running):
            raw_scores, allowed = block_scores(
                queries3, key_block, query_pos, query_seg, key_pos, key_seg
            )
            prob_values = jnp.exp(
                jnp.where(allowed, raw_scores - log_total[..., None], masked_value)
            )
            grad_values = jnp.einsum(
                "hqk,qhd->khd",
                prob_values.astype(jnp.bfloat16),
                grad_heads,
                preferred_element_type=jnp.float32,
            )
            grad_probs = jnp.einsum(
                "qhd,khd->hqk", grad_heads, value_block, preferred_element_type=jnp.float32
            )
            grad_scores = (prob_values * (grad_probs - row_dots[..., None])).astype(jnp.bfloat16)
            running = (
                running
                + jnp.einsum(
                    "hqk,khd->qhd", grad_scores, key_block, preferred_element_type=jnp.float32
                )
                * scaling
            )
            grad_keys = (
                jnp.einsum(
                    "hqk,qhd->khd", grad_scores, queries3, preferred_element_type=jnp.float32
                )
                * scaling
            )
            return (running, grad_keys, grad_values)

        def skip_block(running):
            empty_rows = jnp.zeros((block_rows, head_count, head_size), jnp.float32)
            return (running, empty_rows, empty_rows)

        needed = block_needed(query_pos, query_seg, key_pos, key_seg)
        grad_queries, grad_keys, grad_values = lax.cond(
            needed, backward_compute, skip_block, grad_queries
        )
        return (grad_queries, (grad_keys, grad_values))

    initial = jnp.zeros((tokens, head_count, head_size), jnp.float32)
    grad_queries, (grad_keys, grad_values) = lax.scan(backward_step, initial, blocks)
    length = block_count * block_rows
    return (
        grad_queries.reshape(tokens, head_count * head_size),
        grad_keys.reshape(length, head_count * head_size),
        grad_values.reshape(length, head_count * head_size),
    )


def layer_forward(stream, residue, weights, query_pos, query_seg, key_seg):
    (
        qkv_weight,
        out_weight,
        ff_in_weight,
        ff_out_weight,
        att_bias,
        ff_in_bias,
        ff_out_bias,
        norm_gain,
        norm_shift,
    ) = weights[:9]
    tokens, features = stream.shape
    stream_low = stream.astype(jnp.bfloat16)
    bias_row = jnp.concatenate([att_bias[0], jnp.zeros_like(att_bias[0]), att_bias[1]]).astype(
        jnp.float32
    )
    joined = (
        jnp.dot(stream_low, qkv_weight, preferred_element_type=jnp.float32) + bias_row
    ).astype(jnp.bfloat16)
    queries3 = joined[:, :features].reshape(tokens, HEADS, features // HEADS)
    keys_values = lax.all_gather(joined[:, features:], "seq", axis=0, tiled=True)
    blocks = key_blocks(keys_values, key_seg)
    mixed_heads, log_total = attention_forward(queries3, blocks, query_pos, query_seg)
    attended = mixed_heads.reshape(tokens, features).astype(jnp.bfloat16)
    branch_att = jnp.dot(attended, out_weight, preferred_element_type=jnp.float32) + att_bias[
        2
    ].astype(jnp.float32)
    middle, pull_first = jax.vjp(
        layer_norm,
        stream + branch_att,
        norm_gain[0].astype(jnp.float32),
        norm_shift[0].astype(jnp.float32),
    )
    residue_mid = residue + branch_att
    middle_low = middle.astype(jnp.bfloat16)
    hidden = jnp.dot(
        middle_low, ff_in_weight, preferred_element_type=jnp.float32
    ) + ff_in_bias.astype(jnp.float32)
    active = smooth_gate(hidden).astype(jnp.bfloat16)
    branch_ff = jnp.dot(
        active, ff_out_weight, preferred_element_type=jnp.float32
    ) + ff_out_bias.astype(jnp.float32)
    stream_next, pull_second = jax.vjp(
        layer_norm,
        middle + branch_ff,
        norm_gain[1].astype(jnp.float32),
        norm_shift[1].astype(jnp.float32),
    )
    saved_state = (
        stream_low,
        queries3,
        blocks,
        mixed_heads,
        log_total,
        attended,
        pull_first,
        middle_low,
        hidden,
        active,
        pull_second,
    )
    return (stream_next, residue_mid + branch_ff, saved_state)


def layer_backward(saved_state, weights, grad_stream, grad_residue, query_pos, query_seg):
    (
        stream_low,
        queries3,
        blocks,
        mixed_heads,
        log_total,
        attended,
        pull_first,
        middle_low,
        hidden,
        active,
        pull_second,
    ) = saved_state
    qkv_weight, out_weight, ff_in_weight, ff_out_weight = weights[:4]
    grad_second, gain_second, shift_second = pull_second(grad_stream)
    grad_ff = (grad_second + grad_residue).astype(jnp.bfloat16)
    grad_ff_out = jnp.einsum("tf,td->fd", active, grad_ff, preferred_element_type=jnp.float32)
    bias_ff_out = jnp.sum(grad_ff.astype(jnp.float32), axis=0)
    grad_active = jnp.einsum(
        "td,fd->tf", grad_ff, ff_out_weight, preferred_element_type=jnp.float32
    )
    unused_gate, pull_gate = jax.vjp(smooth_gate, hidden)
    grad_hidden = pull_gate(grad_active)[0].astype(jnp.bfloat16)
    grad_ff_in = jnp.einsum(
        "td,tf->df", middle_low, grad_hidden, preferred_element_type=jnp.float32
    )
    bias_ff_in = jnp.sum(grad_hidden.astype(jnp.float32), axis=0)
    grad_middle = grad_second + jnp.einsum(
        "tf,df->td", grad_hidden, ff_in_weight, preferred_element_type=jnp.float32
    )
    grad_first, gain_first, shift_first = pull_first(grad_middle)
    grad_att = (grad_first + grad_residue).astype(jnp.bfloat16)
    grad_out = jnp.einsum("te,td->ed", attended, grad_att, preferred_element_type=jnp.float32)
    bias_att_out = jnp.sum(grad_att.astype(jnp.float32), axis=0)
    grad_attended = jnp.einsum(
        "td,ed->te", grad_att, out_weight, preferred_element_type=jnp.float32
    )
    grad_attended = grad_attended.astype(jnp.bfloat16)
    tokens, features = grad_attended.shape
    grad_queries, grad_keys, grad_values = attention_backward(
        queries3,
        blocks,
        query_pos,
        query_seg,
        log_total,
        mixed_heads,
        grad_attended.reshape(tokens, HEADS, features // HEADS),
    )
    key_grads, value_grads = (
        lax.psum_scatter(
            grad_keys.astype(jnp.bfloat16), "seq", scatter_dimension=0, tiled=True
        ).astype(jnp.float32),
        lax.psum_scatter(
            grad_values.astype(jnp.bfloat16), "seq", scatter_dimension=0, tiled=True
        ).astype(jnp.float32),
    )
    grad_joined = jnp.concatenate([grad_queries, key_grads, value_grads], axis=1).astype(
        jnp.bfloat16
    )
    grad_qkv = jnp.einsum("td,te->de", stream_low, grad_joined, preferred_element_type=jnp.float32)
    column_sums = jnp.sum(grad_joined.astype(jnp.float32), axis=0)
    bias_att = jnp.stack([column_sums[:features], column_sums[2 * features :], bias_att_out])
    grad_stream_in = grad_first + jnp.einsum(
        "te,de->td", grad_joined, qkv_weight, preferred_element_type=jnp.float32
    )
    layer_grads = (
        grad_qkv,
        grad_out,
        grad_ff_in,
        grad_ff_out,
        bias_att,
        bias_ff_in,
        bias_ff_out,
        jnp.stack([gain_first, gain_second]),
        jnp.stack([shift_first, shift_second]),
    )
    return (grad_stream_in, layer_grads)


def product(left, right):
    return lax.dot_general(left, right, (((1,), (0,)), ((), ())), preferred_element_type=jnp.float32)


def product_rows(left, right):
    return lax.dot_general(left, right, (((1,), (1,)), ((), ())), preferred_element_type=jnp.float32)


def product_tokens(left, right):
    return lax.dot_general(left, right, (((0,), (0,)), ((), ())), preferred_element_type=jnp.float32)


def wide(value):
    return value.astype(jnp.float32)


def low(value):
    return value.astype(jnp.bfloat16)


def normalize(values):
    centred = values - jnp.mean(values, axis=-1, keepdims=True)
    inverse = lax.rsqrt(jnp.mean(centred * centred, axis=-1, keepdims=True) + epsilon)
    return centred * inverse, inverse


def normalize_back(grad, normal, inverse, gain):
    scaled = grad * gain
    return (
        scaled
        - jnp.mean(scaled, axis=-1, keepdims=True)
        - normal * jnp.mean(scaled * normal, axis=-1, keepdims=True)
    ) * inverse


def column_sums(values):
    return jnp.sum(values, axis=0, keepdims=True)


def gelu_pair(v):
    rate = math.sqrt(2.0 / math.pi)
    square = v * v
    bent = jnp.tanh(v * (rate + (rate * 0.044715) * square))
    rise = 0.5 + 0.5 * bent
    slope = rise + v * (0.5 - 0.5 * bent * bent) * (rate + (3.0 * rate * 0.044715) * square)
    return v * rise, slope


class Gather:
    def __init__(self, geo, w, l, start, size, cut, sems, number):
        self.geo, self.w, self.l, self.start, self.size, self.cut = geo, w, l, start, size, cut
        self.sems = [sem.at[number] for sem in sems]
        self.z, self.x, self.y, self.c = geo.here()

    def at(self, k, i, j, low=None):
        geo = self.geo
        rows = (self.start, self.size)
        if low is not None:
            rows = (self.start + self.cut, self.size - self.cut) if low else (self.start, self.cut)
        return self.w.at[
            self.l,
            lax.rem(self.z + geo.nz - k, geo.nz),
            lax.rem(self.x + geo.nx - i, geo.nx),
            lax.rem(self.y + geo.ny - j, geo.ny),
            self.c,
            pl.ds(*rows),
        ]

    def along_x(self, i):
        return self.geo.device(self.z, lax.rem(self.x + i, self.geo.nx), self.y, self.c)

    def along_y(self, j):
        return self.geo.device(self.z, self.x, lax.rem(self.y + j, self.geo.ny), self.c)

    def copy(self, piece, number, index, device):
        send, recv = self.sems[number], self.sems[number + 1]
        return remote(piece, piece, send.at[index], recv.at[index], device)

    def z_copy(self, k):
        return self.copy(
            self.at(0, 0, 0), 0, (k - 1,),
            self.geo.device(lax.rem(self.z + k, self.geo.nz), self.x, self.y, self.c),
        )

    def x_copy(self, k, i):
        return self.copy(self.at(k, 0, 0), 2, (k, i - 1), self.along_x(i))

    def y_copy(self, k, j):
        return self.copy(self.at(k, 0, 0), 4, (k, j - 1), self.along_y(j))

    def x_forward(self, k, i, j):
        return self.copy(self.at(k, 0, j, True), 6, (k, i - 1, j - 1), self.along_x(i))

    def y_forward(self, k, i, j):
        return self.copy(self.at(k, i, 0, False), 8, (k, i - 1, j - 1), self.along_y(j))

    def c_copy(self, k, i, j):
        return self.copy(
            self.at(k, i, j), 10, (k, i, j), self.geo.device(self.z, self.x, self.y, 1 - self.c)
        )

    def fan(self, k):
        for i in range(1, self.geo.nx):
            self.x_copy(k, i).start()
        for j in range(1, self.geo.ny):
            self.y_copy(k, j).start()
        self.c_copy(k, 0, 0).start()

    def own(self):
        for k in range(1, self.geo.nz):
            self.z_copy(k).start()
        self.fan(0)

    def from_z(self, k):
        self.z_copy(k).wait_recv()
        self.fan(k)

    def from_line(self, k):
        nx, ny = self.geo.nx, self.geo.ny
        for j in range(1, ny):
            self.y_copy(k, j).wait_recv()
            for i in range(1, nx):
                self.x_forward(k, i, j).start()
            self.c_copy(k, 0, j).start()
        for i in range(1, nx):
            self.x_copy(k, i).wait_recv()
            for j in range(1, ny):
                self.y_forward(k, i, j).start()
            self.c_copy(k, i, 0).start()

    def from_corner(self, k):
        for i in range(1, self.geo.nx):
            for j in range(1, self.geo.ny):
                self.x_forward(k, i, j).wait_recv()
                self.y_forward(k, i, j).wait_recv()
                self.c_copy(k, i, j).start()

    def steps(self):
        every = range(self.geo.nz)
        return (
            [functools.partial(self.from_z, k) for k in every if k]
            + [functools.partial(self.from_line, k) for k in every]
            + [functools.partial(self.from_corner, k) for k in every]
        )

    def arrive(self):
        for k in range(self.geo.nz):
            for i in range(self.geo.nx):
                for j in range(self.geo.ny):
                    self.c_copy(k, i, j).wait_recv()

    def finish(self):
        nx, ny = self.geo.nx, self.geo.ny
        for k in range(self.geo.nz):
            if k:
                self.z_copy(k).wait_send()
            for i in range(1, nx):
                self.x_copy(k, i).wait_send()
            for j in range(1, ny):
                self.y_copy(k, j).wait_send()
            for i in range(nx):
                for j in range(ny):
                    self.c_copy(k, i, j).wait_send()
                    if i and j:
                        self.x_forward(k, i, j).wait_send()
                        self.y_forward(k, i, j).wait_send()

    @staticmethod
    def semaphores(geo, count):
        dma = pltpu.SemaphoreType.DMA
        nz, nx, ny = geo.nz, geo.nx, geo.ny
        return (
            [dma((count, nz - 1))] * 2
            + [dma((count, nz, nx - 1))] * 2
            + [dma((count, nz, ny - 1))] * 2
            + [dma((count, nz, nx - 1, ny - 1))] * 4
            + [dma((count, nz, nx, ny))] * 2
        )


class Scatter:
    def __init__(self, geo, g, own, r1h, r1l, r2h, r2l, zin, total, l, cut, sems, number):
        self.geo, self.g, self.own, self.l, self.cut = geo, g, own.at[l], l, cut
        self.r1h, self.r1l, self.r2h, self.r2l, self.zin = (ref.at[l] for ref in (r1h, r1l, r2h, r2l, zin))
        self.total = total
        self.rows = g.shape[4]
        self.sems = [sem.at[number] for sem in sems]
        self.z, self.x, self.y, self.c = geo.here()
        self.order = list(range(1, geo.nz)) + [0]

    def copy(self, src, dst, number, index, device):
        return remote(src, dst, self.sems[number].at[index], self.sems[number + 1].at[index], device)

    def cross(self, k):
        return self.copy(
            self.g.at[lax.rem(self.z + k, self.geo.nz), :, :, 1 - self.c], self.own.at[k], 0, (k,),
            self.geo.device(self.z, self.x, self.y, 1 - self.c),
        )

    def to_x(self, src, dst, number, index, i):
        return self.copy(src, dst, number, index, self.geo.device(self.z, lax.rem(self.x + i, self.geo.nx), self.y, self.c))

    def to_y(self, src, dst, number, index, j):
        return self.copy(src, dst, number, index, self.geo.device(self.z, self.x, lax.rem(self.y + j, self.geo.ny), self.c))

    def one(self, k):
        nx, ny = self.geo.nx, self.geo.ny
        top, rest = pl.ds(0, self.cut), pl.ds(self.cut, self.rows - self.cut)
        return [
            self.to_y(self.own.at[k, :, lax.rem(self.y + j, ny), top], self.r1h.at[k, j - 1], 2, (k, j - 1), j)
            for j in range(1, ny)
        ] + [
            self.to_x(self.own.at[k, lax.rem(self.x + i, nx), :, rest], self.r1l.at[k, i - 1], 4, (k, i - 1), i)
            for i in range(1, nx)
        ]

    def two(self, k):
        nx, ny = self.geo.nx, self.geo.ny
        top, rest = pl.ds(0, self.cut), pl.ds(self.cut, self.rows - self.cut)
        return [
            self.to_x(self.own.at[k, lax.rem(self.x + i, nx), self.y, top], self.r2h.at[k, i - 1], 6, (k, i - 1), i)
            for i in range(1, nx)
        ] + [
            self.to_y(self.own.at[k, self.x, lax.rem(self.y + j, ny), rest], self.r2l.at[k, j - 1], 8, (k, j - 1), j)
            for j in range(1, ny)
        ]

    def three(self, k):
        return self.copy(
            self.own.at[k, self.x, self.y], self.zin.at[k - 1], 10, (k - 1,),
            self.geo.device(lax.rem(self.z + k, self.geo.nz), self.x, self.y, self.c),
        )

    def begin(self):
        for k in self.order:
            self.cross(k).start()

    def step_one(self, k):
        own = self.own
        self.cross(k).wait()
        for i in range(self.geo.nx):
            for j in range(self.geo.ny):
                mine = self.g[lax.rem(self.z + k, self.geo.nz), i, j, self.c]
                own[k, i, j] = low(wide(mine) + wide(own[k, i, j]))
        for copy in self.one(k):
            copy.start()

    def step_two(self, k):
        own, x, y = self.own, self.x, self.y
        top, rest = pl.ds(0, self.cut), pl.ds(self.cut, self.rows - self.cut)
        for copy in self.one(k):
            copy.wait()
        for i in range(self.geo.nx):
            total = wide(own[k, i, y, top])
            for j in range(1, self.geo.ny):
                total = total + wide(self.r1h[k, j - 1, i])
            own[k, i, y, top] = low(total)
        for j in range(self.geo.ny):
            total = wide(own[k, x, j, rest])
            for i in range(1, self.geo.nx):
                total = total + wide(self.r1l[k, i - 1, j])
            own[k, x, j, rest] = low(total)
        for copy in self.two(k):
            copy.start()

    def step_three(self, k):
        own, x, y = self.own, self.x, self.y
        top, rest = pl.ds(0, self.cut), pl.ds(self.cut, self.rows - self.cut)
        for copy in self.two(k):
            copy.wait()
        upper = wide(own[k, x, y, top])
        for i in range(1, self.geo.nx):
            upper = upper + wide(self.r2h[k, i - 1])
        lower = wide(own[k, x, y, rest])
        for j in range(1, self.geo.ny):
            lower = lower + wide(self.r2l[k, j - 1])
        if k:
            own[k, x, y, top] = low(upper)
            own[k, x, y, rest] = low(lower)
            self.three(k).start()
        else:
            self.total[top] = upper
            self.total[rest] = lower

    def finish(self):
        total = self.total[...]
        for k in range(1, self.geo.nz):
            self.three(k).wait()
            total = total + wide(self.zin[k - 1])
        self.total[...] = total

    def steps(self):
        return [
            [functools.partial(step, k) for k in self.order]
            for step in (self.step_one, self.step_two, self.step_three)
        ]

    @staticmethod
    def buffers(geo, levels, rows, cut, columns, kind):
        vmem = pltpu.VMEM
        nz, nx, ny = geo.nz, geo.nx, geo.ny
        rest = rows - cut
        return [
            vmem((nz, nx, ny, 2, rows, columns), kind),
            vmem((levels, nz, nx, ny, rows, columns), kind),
            vmem((levels, nz, ny - 1, nx, cut, columns), kind),
            vmem((levels, nz, nx - 1, ny, rest, columns), kind),
            vmem((levels, nz, nx - 1, cut, columns), kind),
            vmem((levels, nz, ny - 1, rest, columns), kind),
            vmem((levels, nz - 1, rows, columns), kind),
            vmem((rows, columns), jnp.float32),
        ]

    @staticmethod
    def semaphores(geo, count):
        dma = pltpu.SemaphoreType.DMA
        nz, nx, ny = geo.nz, geo.nx, geo.ny
        return (
            [dma((count, nz))] * 2
            + [dma((count, nz, ny - 1))] * 2
            + [dma((count, nz, nx - 1))] * 2
            + [dma((count, nz, nx - 1))] * 2
            + [dma((count, nz, ny - 1))] * 2
            + [dma((count, nz - 1))] * 2
        )


ROW_ATT_BIAS, ROW_IN_BIAS, ROW_OUT_BIAS, ROW_GAIN, ROW_SHIFT, ROW_FINAL, ROWS = 0, 3, 7, 8, 10, 12, 16


def step_kernel(geo, half_a, half_f, *refs):
    refs = list(refs)

    def take(count):
        taken = refs[:count]
        del refs[:count]
        return taken

    (stream_in, residue_in, seg, cot, qkv_in, out_in, ff_in_in, ff_out_in, att_in, in_bias_in, out_bias_in, gain_in,
     shift_in, final_gain_in, final_shift_in) = take(15)
    (out, stream_grad, residue_grad, qkv_grad, out_grad, ff_in_grad, ff_out_grad, att_grad, in_bias_grad, out_bias_grad,
     gain_grad, shift_grad, final_gain_grad, final_shift_grad) = take(14)
    (w, par, own_small, xl_next, xn, qs, kv, kt, pt, att, mid, act, slope, n1, n2, i1, i2, bias, segs, dkv, ob, sb, sc,
     rb, rc, small, sbuf, sin) = take(28)
    buffers_a, buffers_f = take(8), take(8)
    gather_sems, scatter_sems = take(12), take(12)
    (load_sem, seg_send, seg_recv, y_send, y_recv, c_send, c_recv, by_send, by_recv, bc_send, bc_recv, s_send,
     s_recv, residue_sem) = take(14)
    assert not refs

    z, xx, y, c = geo.here()
    s = 2 * y + c
    shard = (z * geo.nx + xx) * geo.seq + s
    count = geo.seq
    tokens, features = residue_in.shape
    levels = w.shape[0]
    width = features // geo.shards
    ff_rows = in_bias_in.shape[1]
    head = features // HEADS
    lanes = 2 * head
    pairs = features // lanes
    parts = act.shape[1]
    sibling, across = geo.device(z, xx, y, 1 - c), geo.device(z, xx, 1 - y, c)
    row_in = 4 * width + ROWS
    row_out = row_in + parts * width
    xl = [stream_in] + [xl_next.at[l - 1] for l in range(1, levels)]

    pieces = [
        (
            Gather(geo, w, l, 0, row_in, half_a, gather_sems, 2 * l),
            Gather(geo, w, l, row_in, parts * width + ff_rows, half_f, gather_sems, 2 * l + 1),
        )
        for l in range(levels)
    ]
    sums = [
        (
            Scatter(geo, *buffers_a, l, half_a, scatter_sems, 2 * l),
            Scatter(geo, *buffers_f, l, half_f, scatter_sems, 2 * l + 1),
        )
        for l in range(levels)
    ]

    def own_loads(l):
        mine = w.at[l, z, xx, y, c]
        pairs_of = [(qkv_in.at[l, :, pl.ds(n * features, features)], n * width, width) for n in range(3)]
        pairs_of.append((out_in.at[l], 3 * width, width))
        for n in range(parts):
            pairs_of.append((ff_in_in.at[l, :, pl.ds(n * features, features)], row_in + n * width, width))
        pairs_of.append((ff_out_in.at[l], row_out, ff_rows))
        return [
            pltpu.make_async_copy(src, mine.at[pl.ds(start, size)], load_sem.at[l, n])
            for n, (src, start, size) in enumerate(pairs_of)
        ]

    for l in range(levels):
        for copy in own_loads(l):
            copy.start()
    lane = lax.broadcasted_iota(jnp.int32, (width, features), 1)
    place = low(jnp.where(lane == shard * width + lax.broadcasted_iota(jnp.int32, (width, features), 0), 1.0, 0.0))
    lane = lax.broadcasted_iota(jnp.int32, (ff_rows, features), 1)
    ff_lane = lax.rem(shard, features // ff_rows) * ff_rows
    ff_place = low(jnp.where(lane == ff_lane + lax.broadcasted_iota(jnp.int32, (ff_rows, features), 0), 1.0, 0.0))
    own_small[...] = jnp.zeros_like(own_small)
    for l in range(levels):
        own_small[l, ROW_ATT_BIAS : ROW_ATT_BIAS + 3, :] = product(att_in[l], place)
        spread = product(in_bias_in[l : l + 1, :], ff_place)
        for j in range(parts):
            own_small[l, ROW_IN_BIAS + j : ROW_IN_BIAS + j + 1, :] = jnp.where(z == j, spread, 0.0)
        own_small[l, ROW_OUT_BIAS : ROW_OUT_BIAS + 1, :] = product(out_bias_in[l : l + 1, :], place)
        own_small[l, ROW_GAIN : ROW_GAIN + 2, :] = product(gain_in[l], place)
        own_small[l, ROW_SHIFT : ROW_SHIFT + 2, :] = product(shift_in[l], place)
        own_small[l, ROW_FINAL : ROW_FINAL + 1, :] = product(final_gain_in[...], place)
        own_small[l, ROW_FINAL + 1 : ROW_FINAL + 2, :] = product(final_shift_in[...], place)
        w[l, z, xx, y, c, 4 * width : row_in, :] = low(own_small[l])

    segs[0] = seg[...]
    greet(geo.peers() + [geo.device(z, xx, 1 - y, 1 - c)])
    line = [(z * geo.nx + xx, lax.rem(s + k, count)) for k in range(1, count)]

    def seg_copy(k):
        return remote(segs.at[0], segs.at[k], seg_send.at[k], seg_recv.at[k], line[k - 1])

    def y_copy(l):
        return remote(xl[l], xn.at[l], y_send.at[l], y_recv.at[l], across)

    def c_copy(l, src):
        return remote(kv.at[l, src], kv.at[l, 1], c_send.at[l], c_recv.at[l], sibling)

    def send_stream(l):
        @pl.when(y == 0)
        def _():
            y_copy(l).start()

    for copy in own_loads(0)[:4]:
        copy.wait()
    pieces[0][0].own()
    for copy in own_loads(0)[4:]:
        copy.wait()
    for k in range(1, count):
        seg_copy(k).start()
    send_stream(0)
    pieces[0][1].own()

    waiting = []

    def tick(number):
        for _ in range(min(number, len(waiting))):
            waiting.pop(0)()

    steps_a, steps_f = pieces[0][0].steps(), pieces[0][1].steps()
    nz = geo.nz
    for step in steps_a[: 2 * nz - 1] + steps_f[: nz - 1] + steps_a[2 * nz - 1 :]:
        step()

    @pl.when(y == 0)
    def _():
        for l in range(levels):
            xn[l] = jnp.zeros_like(xn[l])

    @pl.when(s == 0)
    def _():
        for l in range(levels):
            kv[l, 1] = jnp.zeros_like(kv[l, 1])

    for k in range(1, count):
        seg_copy(k).wait()
    query_seg = segs[0, 0:1, :]
    query_pos = s * tokens + lax.broadcasted_iota(jnp.int32, (tokens, tokens), 1)
    for b in range(3):
        block = lax.rem(s + count - b, count)
        key_seg = jnp.transpose(jnp.broadcast_to(wide(segs[b, 0:1, :]), (128, tokens)))[:, 0:1]
        key_pos = block * tokens + lax.broadcasted_iota(jnp.int32, (tokens, tokens), 0)
        allowed = (key_seg == wide(query_seg)) & (key_pos <= query_pos)
        bias[b] = jnp.where(allowed, 0.0, masked_value)
    for l in range(levels):
        small[l] = jnp.zeros_like(small[l])

    def weight(l, start):
        return w[l, :, :, :, :, pl.ds(start, width), :].reshape(features, features)

    def out_weight(l, j):
        return w[l, j, :, :, :, pl.ds(row_out, ff_rows), :].reshape(features, features)

    g_a, g_f = buffers_a[0], buffers_f[0]

    def keep(ref, start, value):
        ref[:, :, :, :, pl.ds(start, width), :] = low(value).reshape(nz, geo.nx, geo.ny, 2, width, features)

    def keep_out(j, value):
        g_f[j, :, :, :, pl.ds(parts * width, ff_rows), :] = low(value).reshape(geo.nx, geo.ny, 2, ff_rows, features)

    def row(l, index):
        return par[l, index : index + 1, :]

    pair_lane = lax.broadcasted_iota(jnp.int32, (1, lanes), 1)

    def one_head(value, side):
        return jnp.where((pair_lane < head) == (side == 0), value, jnp.zeros_like(value))

    def ready(piece):
        while waiting:
            tick(1)
        piece.arrive()

    x, r = stream_grad, out
    residue_load = pltpu.make_async_copy(residue_in, r, residue_sem)
    residue_load.start()

    def forward(l):
        ready(pieces[l][0])
        par[l] = jnp.sum(
            wide(w[l, :, :, :, :, pl.ds(4 * width, ROWS), :]).reshape(geo.shards, ROWS, features), axis=0
        )
        if l == 0:
            waiting.extend(steps_f[nz - 1 :])
        else:
            waiting.extend(pieces[l][1].steps())
        xv = xl[l][...]
        keys = product(xv, weight(l, width))
        values = product(xv, weight(l, 2 * width)) + row(l, ROW_ATT_BIAS + 1)
        kv[l, 0, :, 0:features] = low(keys)
        kv[l, 0, :, features:] = low(values)

        @pl.when(c == 0)
        def _():
            c_copy(l, 0).start()

        tick(4)
        queries = low(product(xv, weight(l, 0)) + row(l, ROW_ATT_BIAS))
        qs[l] = queries * (1.0 / math.sqrt(head))

        @pl.when(y == 1)
        def _():
            y_copy(l).wait_recv()

        xv = xn[l]
        keys = product(xv, weight(l, width))
        values = product(xv, weight(l, 2 * width)) + row(l, ROW_ATT_BIAS + 1)
        kv[l, 2, :, 0:features] = low(keys)
        kv[l, 2, :, features:] = low(values)

        @pl.when((y == 1) & (c == 1))
        def _():
            c_copy(l, 2).start()

        tick(4)

        @pl.when((y == 1) | (c == 1))
        def _():
            c_copy(l, 0).wait_recv()

        for b in range(3):
            kt[:, b * tokens : (b + 1) * tokens] = jnp.transpose(kv[l, b, :, features:])

        def attend(p, carry):
            at = pl.ds(pl.multiple_of(p * lanes, lanes), lanes)
            queries = qs[l, :, at]
            keys = kv[l, :, :, at].reshape(3 * tokens, lanes)
            for side in range(2):
                scores = product_rows(keys, one_head(queries, side)) + bias[...].reshape(3 * tokens, tokens)
                terms = jnp.exp(scores - jnp.max(scores, axis=0, keepdims=True))
                probs = low(terms * (1.0 / jnp.sum(terms, axis=0, keepdims=True)))
                pt[l, 2 * p + side] = probs
                rows = pl.ds(pl.multiple_of(p * lanes + side * head, head), head)
                ob[rows, :] = product(kt[rows, :], probs)
            return carry

        lax.fori_loop(0, pairs, attend, 0)
        ready(pieces[l][1])
        if l + 1 < levels:
            for copy in own_loads(l + 1):
                copy.wait()
            pieces[l + 1][0].own()
            pieces[l + 1][1].own()
            waiting.extend(pieces[l + 1][0].steps())
        att[l] = low(jnp.transpose(ob[...]))
        branch = product(att[l], weight(l, 3 * width)) + row(l, ROW_ATT_BIAS + 2)
        normal, inverse = normalize((wide(stream_in[...]) if l == 0 else x[...]) + branch)
        n1[l] = normal
        i1[l] = inverse
        middle = normal * row(l, ROW_GAIN) + row(l, ROW_SHIFT)
        mid[l] = low(middle)
        x[...] = middle
        if l == 0:
            residue_load.wait()
        r[...] = r[...] + branch
        tick(3)
        total = jnp.broadcast_to(row(l, ROW_OUT_BIAS), (tokens, features))
        for j in range(parts):
            hidden = product(mid[l], weight(l, row_in + j * width)) + row(l, ROW_IN_BIAS + j)
            active, rise = gelu_pair(hidden)
            act[l, j] = low(active)
            slope[l, j] = low(rise)
            total = total + product(act[l, j], out_weight(l, j))
            tick(2)
        r[...] = r[...] + total
        normal, inverse = normalize(x[...] + total)
        n2[l] = normal
        i2[l] = inverse
        next_x = normal * row(l, ROW_GAIN + 1) + row(l, ROW_SHIFT + 1)
        x[...] = next_x
        if l + 1 < levels:
            xl[l + 1][...] = low(next_x)
            send_stream(l + 1)

    def note(l, index, value):
        small[l, index : index + 1, :] = value

    def by_copy(l):
        return remote(sc.at[l], rc.at[l], by_send.at[l], by_recv.at[l], across)

    def bc_copy(l):
        return remote(sb.at[l], rb.at[l], bc_send.at[l], bc_recv.at[l], sibling)

    gx = stream_grad

    def backward(l):
        sum_a, sum_f = sums[l]
        grad = gx[...]
        note(l, ROW_GAIN + 1, column_sums(grad * n2[l]))
        note(l, ROW_SHIFT + 1, column_sums(grad))
        g2 = normalize_back(grad, n2[l], i2[l], row(l, ROW_GAIN + 1))
        d_ff = low(g2 + residue_grad[...])
        note(l, ROW_OUT_BIAS, column_sums(wide(d_ff)))
        total = g2
        for j in range(parts):
            keep_out(j, product_tokens(act[l, j], d_ff))
            d_hidden = low(product_rows(d_ff, out_weight(l, j)) * wide(slope[l, j]))
            note(l, ROW_IN_BIAS + j, column_sums(wide(d_hidden)))
            keep(g_f, j * width, product_tokens(mid[l], d_hidden))
            total = total + product_rows(d_hidden, weight(l, row_in + j * width))
            tick(1)
        tick(4)
        sum_f.begin()
        note(l, ROW_GAIN, column_sums(total * n1[l]))
        note(l, ROW_SHIFT, column_sums(total))
        g1 = normalize_back(total, n1[l], i1[l], row(l, ROW_GAIN))
        gx[...] = g1
        d_att = low(g1 + residue_grad[...])
        note(l, ROW_ATT_BIAS + 2, column_sums(wide(d_att)))
        keep(g_a, 3 * width, product_tokens(att[l], d_att))
        att[l] = low(product_rows(d_att, weight(l, 3 * width)))
        while waiting:
            tick(1)
        one, two, three = sum_f.steps()
        waiting.extend(one + two + three)
        tick(4)
        for b in range(3):
            kt[:, b * tokens : (b + 1) * tokens] = jnp.transpose(kv[l, b, :, 0:features])

        def attend(p, carry):
            start = pl.multiple_of(p * lanes, lanes)
            at, at_values = pl.ds(start, lanes), pl.ds(start + features, lanes)
            queries, d_out = qs[l, :, at], att[l, :, at]
            values = kv[l, :, :, at_values].reshape(3 * tokens, lanes)
            d_keys = jnp.zeros((3 * tokens, lanes), jnp.float32)
            d_values = jnp.zeros((3 * tokens, lanes), jnp.float32)
            for side in range(2):
                own = one_head(d_out, side)
                probs = pt[l, 2 * p + side]
                terms = product_rows(values, own)
                weighted = terms * wide(probs)
                d_scores = low(weighted - wide(probs) * jnp.sum(weighted, axis=0, keepdims=True))
                d_values = d_values + product(probs, own)
                d_keys = d_keys + product(d_scores, one_head(queries, side))
                rows = pl.ds(pl.multiple_of(p * lanes + side * head, head), head)
                ob[rows, :] = product(kt[rows, :], d_scores)
            for where, value in ((at, d_keys), (at_values, d_values)):
                dkv[0, :, where] = value[:tokens]
                sb[l, :, where] = low(value[tokens : 2 * tokens])
                dkv[1, :, where] = value[2 * tokens :]
            return carry

        lax.fori_loop(0, pairs, attend, 0)

        @pl.when((c == 1) | (y == 1))
        def _():
            bc_copy(l).start()

        @pl.when((y == 1) & (c == 1))
        def _():
            bc_copy(l).wait_recv()
            dkv[1] = dkv[1] + wide(rb[l])

        far_keys, far_values = low(dkv[1, :, 0:features]), low(dkv[1, :, features:])

        @pl.when(y == 1)
        def _():
            sc[l] = low(product_rows(far_keys, weight(l, width)) + product_rows(far_values, weight(l, 2 * width)))
            by_copy(l).start()

        tick(4)
        d_queries = low(jnp.transpose(ob[...]) * (1.0 / math.sqrt(head)))
        keep(g_a, 0, product_tokens(xl[l][...], d_queries))
        note(l, ROW_ATT_BIAS, column_sums(wide(d_queries)))

        @pl.when(c == 0)
        def _():
            bc_copy(l).wait_recv()
            dkv[0] = dkv[0] + wide(rb[l])

        d_keys, d_values = low(dkv[0, :, 0:features]), low(dkv[0, :, features:])
        keep(g_a, width, product_tokens(xl[l][...], d_keys) + product_tokens(xn[l], far_keys))
        keep(g_a, 2 * width, product_tokens(xl[l][...], d_values) + product_tokens(xn[l], far_values))
        note(l, ROW_ATT_BIAS + 1, column_sums(wide(d_values)) + column_sums(wide(far_values)))
        sum_a.begin()
        tick(4)
        gx[...] = (
            gx[...]
            + product_rows(d_queries, weight(l, 0))
            + product_rows(d_keys, weight(l, width))
            + product_rows(d_values, weight(l, 2 * width))
        )
        while waiting:
            tick(1)

        @pl.when(y == 0)
        def _():
            by_copy(l).wait_recv()
            gx[...] = gx[...] + wide(rc[l])

        one, two, three = sum_a.steps()
        waiting.extend(one + two + three)

    def store_f(l):
        sum_f = sums[l][1]
        sum_f.finish()
        for n in range(parts):
            ff_in_grad[l, :, n * features : (n + 1) * features] = sum_f.total[n * width : (n + 1) * width]
        ff_out_grad[l] = sum_f.total[parts * width :]

    def store_a(l):
        sum_a = sums[l][0]
        sum_a.finish()
        for n in range(3):
            qkv_grad[l, :, n * features : (n + 1) * features] = sum_a.total[n * width : (n + 1) * width]
        out_grad[l] = sum_a.total[3 * width :]

    for l in range(levels):
        forward(l)
    last = levels - 1
    normal, inverse = normalize(r[...])
    gain = row(last, ROW_FINAL)
    out[...] = x[...] + normal * gain + row(last, ROW_FINAL + 1)
    grad = cot[...]
    note(last, ROW_FINAL, column_sums(grad * normal))
    note(last, ROW_FINAL + 1, column_sums(grad))
    residue_grad[...] = normalize_back(grad, normal, inverse, gain)
    gx[...] = grad
    for l in reversed(range(levels)):
        backward(l)
        store_f(l)
        if l + 1 < levels:
            store_a(l + 1)

    lines = [
        [sibling],
        [geo.device(z, lax.rem(xx + i, geo.nx), y, c) for i in range(1, geo.nx)],
        [geo.device(z, xx, lax.rem(y + j, geo.ny), c) for j in range(1, geo.ny)],
        [geo.device(lax.rem(z + k, nz), xx, y, c) for k in range(1, nz)],
    ]

    first = [sum(len(line) for line in lines[:p]) for p in range(4)]

    def small_copies(p):
        return [
            remote(sbuf.at[p], sin.at[first[p] + n], s_send.at[first[p] + n], s_recv.at[first[p] + n], device)
            for n, device in enumerate(lines[p])
        ]

    def small_start(p, value):
        sbuf[p] = value
        for copy in small_copies(p):
            copy.start()

    def small_sum(p):
        total = sbuf[p]
        for n, copy in enumerate(small_copies(p)):
            copy.wait()
            total = total + sin[first[p] + n]
        return total

    small_start(0, small[...].reshape(levels * ROWS, features))
    for p in range(1, 4):
        tick(4)
        small_start(p, small_sum(p - 1))
    total = small_sum(3)
    hot = jnp.where(
        lax.broadcasted_iota(jnp.int32, (features, width), 0)
        == shard * width + lax.broadcasted_iota(jnp.int32, (features, width), 1),
        1.0,
        0.0,
    )
    ff_hot = jnp.where(
        lax.broadcasted_iota(jnp.int32, (features, ff_rows), 0)
        == ff_lane + lax.broadcasted_iota(jnp.int32, (features, ff_rows), 1),
        1.0,
        0.0,
    )
    exact = functools.partial(jnp.dot, preferred_element_type=jnp.float32, precision=lax.Precision.HIGHEST)
    mine = exact(total, hot)
    part = lax.broadcasted_iota(jnp.int32, (ROWS, 1), 0)
    for l in range(levels):
        own = mine[l * ROWS : (l + 1) * ROWS]
        att_grad[l] = own[ROW_ATT_BIAS:ROW_IN_BIAS]
        ff_row = column_sums(jnp.where(part == ROW_IN_BIAS + z, total[l * ROWS : (l + 1) * ROWS], 0.0))
        in_bias_grad[l : l + 1, :] = exact(jnp.broadcast_to(ff_row, (8, features)), ff_hot)[0:1]
        out_bias_grad[l : l + 1, :] = own[ROW_OUT_BIAS : ROW_OUT_BIAS + 1]
        gain_grad[l] = own[ROW_GAIN : ROW_GAIN + 2]
        shift_grad[l] = own[ROW_SHIFT : ROW_SHIFT + 2]
    final_gain_grad[...] = own[ROW_FINAL : ROW_FINAL + 1]
    final_shift_grad[...] = own[ROW_FINAL + 1 : ROW_FINAL + 2]
    store_a(0)

    for l in range(levels):
        for piece in pieces[l]:
            piece.finish()

        @pl.when(y == 0)
        def _(l=l):
            y_copy(l).wait_send()

        @pl.when((y == 1) | (c == 0))
        def _(l=l):
            c_copy(l, 0).wait_send()

        @pl.when((c == 1) | (y == 1))
        def _(l=l):
            bc_copy(l).wait_send()

        @pl.when(y == 1)
        def _(l=l):
            by_copy(l).wait_send()


def run_step(geo, stream_in, residue_in, seg, cot, shards):
    tokens, features = residue_in.shape
    levels, width, qkv_columns = shards[0].shape
    parts = shards[2].shape[2] // features
    ff_rows = shards[3].shape[1]
    rows_a, rows_f = 4 * width, parts * width + ff_rows
    shape = (geo.nz, geo.nx, geo.ny, 2)
    dma, vmem = pltpu.SemaphoreType.DMA, pltpu.VMEM
    wide_kind, kind = jnp.float32, jnp.bfloat16
    whole = pl.BlockSpec(memory_space=pltpu.VMEM)
    away = pl.BlockSpec(memory_space=pl.ANY)
    row = (tokens, features)
    half_a, half_f = 2 * width, 3 * width
    others = geo.nx + geo.ny + geo.nz - 2
    outs = [row, row, row] + [member.shape for member in shards]
    scratch = [
        vmem((levels,) + shape + (rows_a + ROWS + rows_f, features), kind),
        vmem((levels, ROWS, features), wide_kind),
        vmem((levels, ROWS, features), wide_kind),
        vmem((levels - 1,) + row, kind),
        vmem((levels,) + row, kind),
        vmem((levels,) + row, kind),
        vmem((levels, 3, tokens, 2 * features), kind),
        vmem((features, 3 * tokens), kind),
        vmem((levels, HEADS, 3 * tokens, tokens), kind),
        vmem((levels,) + row, kind),
        vmem((levels,) + row, kind),
        vmem((levels, parts) + row, kind),
        vmem((levels, parts) + row, kind),
        vmem((levels,) + row, wide_kind),
        vmem((levels,) + row, wide_kind),
        vmem((levels, tokens, 1), wide_kind),
        vmem((levels, tokens, 1), wide_kind),
        vmem((3, tokens, tokens), wide_kind),
        vmem((geo.seq, 8, tokens), jnp.int32),
        vmem((2, tokens, 2 * features), wide_kind),
        vmem((features, tokens), wide_kind),
        vmem((levels, tokens, 2 * features), kind),
        vmem((levels,) + row, kind),
        vmem((levels, tokens, 2 * features), kind),
        vmem((levels,) + row, kind),
        vmem((levels, ROWS, features), wide_kind),
        vmem((4, levels * ROWS, features), wide_kind),
        vmem((others, levels * ROWS, features), wide_kind),
    ]
    scratch += Scatter.buffers(geo, levels, rows_a, half_a, features, kind)
    scratch += Scatter.buffers(geo, levels, rows_f, half_f, features, kind)
    scratch += Gather.semaphores(geo, 2 * levels) + Scatter.semaphores(geo, 2 * levels)
    scratch += [dma((levels, 5 + parts))] + [dma((geo.seq,))] * 2 + [dma((levels,))] * 8 + [dma((others,))] * 2 + [dma(())]
    return pl.pallas_call(
        functools.partial(step_kernel, geo, half_a, half_f),
        out_shape=tuple(jax.ShapeDtypeStruct(shape_of, wide_kind) for shape_of in outs),
        in_specs=[whole, away, whole, whole] + [away] * 4 + [whole] * 7,
        out_specs=(whole,) * len(outs),
        scratch_shapes=scratch,
        compiler_params=pltpu.CompilerParams(
            collective_id=0, has_side_effects=True, vmem_limit_bytes=64 << 20
        ),
        name="run_step",
    )(stream_in, residue_in, seg, cot, *shards)


def gather_plain(shards, number):
    gathered = [
        lax.all_gather(shards[member][number], ("dp", "seq"), axis=axis, tiled=True)
        for member, axis in enumerate((0, 0, 0, 0, 1, 0, 0, 1, 1))
    ]
    return tuple(gathered) + tuple(
        lax.all_gather(shards[member], ("dp", "seq"), axis=0, tiled=True) for member in (9, 10)
    )


def body_plain(geo, *args):
    stream_in, residue_in, segments, out_cot = args[:4]
    shards = args[4:]
    levels, width, _ = shards[1].shape
    ff_width = shards[3].shape[1]
    stream = stream_in[0].astype(jnp.float32)
    residue = residue_in[0]
    cotangent = out_cot[0]
    tokens = stream.shape[0]
    query_seg = segments[0]
    whole_seg = lax.all_gather(query_seg, "seq", axis=0, tiled=True)
    seq_index = lax.axis_index("seq")
    query_pos = seq_index * tokens + jnp.arange(tokens, dtype=jnp.int32)
    weights = [gather_plain(shards, number) for number in range(levels)]
    states = []
    for number in range(levels):
        stream, residue, state = layer_forward(stream, residue, weights[number], query_pos, query_seg, whole_seg)
        states.append(state)
    final_norm, pull_final = jax.vjp(
        layer_norm,
        residue,
        weights[-1][9].astype(jnp.float32),
        weights[-1][10].astype(jnp.float32),
    )
    output = stream + final_norm
    grad_residue, final_gain_grad, final_shift_grad = pull_final(cotangent)
    grad_stream = cotangent
    grads = [None] * levels
    for number in reversed(range(levels)):
        grad_stream, grads[number] = layer_backward(
            states[number], weights[number], grad_stream, grad_residue, query_pos, query_seg
        )
    summed = [
        jnp.stack(
            [
                lax.psum_scatter(grads[number][member], ("dp", "seq"), scatter_dimension=axis, tiled=True)
                for number in range(levels)
            ]
        )
        for member, axis in enumerate((0, 0, 0, 0, 1, 0, 0, 1, 1))
    ] + [
        lax.psum_scatter(final_gain_grad, ("dp", "seq"), scatter_dimension=0, tiled=True),
        lax.psum_scatter(final_shift_grad, ("dp", "seq"), scatter_dimension=0, tiled=True),
    ]
    return (output[None], grad_stream[None], grad_residue[None]) + tuple(summed)


def body(geo, *args):
    stream_in, residue_in, segments, out_cot = args[:4]
    shards = list(args[4:])
    shards[-2:] = [shards[-2][None], shards[-1][None]]
    tokens = stream_in.shape[1]
    seg = jnp.broadcast_to(segments, (8, tokens))
    results = run_step(geo, stream_in[0], residue_in[0], seg, out_cot[0], shards)
    return tuple(value[None] for value in results[:3]) + tuple(results[3:-2]) + (results[-2][0], results[-1][0])


def solution(mesh):
    geo = Geometry(mesh)
    chosen = body if geo.seq == 4 and geo.nz == 4 else body_plain
    return jax.shard_map(
        functools.partial(chosen, geo),
        mesh=mesh,
        in_specs=(
            P("dp", "seq", None),
            P("dp", "seq", None),
            P("dp", "seq"),
            P("dp", "seq", None),
            P(None, ("dp", "seq"), None),
            P(None, ("dp", "seq"), None),
            P(None, ("dp", "seq"), None),
            P(None, ("dp", "seq"), None),
            P(None, None, ("dp", "seq")),
            P(None, ("dp", "seq")),
            P(None, ("dp", "seq")),
            P(None, None, ("dp", "seq")),
            P(None, None, ("dp", "seq")),
            P(("dp", "seq")),
            P(("dp", "seq")),
        ),
        out_specs=(
            P("dp", "seq", None),
            P("dp", "seq", None),
            P("dp", "seq", None),
            P(None, ("dp", "seq"), None),
            P(None, ("dp", "seq"), None),
            P(None, ("dp", "seq"), None),
            P(None, ("dp", "seq"), None),
            P(None, None, ("dp", "seq")),
            P(None, ("dp", "seq")),
            P(None, ("dp", "seq")),
            P(None, None, ("dp", "seq")),
            P(None, None, ("dp", "seq")),
            P(("dp", "seq")),
            P(("dp", "seq")),
        ),
        check_vma=False,
    )
```

```python
import functools
import itertools
import math

import jax
import jax.numpy as jnp
from jax import lax
from jax.experimental import pallas as pl
from jax.experimental.pallas import tpu as pltpu
from jax.sharding import PartitionSpec as P

HEADS = 8
MESH = pl.DeviceIdType.MESH


class Geometry:
    def __init__(self, mesh):
        self.dp, self.seq = mesh.shape["dp"], mesh.shape["seq"]
        self.ny = self.seq // 2
        self.nx = self.ny
        self.nz = self.dp // self.nx
        self.shards = self.dp * self.seq

    def here(self):
        dp, seq = lax.axis_index("dp"), lax.axis_index("seq")
        return lax.div(dp, self.nx), lax.rem(dp, self.nx), lax.div(seq, 2), lax.rem(seq, 2)

    def device(self, z, x, y, c):
        return (z * self.nx + x, y * 2 + c)

    def peers(self):
        z, x, y, c = self.here()
        found = [self.device(lax.rem(z + k, self.nz), x, y, c) for k in range(1, self.nz)]
        found += [self.device(z, lax.rem(x + k, self.nx), y, c) for k in range(1, self.nx)]
        found += [self.device(z, x, lax.rem(y + k, self.ny), c) for k in range(1, self.ny)]
        return found + [self.device(z, x, y, 1 - c)]


def greet(devices):
    barrier = pltpu.get_barrier_semaphore()
    for device in devices:
        pl.semaphore_signal(barrier, inc=1, device_id=device, device_id_type=MESH)
    pl.semaphore_wait(barrier, len(devices))


def remote(src, dst, send_sem, recv_sem, device):
    return pltpu.make_async_remote_copy(
        src_ref=src,
        dst_ref=dst,
        send_sem=send_sem,
        recv_sem=recv_sem,
        device_id=device,
        device_id_type=MESH,
    )


epsilon = 1e-05
masked_value = -1e30


def smooth_gate(values):
    return jax.nn.gelu(values, approximate=True)


def layer_norm(values, norm_gain, norm_shift):
    average = jnp.mean(values, axis=-1, keepdims=True)
    centred = values - average
    variance = jnp.mean(centred * centred, axis=-1, keepdims=True)
    return centred * lax.rsqrt(variance + epsilon) * norm_gain + norm_shift


def keep_state(carried):
    return carried


def allowed_pairs(query_pos, query_seg, key_pos, key_seg):
    return (query_seg[:, None] == key_seg[None, :]) & (key_pos[None, :] <= query_pos[:, None])


def block_needed(query_pos, query_seg, key_pos, key_seg):
    return (key_pos[0] <= query_pos[-1]) & (key_seg[-1] >= query_seg[0])


def key_blocks(keys_values, key_seg):
    length = keys_values.shape[0]
    features = keys_values.shape[1] // 2
    head_size = features // HEADS
    block_rows = math.gcd(length, 512)
    block_count = length // block_rows
    split_kv = keys_values.reshape(block_count, block_rows, 2, HEADS, head_size)
    key_pos = jnp.arange(length, dtype=jnp.int32).reshape(block_count, block_rows)
    return (split_kv[:, :, 0], split_kv[:, :, 1], key_pos, key_seg.reshape(block_count, block_rows))


def block_scores(queries3, key_block, query_pos, query_seg, key_pos, key_seg):
    scaling = 1.0 / math.sqrt(queries3.shape[-1])
    raw_scores = (
        jnp.einsum("qhd,khd->hqk", queries3, key_block, preferred_element_type=jnp.float32)
        * scaling
    )
    return (raw_scores, allowed_pairs(query_pos, query_seg, key_pos, key_seg)[None])


def attention_forward(queries3, blocks, query_pos, query_seg):
    tokens, head_count, head_size = queries3.shape

    def statistics(carried, block_items):
        key_block, value_block, key_pos, key_seg = block_items

        def statistics_compute(running):
            run_max, run_sum = running
            raw_scores, allowed = block_scores(
                queries3, key_block, query_pos, query_seg, key_pos, key_seg
            )
            new_max = jnp.maximum(
                run_max, jnp.max(jnp.where(allowed, raw_scores, masked_value), axis=-1)
            )
            exp_terms = jnp.exp(jnp.where(allowed, raw_scores - new_max[..., None], masked_value))
            return (new_max, run_sum * jnp.exp(run_max - new_max) + jnp.sum(exp_terms, axis=-1))

        needed = block_needed(query_pos, query_seg, key_pos, key_seg)
        return (lax.cond(needed, statistics_compute, keep_state, carried), None)

    initial = (
        jnp.full((head_count, tokens), masked_value, jnp.float32),
        jnp.zeros((head_count, tokens), jnp.float32),
    )
    (run_max, run_sum), unused = lax.scan(statistics, initial, blocks)
    log_total = run_max + jnp.log(run_sum)

    def accumulate(carried, block_items):
        key_block, value_block, key_pos, key_seg = block_items

        def accumulate_compute(running):
            raw_scores, allowed = block_scores(
                queries3, key_block, query_pos, query_seg, key_pos, key_seg
            )
            weights = jnp.exp(jnp.where(allowed, raw_scores - log_total[..., None], masked_value))
            weights = weights.astype(jnp.bfloat16)
            return running + jnp.einsum(
                "hqk,khd->qhd", weights, value_block, preferred_element_type=jnp.float32
            )

        needed = block_needed(query_pos, query_seg, key_pos, key_seg)
        return (lax.cond(needed, accumulate_compute, keep_state, carried), None)

    mixed_heads, unused = lax.scan(
        accumulate, jnp.zeros((tokens, head_count, head_size), jnp.float32), blocks
    )
    return (mixed_heads, log_total)


def attention_backward(queries3, blocks, query_pos, query_seg, log_total, mixed_heads, grad_heads):
    tokens, head_count, head_size = queries3.shape
    scaling = 1.0 / math.sqrt(head_size)
    row_dots = jnp.sum(mixed_heads * grad_heads.astype(jnp.float32), axis=-1).T
    block_rows = blocks[0].shape[1]
    block_count = blocks[0].shape[0]

    def backward_step(grad_queries, block_items):
        key_block, value_block, key_pos, key_seg = block_items

        def backward_compute(running):
            raw_scores, allowed = block_scores(
                queries3, key_block, query_pos, query_seg, key_pos, key_seg
            )
            prob_values = jnp.exp(
                jnp.where(allowed, raw_scores - log_total[..., None], masked_value)
            )
            grad_values = jnp.einsum(
                "hqk,qhd->khd",
                prob_values.astype(jnp.bfloat16),
                grad_heads,
                preferred_element_type=jnp.float32,
            )
            grad_probs = jnp.einsum(
                "qhd,khd->hqk", grad_heads, value_block, preferred_element_type=jnp.float32
            )
            grad_scores = (prob_values * (grad_probs - row_dots[..., None])).astype(jnp.bfloat16)
            running = (
                running
                + jnp.einsum(
                    "hqk,khd->qhd", grad_scores, key_block, preferred_element_type=jnp.float32
                )
                * scaling
            )
            grad_keys = (
                jnp.einsum(
                    "hqk,qhd->khd", grad_scores, queries3, preferred_element_type=jnp.float32
                )
                * scaling
            )
            return (running, grad_keys, grad_values)

        def skip_block(running):
            empty_rows = jnp.zeros((block_rows, head_count, head_size), jnp.float32)
            return (running, empty_rows, empty_rows)

        needed = block_needed(query_pos, query_seg, key_pos, key_seg)
        grad_queries, grad_keys, grad_values = lax.cond(
            needed, backward_compute, skip_block, grad_queries
        )
        return (grad_queries, (grad_keys, grad_values))

    initial = jnp.zeros((tokens, head_count, head_size), jnp.float32)
    grad_queries, (grad_keys, grad_values) = lax.scan(backward_step, initial, blocks)
    length = block_count * block_rows
    return (
        grad_queries.reshape(tokens, head_count * head_size),
        grad_keys.reshape(length, head_count * head_size),
        grad_values.reshape(length, head_count * head_size),
    )


def layer_forward(stream, residue, weights, query_pos, query_seg, key_seg):
    (
        qkv_weight,
        out_weight,
        ff_in_weight,
        ff_out_weight,
        att_bias,
        ff_in_bias,
        ff_out_bias,
        norm_gain,
        norm_shift,
    ) = weights[:9]
    tokens, features = stream.shape
    stream_low = stream.astype(jnp.bfloat16)
    bias_row = jnp.concatenate([att_bias[0], jnp.zeros_like(att_bias[0]), att_bias[1]]).astype(
        jnp.float32
    )
    joined = (
        jnp.dot(stream_low, qkv_weight, preferred_element_type=jnp.float32) + bias_row
    ).astype(jnp.bfloat16)
    queries3 = joined[:, :features].reshape(tokens, HEADS, features // HEADS)
    keys_values = lax.all_gather(joined[:, features:], "seq", axis=0, tiled=True)
    blocks = key_blocks(keys_values, key_seg)
    mixed_heads, log_total = attention_forward(queries3, blocks, query_pos, query_seg)
    attended = mixed_heads.reshape(tokens, features).astype(jnp.bfloat16)
    branch_att = jnp.dot(attended, out_weight, preferred_element_type=jnp.float32) + att_bias[
        2
    ].astype(jnp.float32)
    middle, pull_first = jax.vjp(
        layer_norm,
        stream + branch_att,
        norm_gain[0].astype(jnp.float32),
        norm_shift[0].astype(jnp.float32),
    )
    residue_mid = residue + branch_att
    middle_low = middle.astype(jnp.bfloat16)
    hidden = jnp.dot(
        middle_low, ff_in_weight, preferred_element_type=jnp.float32
    ) + ff_in_bias.astype(jnp.float32)
    active = smooth_gate(hidden).astype(jnp.bfloat16)
    branch_ff = jnp.dot(
        active, ff_out_weight, preferred_element_type=jnp.float32
    ) + ff_out_bias.astype(jnp.float32)
    stream_next, pull_second = jax.vjp(
        layer_norm,
        middle + branch_ff,
        norm_gain[1].astype(jnp.float32),
        norm_shift[1].astype(jnp.float32),
    )
    saved_state = (
        stream_low,
        queries3,
        blocks,
        mixed_heads,
        log_total,
        attended,
        pull_first,
        middle_low,
        hidden,
        active,
        pull_second,
    )
    return (stream_next, residue_mid + branch_ff, saved_state)


def layer_backward(saved_state, weights, grad_stream, grad_residue, query_pos, query_seg):
    (
        stream_low,
        queries3,
        blocks,
        mixed_heads,
        log_total,
        attended,
        pull_first,
        middle_low,
        hidden,
        active,
        pull_second,
    ) = saved_state
    qkv_weight, out_weight, ff_in_weight, ff_out_weight = weights[:4]
    grad_second, gain_second, shift_second = pull_second(grad_stream)
    grad_ff = (grad_second + grad_residue).astype(jnp.bfloat16)
    grad_ff_out = jnp.einsum("tf,td->fd", active, grad_ff, preferred_element_type=jnp.float32)
    bias_ff_out = jnp.sum(grad_ff.astype(jnp.float32), axis=0)
    grad_active = jnp.einsum(
        "td,fd->tf", grad_ff, ff_out_weight, preferred_element_type=jnp.float32
    )
    unused_gate, pull_gate = jax.vjp(smooth_gate, hidden)
    grad_hidden = pull_gate(grad_active)[0].astype(jnp.bfloat16)
    grad_ff_in = jnp.einsum(
        "td,tf->df", middle_low, grad_hidden, preferred_element_type=jnp.float32
    )
    bias_ff_in = jnp.sum(grad_hidden.astype(jnp.float32), axis=0)
    grad_middle = grad_second + jnp.einsum(
        "tf,df->td", grad_hidden, ff_in_weight, preferred_element_type=jnp.float32
    )
    grad_first, gain_first, shift_first = pull_first(grad_middle)
    grad_att = (grad_first + grad_residue).astype(jnp.bfloat16)
    grad_out = jnp.einsum("te,td->ed", attended, grad_att, preferred_element_type=jnp.float32)
    bias_att_out = jnp.sum(grad_att.astype(jnp.float32), axis=0)
    grad_attended = jnp.einsum(
        "td,ed->te", grad_att, out_weight, preferred_element_type=jnp.float32
    )
    grad_attended = grad_attended.astype(jnp.bfloat16)
    tokens, features = grad_attended.shape
    grad_queries, grad_keys, grad_values = attention_backward(
        queries3,
        blocks,
        query_pos,
        query_seg,
        log_total,
        mixed_heads,
        grad_attended.reshape(tokens, HEADS, features // HEADS),
    )
    key_grads, value_grads = (
        lax.psum_scatter(
            grad_keys.astype(jnp.bfloat16), "seq", scatter_dimension=0, tiled=True
        ).astype(jnp.float32),
        lax.psum_scatter(
            grad_values.astype(jnp.bfloat16), "seq", scatter_dimension=0, tiled=True
        ).astype(jnp.float32),
    )
    grad_joined = jnp.concatenate([grad_queries, key_grads, value_grads], axis=1).astype(
        jnp.bfloat16
    )
    grad_qkv = jnp.einsum("td,te->de", stream_low, grad_joined, preferred_element_type=jnp.float32)
    column_sums = jnp.sum(grad_joined.astype(jnp.float32), axis=0)
    bias_att = jnp.stack([column_sums[:features], column_sums[2 * features :], bias_att_out])
    grad_stream_in = grad_first + jnp.einsum(
        "te,de->td", grad_joined, qkv_weight, preferred_element_type=jnp.float32
    )
    layer_grads = (
        grad_qkv,
        grad_out,
        grad_ff_in,
        grad_ff_out,
        bias_att,
        bias_ff_in,
        bias_ff_out,
        jnp.stack([gain_first, gain_second]),
        jnp.stack([shift_first, shift_second]),
    )
    return (grad_stream_in, layer_grads)


def product(left, right):
    return lax.dot_general(left, right, (((1,), (0,)), ((), ())), preferred_element_type=jnp.float32)


def product_rows(left, right):
    return lax.dot_general(left, right, (((1,), (1,)), ((), ())), preferred_element_type=jnp.float32)


def product_tokens(left, right):
    return lax.dot_general(left, right, (((0,), (0,)), ((), ())), preferred_element_type=jnp.float32)


def wide(value):
    return value.astype(jnp.float32)


def low(value):
    return value.astype(jnp.bfloat16)


def normalize(values):
    centred = values - jnp.mean(values, axis=-1, keepdims=True)
    inverse = lax.rsqrt(jnp.mean(centred * centred, axis=-1, keepdims=True) + epsilon)
    return centred * inverse, inverse


def normalize_back(grad, normal, inverse, gain):
    scaled = grad * gain
    return (
        scaled
        - jnp.mean(scaled, axis=-1, keepdims=True)
        - normal * jnp.mean(scaled * normal, axis=-1, keepdims=True)
    ) * inverse


def column_sums(values):
    return jnp.sum(values, axis=0, keepdims=True)


def gelu_pair(v):
    rate = math.sqrt(2.0 / math.pi)
    square = v * v
    bent = jnp.tanh(v * (rate + (rate * 0.044715) * square))
    rise = 0.5 + 0.5 * bent
    slope = rise + v * (0.5 - 0.5 * bent * bent) * (rate + (3.0 * rate * 0.044715) * square)
    return v * rise, slope


class Gather:
    def __init__(self, geo, w, l, start, segments, sems, number):
        self.geo, self.w, self.l, self.start, self.segments = geo, w, l, start, segments
        self.send, self.recv, self.c_send, self.c_recv = (sem.at[number] for sem in sems)
        self.here = geo.here()
        self.sizes = (geo.nz, geo.nx, geo.ny)
        self.size = sum(size for size, _ in segments)
        offsets = list(itertools.product(*map(range, self.sizes)))
        self.offsets = sorted(offsets, key=lambda offset: sum(1 for step in offset if step))

    def source(self, number, offset):
        axis = [axis for axis in map("zxy".index, self.segments[number][1]) if offset[axis]][-1]
        return tuple(0 if n == axis else step for n, step in enumerate(offset)), axis

    def copies(self, offset):
        ways = [self.source(number, offset) for number in range(len(self.segments))]
        starts = [self.start + sum(size for size, _ in self.segments[:n]) for n in range(len(ways))]
        rows = [(n, way, starts[n], self.segments[n][0]) for n, way in enumerate(ways)]
        if len(set(ways)) == 1:
            rows = [(0, ways[0], self.start, self.size)]
        found = []
        for number, (source, axis), start, size in rows:
            place = [lax.rem(mine + n - step, n) for mine, n, step in zip(self.here, self.sizes, source)]
            piece = self.w.at[(self.l, *place, self.here[3], pl.ds(start, size))]
            target = list(self.here)
            target[axis] = lax.rem(target[axis] + offset[axis], self.sizes[axis])
            index = (number, *offset)
            copy = remote(piece, piece, self.send.at[index], self.recv.at[index], self.geo.device(*target))
            found.append((copy, source))
        return found

    def c_copy(self, k):
        z, x, y, c = self.here
        piece = self.w.at[self.l, lax.rem(z + self.sizes[0] - k, self.sizes[0]), :, :, c, pl.ds(self.start, self.size)]
        return remote(piece, piece, self.c_send.at[k], self.c_recv.at[k], self.geo.device(z, x, y, 1 - c))

    def spread(self, offset):
        for other in self.offsets[1:]:
            for copy, source in self.copies(other):
                if source == offset:
                    copy.start()
        if offset[1:] == (self.sizes[1] - 1, self.sizes[2] - 1):
            self.c_copy(offset[0]).start()

    def own(self):
        self.spread(self.offsets[0])

    def step(self, offset):
        for copy, _ in self.copies(offset):
            copy.wait_recv()
        self.spread(offset)

    def steps(self, hops):
        return [
            functools.partial(self.step, offset)
            for offset in self.offsets
            if sum(1 for step in offset if step) == hops
        ]

    def arrive(self):
        for k in range(self.sizes[0]):
            self.c_copy(k).wait_recv()

    def finish(self):
        for k in range(self.sizes[0]):
            self.c_copy(k).wait_send()
        for offset in self.offsets[1:]:
            for copy, _ in self.copies(offset):
                copy.wait_send()

    @staticmethod
    def semaphores(geo, count, segments):
        dma = pltpu.SemaphoreType.DMA
        return [dma((count, segments, geo.nz, geo.nx, geo.ny))] * 2 + [dma((count, geo.nz))] * 2


class Scatter:
    def __init__(self, geo, g, own, r1h, r1l, r2h, r2l, zin, total, l, cut, sems, number):
        self.geo, self.g, self.own, self.l, self.cut = geo, g, own.at[l], l, cut
        self.r1h, self.r1l, self.r2h, self.r2l, self.zin = (ref.at[l] for ref in (r1h, r1l, r2h, r2l, zin))
        self.total = total
        self.rows = g.shape[4]
        self.sems = [sem.at[number] for sem in sems]
        self.z, self.x, self.y, self.c = geo.here()
        self.order = list(range(1, geo.nz)) + [0]

    def copy(self, src, dst, number, index, device):
        return remote(src, dst, self.sems[number].at[index], self.sems[number + 1].at[index], device)

    def cross(self, k):
        return self.copy(
            self.g.at[lax.rem(self.z + k, self.geo.nz), :, :, 1 - self.c], self.own.at[k], 0, (k,),
            self.geo.device(self.z, self.x, self.y, 1 - self.c),
        )

    def to_x(self, src, dst, number, index, i):
        return self.copy(src, dst, number, index, self.geo.device(self.z, lax.rem(self.x + i, self.geo.nx), self.y, self.c))

    def to_y(self, src, dst, number, index, j):
        return self.copy(src, dst, number, index, self.geo.device(self.z, self.x, lax.rem(self.y + j, self.geo.ny), self.c))

    def one(self, k):
        nx, ny = self.geo.nx, self.geo.ny
        top, rest = pl.ds(0, self.cut), pl.ds(self.cut, self.rows - self.cut)
        return [
            self.to_y(self.own.at[k, :, lax.rem(self.y + j, ny), top], self.r1h.at[k, j - 1], 2, (k, j - 1), j)
            for j in range(1, ny)
        ] + [
            self.to_x(self.own.at[k, lax.rem(self.x + i, nx), :, rest], self.r1l.at[k, i - 1], 4, (k, i - 1), i)
            for i in range(1, nx)
        ]

    def two(self, k):
        nx, ny = self.geo.nx, self.geo.ny
        top, rest = pl.ds(0, self.cut), pl.ds(self.cut, self.rows - self.cut)
        return [
            self.to_x(self.own.at[k, lax.rem(self.x + i, nx), self.y, top], self.r2h.at[k, i - 1], 6, (k, i - 1), i)
            for i in range(1, nx)
        ] + [
            self.to_y(self.own.at[k, self.x, lax.rem(self.y + j, ny), rest], self.r2l.at[k, j - 1], 8, (k, j - 1), j)
            for j in range(1, ny)
        ]

    def three(self, k):
        return self.copy(
            self.own.at[k, self.x, self.y], self.zin.at[k - 1], 10, (k - 1,),
            self.geo.device(lax.rem(self.z + k, self.geo.nz), self.x, self.y, self.c),
        )

    def begin(self):
        for k in self.order:
            self.cross(k).start()

    def step_one(self, k):
        own = self.own
        self.cross(k).wait()
        for i in range(self.geo.nx):
            for j in range(self.geo.ny):
                mine = self.g[lax.rem(self.z + k, self.geo.nz), i, j, self.c]
                own[k, i, j] = low(wide(mine) + wide(own[k, i, j]))
        for copy in self.one(k):
            copy.start()

    def step_two(self, k):
        own, x, y = self.own, self.x, self.y
        top, rest = pl.ds(0, self.cut), pl.ds(self.cut, self.rows - self.cut)
        for copy in self.one(k):
            copy.wait()
        for i in range(self.geo.nx):
            total = wide(own[k, i, y, top])
            for j in range(1, self.geo.ny):
                total = total + wide(self.r1h[k, j - 1, i])
            own[k, i, y, top] = low(total)
        for j in range(self.geo.ny):
            total = wide(own[k, x, j, rest])
            for i in range(1, self.geo.nx):
                total = total + wide(self.r1l[k, i - 1, j])
            own[k, x, j, rest] = low(total)
        for copy in self.two(k):
            copy.start()

    def step_three(self, k):
        own, x, y = self.own, self.x, self.y
        top, rest = pl.ds(0, self.cut), pl.ds(self.cut, self.rows - self.cut)
        for copy in self.two(k):
            copy.wait()
        upper = wide(own[k, x, y, top])
        for i in range(1, self.geo.nx):
            upper = upper + wide(self.r2h[k, i - 1])
        lower = wide(own[k, x, y, rest])
        for j in range(1, self.geo.ny):
            lower = lower + wide(self.r2l[k, j - 1])
        if k:
            own[k, x, y, top] = low(upper)
            own[k, x, y, rest] = low(lower)
            self.three(k).start()
        else:
            self.total[top] = upper
            self.total[rest] = lower

    def finish(self):
        total = self.total[...]
        for k in range(1, self.geo.nz):
            self.three(k).wait()
            total = total + wide(self.zin[k - 1])
        self.total[...] = total

    def steps(self):
        return [
            [functools.partial(step, k) for k in self.order]
            for step in (self.step_one, self.step_two, self.step_three)
        ]

    @staticmethod
    def buffers(geo, levels, rows, cut, columns, kind):
        vmem = pltpu.VMEM
        nz, nx, ny = geo.nz, geo.nx, geo.ny
        rest = rows - cut
        return [
            vmem((nz, nx, ny, 2, rows, columns), kind),
            vmem((levels, nz, nx, ny, rows, columns), kind),
            vmem((levels, nz, ny - 1, nx, cut, columns), kind),
            vmem((levels, nz, nx - 1, ny, rest, columns), kind),
            vmem((levels, nz, nx - 1, cut, columns), kind),
            vmem((levels, nz, ny - 1, rest, columns), kind),
            vmem((levels, nz - 1, rows, columns), kind),
            vmem((rows, columns), jnp.float32),
        ]

    @staticmethod
    def semaphores(geo, count):
        dma = pltpu.SemaphoreType.DMA
        nz, nx, ny = geo.nz, geo.nx, geo.ny
        return (
            [dma((count, nz))] * 2
            + [dma((count, nz, ny - 1))] * 2
            + [dma((count, nz, nx - 1))] * 2
            + [dma((count, nz, nx - 1))] * 2
            + [dma((count, nz, ny - 1))] * 2
            + [dma((count, nz - 1))] * 2
        )


ROW_ATT_BIAS, ROW_IN_BIAS, ROW_OUT_BIAS, ROW_GAIN, ROW_SHIFT, ROW_FINAL, ROWS = 0, 3, 7, 8, 10, 12, 16


def step_kernel(geo, routes_a, routes_f, half_a, half_f, *refs):
    refs = list(refs)

    def take(count):
        taken = refs[:count]
        del refs[:count]
        return taken

    (stream_in, residue_in, seg, cot, qkv_in, out_in, ff_in_in, ff_out_in, att_in, in_bias_in, out_bias_in, gain_in,
     shift_in, final_gain_in, final_shift_in) = take(15)
    (out, stream_grad, residue_grad, qkv_grad, out_grad, ff_in_grad, ff_out_grad, att_grad, in_bias_grad, out_bias_grad,
     gain_grad, shift_grad, final_gain_grad, final_shift_grad) = take(14)
    (w, par, own_small, xl_next, xn, qs, kv, kt, pt, att, mid, act, slope, n1, n2, i1, i2, bias, segs, dkv, ob, sb, sc,
     rb, rc, small, sbuf, sin) = take(28)
    buffers_a, buffers_f = take(8), take(8)
    gather_sems, scatter_sems = take(4), take(12)
    (load_sem, seg_send, seg_recv, y_send, y_recv, c_send, c_recv, by_send, by_recv, bc_send, bc_recv, s_send,
     s_recv, residue_sem) = take(14)
    assert not refs

    z, xx, y, c = geo.here()
    s = 2 * y + c
    shard = (z * geo.nx + xx) * geo.seq + s
    count = geo.seq
    tokens, features = residue_in.shape
    levels = w.shape[0]
    width = features // geo.shards
    ff_rows = in_bias_in.shape[1]
    head = features // HEADS
    lanes = 2 * head
    pairs = features // lanes
    parts = act.shape[1]
    sibling, across = geo.device(z, xx, y, 1 - c), geo.device(z, xx, 1 - y, c)
    row_in = 4 * width + ROWS
    row_out = row_in + parts * width
    xl = [stream_in] + [xl_next.at[l - 1] for l in range(1, levels)]

    pieces = [
        (
            Gather(geo, w, l, 0, routes_a, gather_sems, 2 * l),
            Gather(geo, w, l, row_in, routes_f, gather_sems, 2 * l + 1),
        )
        for l in range(levels)
    ]
    sums = [
        (
            Scatter(geo, *buffers_a, l, half_a, scatter_sems, 2 * l),
            Scatter(geo, *buffers_f, l, half_f, scatter_sems, 2 * l + 1),
        )
        for l in range(levels)
    ]

    def own_loads(l):
        mine = w.at[l, z, xx, y, c]
        pairs_of = [(qkv_in.at[l, :, pl.ds(n * features, features)], n * width, width) for n in range(3)]
        pairs_of.append((out_in.at[l], 3 * width, width))
        for n in range(parts):
            pairs_of.append((ff_in_in.at[l, :, pl.ds(n * features, features)], row_in + n * width, width))
        pairs_of.append((ff_out_in.at[l], row_out, ff_rows))
        return [
            pltpu.make_async_copy(src, mine.at[pl.ds(start, size)], load_sem.at[l, n])
            for n, (src, start, size) in enumerate(pairs_of)
        ]

    for l in range(levels):
        for copy in own_loads(l):
            copy.start()
    lane = lax.broadcasted_iota(jnp.int32, (width, features), 1)
    place = low(jnp.where(lane == shard * width + lax.broadcasted_iota(jnp.int32, (width, features), 0), 1.0, 0.0))
    lane = lax.broadcasted_iota(jnp.int32, (ff_rows, features), 1)
    ff_lane = lax.rem(shard, features // ff_rows) * ff_rows
    ff_place = low(jnp.where(lane == ff_lane + lax.broadcasted_iota(jnp.int32, (ff_rows, features), 0), 1.0, 0.0))
    own_small[...] = jnp.zeros_like(own_small)
    for l in range(levels):
        own_small[l, ROW_ATT_BIAS : ROW_ATT_BIAS + 3, :] = product(att_in[l], place)
        spread = product(in_bias_in[l : l + 1, :], ff_place)
        for j in range(parts):
            own_small[l, ROW_IN_BIAS + j : ROW_IN_BIAS + j + 1, :] = jnp.where(z == j, spread, 0.0)
        own_small[l, ROW_OUT_BIAS : ROW_OUT_BIAS + 1, :] = product(out_bias_in[l : l + 1, :], place)
        own_small[l, ROW_GAIN : ROW_GAIN + 2, :] = product(gain_in[l], place)
        own_small[l, ROW_SHIFT : ROW_SHIFT + 2, :] = product(shift_in[l], place)
        own_small[l, ROW_FINAL : ROW_FINAL + 1, :] = product(final_gain_in[...], place)
        own_small[l, ROW_FINAL + 1 : ROW_FINAL + 2, :] = product(final_shift_in[...], place)
        w[l, z, xx, y, c, 4 * width : row_in, :] = low(own_small[l])

    segs[0] = seg[...]
    greet(
        [geo.device(lax.rem(z + k, geo.nz), xx, y, c) for k in range(1, geo.nz)]
        + [
            geo.device(z, lax.rem(xx + i, geo.nx), lax.rem(y + j, geo.ny), lax.rem(c + k, 2))
            for i in range(geo.nx)
            for j in range(geo.ny)
            for k in range(2)
            if i or j or k
        ]
    )
    line = [(z * geo.nx + xx, lax.rem(s + k, count)) for k in range(1, count)]

    def seg_copy(k):
        return remote(segs.at[0], segs.at[k], seg_send.at[k], seg_recv.at[k], line[k - 1])

    def y_copy(l):
        return remote(xl[l], xn.at[l], y_send.at[l], y_recv.at[l], across)

    def c_copy(l, src):
        return remote(kv.at[l, src], kv.at[l, 1], c_send.at[l], c_recv.at[l], sibling)

    def send_stream(l):
        @pl.when(y == 0)
        def _():
            y_copy(l).start()

    for copy in own_loads(0)[:4]:
        copy.wait()
    nz = geo.nz
    (first_a, first_f), (next_a, next_f) = pieces
    first_a.own()
    for copy in own_loads(0)[4:]:
        copy.wait()
    for k in range(1, count):
        seg_copy(k).start()
    send_stream(0)
    first_f.own()
    for copy in own_loads(1):
        copy.wait()

    waiting = []

    def tick(number):
        for _ in range(min(number, len(waiting))):
            waiting.pop(0)()

    def drain(last):
        while any(task is last for task in waiting):
            tick(1)

    waiting.extend(first_a.steps(1) + first_a.steps(2) + first_f.steps(1) + first_a.steps(3) + [next_a.own])
    waiting.extend(first_f.steps(2) + next_a.steps(1) + first_f.steps(3) + [next_f.own])
    waiting.extend(next_a.steps(2) + next_f.steps(1) + next_a.steps(3) + next_f.steps(2) + next_f.steps(3))
    last_step = {}
    for piece in (first_a, first_f, next_a, next_f):
        own_steps = [task for task in waiting if task.__class__ is functools.partial and task.func.__self__ is piece]
        last_step[piece] = own_steps[-1]

    @pl.when(y == 0)
    def _():
        for l in range(levels):
            xn[l] = jnp.zeros_like(xn[l])

    @pl.when(s == 0)
    def _():
        for l in range(levels):
            kv[l, 1] = jnp.zeros_like(kv[l, 1])

    for k in range(1, count):
        seg_copy(k).wait()
    query_seg = segs[0, 0:1, :]
    query_pos = s * tokens + lax.broadcasted_iota(jnp.int32, (tokens, tokens), 1)
    for b in range(3):
        block = lax.rem(s + count - b, count)
        key_seg = jnp.transpose(jnp.broadcast_to(wide(segs[b, 0:1, :]), (128, tokens)))[:, 0:1]
        key_pos = block * tokens + lax.broadcasted_iota(jnp.int32, (tokens, tokens), 0)
        allowed = (key_seg == wide(query_seg)) & (key_pos <= query_pos)
        bias[b] = jnp.where(allowed, 0.0, masked_value)
    for l in range(levels):
        small[l] = jnp.zeros_like(small[l])

    def weight(l, start):
        return w[l, :, :, :, :, pl.ds(start, width), :].reshape(features, features)

    def out_weight(l, j):
        return w[l, j, :, :, :, pl.ds(row_out, ff_rows), :].reshape(features, features)

    g_a, g_f = buffers_a[0], buffers_f[0]

    def keep(ref, start, value):
        ref[:, :, :, :, pl.ds(start, width), :] = low(value).reshape(nz, geo.nx, geo.ny, 2, width, features)

    def keep_out(j, value):
        g_f[j, :, :, :, pl.ds(parts * width, ff_rows), :] = low(value).reshape(geo.nx, geo.ny, 2, ff_rows, features)

    def row(l, index):
        return par[l, index : index + 1, :]

    pair_lane = lax.broadcasted_iota(jnp.int32, (1, lanes), 1)

    def one_head(value, side):
        return jnp.where((pair_lane < head) == (side == 0), value, jnp.zeros_like(value))

    def ready(piece):
        drain(last_step[piece])
        piece.arrive()

    x, r = stream_grad, out
    residue_load = pltpu.make_async_copy(residue_in, r, residue_sem)
    residue_load.start()

    def forward(l):
        ready(pieces[l][0])
        par[l] = jnp.sum(
            wide(w[l, :, :, :, :, pl.ds(4 * width, ROWS), :]).reshape(geo.shards, ROWS, features), axis=0
        )
        xv = xl[l][...]
        keys = product(xv, weight(l, width))
        values = product(xv, weight(l, 2 * width)) + row(l, ROW_ATT_BIAS + 1)
        kv[l, 0, :, 0:features] = low(keys)
        kv[l, 0, :, features:] = low(values)

        @pl.when(c == 0)
        def _():
            c_copy(l, 0).start()

        tick(2)
        queries = low(product(xv, weight(l, 0)) + row(l, ROW_ATT_BIAS))
        qs[l] = queries * (1.0 / math.sqrt(head))

        @pl.when(y == 1)
        def _():
            y_copy(l).wait_recv()

        xv = xn[l]
        keys = product(xv, weight(l, width))
        values = product(xv, weight(l, 2 * width)) + row(l, ROW_ATT_BIAS + 1)
        kv[l, 2, :, 0:features] = low(keys)
        kv[l, 2, :, features:] = low(values)

        @pl.when((y == 1) & (c == 1))
        def _():
            c_copy(l, 2).start()

        tick(2)

        @pl.when((y == 1) | (c == 1))
        def _():
            c_copy(l, 0).wait_recv()

        for b in range(3):
            kt[:, b * tokens : (b + 1) * tokens] = jnp.transpose(kv[l, b, :, features:])

        for p in range(pairs):
            at = pl.ds(p * lanes, lanes)
            queries = qs[l, :, at]
            keys = kv[l, :, :, at].reshape(3 * tokens, lanes)
            for side in range(2):
                scores = product_rows(keys, one_head(queries, side)) + bias[...].reshape(3 * tokens, tokens)
                terms = jnp.exp(scores - jnp.max(scores, axis=0, keepdims=True))
                probs = low(terms * (1.0 / jnp.sum(terms, axis=0, keepdims=True)))
                pt[l, 2 * p + side] = probs
                rows = pl.ds(p * lanes + side * head, head)
                ob[rows, :] = product(kt[rows, :], probs)
            tick(3)
        att[l] = low(jnp.transpose(ob[...]))
        branch = product(att[l], weight(l, 3 * width)) + row(l, ROW_ATT_BIAS + 2)
        normal, inverse = normalize((wide(stream_in[...]) if l == 0 else x[...]) + branch)
        n1[l] = normal
        i1[l] = inverse
        middle = normal * row(l, ROW_GAIN) + row(l, ROW_SHIFT)
        mid[l] = low(middle)
        x[...] = middle
        if l == 0:
            residue_load.wait()
        r[...] = r[...] + branch
        ready(pieces[l][1])
        total = jnp.broadcast_to(row(l, ROW_OUT_BIAS), (tokens, features))
        for j in range(parts):
            hidden = product(mid[l], weight(l, row_in + j * width)) + row(l, ROW_IN_BIAS + j)
            active, rise = gelu_pair(hidden)
            act[l, j] = low(active)
            slope[l, j] = low(rise)
            total = total + product(act[l, j], out_weight(l, j))
            tick(2)
        r[...] = r[...] + total
        normal, inverse = normalize(x[...] + total)
        n2[l] = normal
        i2[l] = inverse
        next_x = normal * row(l, ROW_GAIN + 1) + row(l, ROW_SHIFT + 1)
        x[...] = next_x
        if l + 1 < levels:
            xl[l + 1][...] = low(next_x)
            send_stream(l + 1)

    def note(l, index, value):
        small[l, index : index + 1, :] = value

    def by_copy(l):
        return remote(sc.at[l], rc.at[l], by_send.at[l], by_recv.at[l], across)

    def bc_copy(l):
        return remote(sb.at[l], rb.at[l], bc_send.at[l], bc_recv.at[l], sibling)

    gx = stream_grad
    block_lanes = features // nz
    last = levels - 1
    sum_ones, stores = {}, []

    def queue_sum(scatter, store, l):
        one, two, three = scatter.steps()
        sum_ones[scatter] = one[-1]
        for n in range(len(one) + 2):
            for stage, lag in ((one, 0), (two, 1), (three, 2)):
                if 0 <= n - lag < len(one):
                    waiting.append(stage[n - lag])
        waiting.extend(stores)
        stores[:] = [functools.partial(store, l)]

    def backward(l):
        sum_a, sum_f = sums[l]
        grad = gx[...]
        note(l, ROW_GAIN + 1, column_sums(grad * n2[l]))
        note(l, ROW_SHIFT + 1, column_sums(grad))
        g2 = normalize_back(grad, n2[l], i2[l], row(l, ROW_GAIN + 1))
        d_ff = low(g2 + residue_grad[...])
        if l < last:
            drain(sum_ones[sums[l + 1][1]])
        note(l, ROW_OUT_BIAS, column_sums(wide(d_ff)))
        total = g2
        for j in range(parts):
            keep_out(j, product_tokens(act[l, j], d_ff))
            d_hidden = low(product_rows(d_ff, out_weight(l, j)) * wide(slope[l, j]))
            sums_in = column_sums(wide(d_hidden))
            for q in range(parts):
                block = sums_in[:, q * block_lanes : (q + 1) * block_lanes]
                small[l, ROW_IN_BIAS + q : ROW_IN_BIAS + q + 1, j * block_lanes : (j + 1) * block_lanes] = block
            keep(g_f, j * width, product_tokens(mid[l], d_hidden))
            total = total + product_rows(d_hidden, weight(l, row_in + j * width))
            tick(2)
        sum_f.begin()
        note(l, ROW_GAIN, column_sums(total * n1[l]))
        note(l, ROW_SHIFT, column_sums(total))
        g1 = normalize_back(total, n1[l], i1[l], row(l, ROW_GAIN))
        gx[...] = g1
        d_att = low(g1 + residue_grad[...])
        note(l, ROW_ATT_BIAS + 2, column_sums(wide(d_att)))
        if l < last:
            drain(sum_ones[sums[l + 1][0]])
        keep(g_a, 3 * width, product_tokens(att[l], d_att))
        att[l] = low(product_rows(d_att, weight(l, 3 * width)))
        queue_sum(sum_f, store_f, l)
        tick(4)
        for b in range(3):
            kt[:, b * tokens : (b + 1) * tokens] = jnp.transpose(kv[l, b, :, 0:features])

        for p in range(pairs):
            at, at_values = pl.ds(p * lanes, lanes), pl.ds(p * lanes + features, lanes)
            queries, d_out = qs[l, :, at], att[l, :, at]
            values = kv[l, :, :, at_values].reshape(3 * tokens, lanes)
            d_keys = jnp.zeros((3 * tokens, lanes), jnp.float32)
            d_values = jnp.zeros((3 * tokens, lanes), jnp.float32)
            for side in range(2):
                own = one_head(d_out, side)
                probs = pt[l, 2 * p + side]
                terms = product_rows(values, own)
                weighted = terms * wide(probs)
                d_scores = low(weighted - wide(probs) * jnp.sum(weighted, axis=0, keepdims=True))
                d_values = d_values + product(probs, own)
                d_keys = d_keys + product(d_scores, one_head(queries, side))
                rows = pl.ds(p * lanes + side * head, head)
                ob[rows, :] = product(kt[rows, :], d_scores)
            for where, value in ((at, d_keys), (at_values, d_values)):
                dkv[0, :, where] = value[:tokens]
                sb[l, :, where] = low(value[tokens : 2 * tokens])
                dkv[1, :, where] = value[2 * tokens :]
            tick(1)

        @pl.when((c == 1) | (y == 1))
        def _():
            bc_copy(l).start()

        @pl.when((y == 1) & (c == 1))
        def _():
            bc_copy(l).wait_recv()
            dkv[1] = dkv[1] + wide(rb[l])

        far_keys, far_values = low(dkv[1, :, 0:features]), low(dkv[1, :, features:])

        @pl.when(y == 1)
        def _():
            sc[l] = low(product_rows(far_keys, weight(l, width)) + product_rows(far_values, weight(l, 2 * width)))
            by_copy(l).start()

        tick(2)
        d_queries = low(jnp.transpose(ob[...]) * (1.0 / math.sqrt(head)))
        keep(g_a, 0, product_tokens(xl[l][...], d_queries))
        note(l, ROW_ATT_BIAS, column_sums(wide(d_queries)))

        @pl.when(c == 0)
        def _():
            bc_copy(l).wait_recv()
            dkv[0] = dkv[0] + wide(rb[l])

        d_keys, d_values = low(dkv[0, :, 0:features]), low(dkv[0, :, features:])
        keep(g_a, width, product_tokens(xl[l][...], d_keys) + product_tokens(xn[l], far_keys))
        keep(g_a, 2 * width, product_tokens(xl[l][...], d_values) + product_tokens(xn[l], far_values))
        note(l, ROW_ATT_BIAS + 1, column_sums(wide(d_values)) + column_sums(wide(far_values)))
        sum_a.begin()
        tick(2)
        gx[...] = (
            gx[...]
            + product_rows(d_queries, weight(l, 0))
            + product_rows(d_keys, weight(l, width))
            + product_rows(d_values, weight(l, 2 * width))
        )
        queue_sum(sum_a, store_a, l)
        tick(2)

        @pl.when(y == 0)
        def _():
            by_copy(l).wait_recv()
            gx[...] = gx[...] + wide(rc[l])

    def store_f(l):
        sum_f = sums[l][1]
        sum_f.finish()
        for n in range(parts):
            ff_in_grad[l, :, n * features : (n + 1) * features] = sum_f.total[n * width : (n + 1) * width]
        ff_out_grad[l] = sum_f.total[parts * width :]

    def store_a(l):
        sum_a = sums[l][0]
        sum_a.finish()
        for n in range(3):
            qkv_grad[l, :, n * features : (n + 1) * features] = sum_a.total[n * width : (n + 1) * width]
        out_grad[l] = sum_a.total[3 * width :]

    for l in range(levels):
        forward(l)
    normal, inverse = normalize(r[...])
    gain = row(last, ROW_FINAL)
    out[...] = x[...] + normal * gain + row(last, ROW_FINAL + 1)
    grad = cot[...]
    note(last, ROW_FINAL, column_sums(grad * normal))
    note(last, ROW_FINAL + 1, column_sums(grad))
    residue_grad[...] = normalize_back(grad, normal, inverse, gain)
    gx[...] = grad
    for l in reversed(range(levels)):
        backward(l)

    z_peers = [geo.device(lax.rem(z + k, nz), xx, y, c) for k in range(1, nz)]
    plane = [
        geo.device(z, lax.rem(xx + i, geo.nx), lax.rem(y + j, geo.ny), lax.rem(c + k, 2))
        for i in range(geo.nx)
        for j in range(geo.ny)
        for k in range(2)
    ][1:]

    def z_small(k):
        return remote(
            sbuf.at[lax.rem(z + k, nz)], sin.at[k - 1], s_send.at[k - 1], s_recv.at[k - 1], z_peers[k - 1]
        )

    def plane_small(n):
        m = nz - 1 + n
        return remote(sbuf.at[nz], sin.at[m], s_send.at[m], s_recv.at[m], plane[n])

    for k in range(nz):
        sbuf[k] = small[:, :, k * block_lanes : (k + 1) * block_lanes].reshape(levels * ROWS, block_lanes)
    for k in range(1, nz):
        z_small(k).start()
    waiting.extend(stores)
    while len(waiting) > 2 * nz + 1:
        tick(1)
    total = sbuf[z]
    for k in range(1, nz):
        z_small(k).wait()
        total = total + sin[k - 1]
    sbuf[nz] = total
    for n in range(len(plane)):
        plane_small(n).start()
    tick(nz)
    total = sbuf[nz]
    for n in range(len(plane)):
        plane_small(n).wait()
        total = total + sin[nz - 1 + n]
    exact = functools.partial(jnp.dot, preferred_element_type=jnp.float32, precision=lax.Precision.HIGHEST)

    def chosen(lane_count, first, size):
        lane = lax.broadcasted_iota(jnp.int32, (lane_count, size), 0)
        return jnp.where(lane == first + lax.broadcasted_iota(jnp.int32, (lane_count, size), 1), 1.0, 0.0)

    mine = exact(total, chosen(block_lanes, lax.rem(shard, geo.shards // nz) * width, width))
    in_block = exact(total, chosen(block_lanes, lax.rem(ff_lane, block_lanes), ff_rows))
    part = lax.broadcasted_iota(jnp.int32, (ROWS, 1), 0)
    for l in range(levels):
        own = mine[l * ROWS : (l + 1) * ROWS]
        att_grad[l] = own[ROW_ATT_BIAS:ROW_IN_BIAS]
        in_rows = in_block[l * ROWS : (l + 1) * ROWS]
        in_bias_grad[l : l + 1, :] = column_sums(
            jnp.where(part == ROW_IN_BIAS + lax.div(ff_lane, block_lanes), in_rows, 0.0)
        )
        out_bias_grad[l : l + 1, :] = own[ROW_OUT_BIAS : ROW_OUT_BIAS + 1]
        gain_grad[l] = own[ROW_GAIN : ROW_GAIN + 2]
        shift_grad[l] = own[ROW_SHIFT : ROW_SHIFT + 2]
    final_gain_grad[...] = own[ROW_FINAL : ROW_FINAL + 1]
    final_shift_grad[...] = own[ROW_FINAL + 1 : ROW_FINAL + 2]
    while waiting:
        tick(1)

    for l in range(levels):
        for piece in pieces[l]:
            piece.finish()

        @pl.when(y == 0)
        def _(l=l):
            y_copy(l).wait_send()

        @pl.when((y == 1) | (c == 0))
        def _(l=l):
            c_copy(l, 0).wait_send()

        @pl.when((c == 1) | (y == 1))
        def _(l=l):
            bc_copy(l).wait_send()

        @pl.when(y == 1)
        def _(l=l):
            by_copy(l).wait_send()


def run_step(geo, stream_in, residue_in, seg, cot, shards):
    tokens, features = residue_in.shape
    levels, width, qkv_columns = shards[0].shape
    parts = shards[2].shape[2] // features
    ff_rows = shards[3].shape[1]
    rows_a, rows_f = 4 * width, parts * width + ff_rows
    shape = (geo.nz, geo.nx, geo.ny, 2)
    dma, vmem = pltpu.SemaphoreType.DMA, pltpu.VMEM
    wide_kind, kind = jnp.float32, jnp.bfloat16
    whole = pl.BlockSpec(memory_space=pltpu.VMEM)
    away = pl.BlockSpec(memory_space=pl.ANY)
    row = (tokens, features)
    half_a, half_f = 2 * width, 3 * width
    routes_a = ((2 * width, "zxy"), (3 * width, "zyx"))
    routes_f = ((3 * width, "zxy"), (5 * width, "zyx"))
    others = geo.nz - 1 + 2 * geo.nx * geo.ny - 1
    outs = [row, row, row] + [member.shape for member in shards]
    scratch = [
        vmem((levels,) + shape + (rows_a + ROWS + rows_f, features), kind),
        vmem((levels, ROWS, features), wide_kind),
        vmem((levels, ROWS, features), wide_kind),
        vmem((levels - 1,) + row, kind),
        vmem((levels,) + row, kind),
        vmem((levels,) + row, kind),
        vmem((levels, 3, tokens, 2 * features), kind),
        vmem((features, 3 * tokens), kind),
        vmem((levels, HEADS, 3 * tokens, tokens), kind),
        vmem((levels,) + row, kind),
        vmem((levels,) + row, kind),
        vmem((levels, parts) + row, kind),
        vmem((levels, parts) + row, kind),
        vmem((levels,) + row, wide_kind),
        vmem((levels,) + row, wide_kind),
        vmem((levels, tokens, 1), wide_kind),
        vmem((levels, tokens, 1), wide_kind),
        vmem((3, tokens, tokens), wide_kind),
        vmem((geo.seq, 8, tokens), jnp.int32),
        vmem((2, tokens, 2 * features), wide_kind),
        vmem((features, tokens), wide_kind),
        vmem((levels, tokens, 2 * features), kind),
        vmem((levels,) + row, kind),
        vmem((levels, tokens, 2 * features), kind),
        vmem((levels,) + row, kind),
        vmem((levels, ROWS, features), wide_kind),
        vmem((geo.nz + 1, levels * ROWS, features // geo.nz), wide_kind),
        vmem((others, levels * ROWS, features // geo.nz), wide_kind),
    ]
    scratch += Scatter.buffers(geo, levels, rows_a, half_a, features, kind)
    scratch += Scatter.buffers(geo, levels, rows_f, half_f, features, kind)
    scratch += Gather.semaphores(geo, 2 * levels, len(routes_f)) + Scatter.semaphores(geo, 2 * levels)
    scratch += [dma((levels, 5 + parts))] + [dma((geo.seq,))] * 2 + [dma((levels,))] * 8 + [dma((others,))] * 2 + [dma(())]
    return pl.pallas_call(
        functools.partial(step_kernel, geo, routes_a, routes_f, half_a, half_f),
        out_shape=tuple(jax.ShapeDtypeStruct(shape_of, wide_kind) for shape_of in outs),
        in_specs=[whole, away, whole, whole] + [away] * 4 + [whole] * 7,
        out_specs=(whole,) * len(outs),
        scratch_shapes=scratch,
        compiler_params=pltpu.CompilerParams(
            collective_id=0, has_side_effects=True, vmem_limit_bytes=64 << 20
        ),
        name="run_step",
    )(stream_in, residue_in, seg, cot, *shards)


def settle_kernel(*refs):
    count = len(refs) // 2
    for src, dst in zip(refs[:count], refs[count:]):
        dst[...] = src[...]


def settle(values):
    whole = pl.BlockSpec(memory_space=pltpu.VMEM)
    return pl.pallas_call(
        settle_kernel,
        out_shape=tuple(jax.ShapeDtypeStruct(value.shape, value.dtype) for value in values),
        in_specs=[whole] * len(values),
        out_specs=(whole,) * len(values),
        name="settle",
    )(*values)


def gather_plain(shards, number):
    gathered = [
        lax.all_gather(shards[member][number], ("dp", "seq"), axis=axis, tiled=True)
        for member, axis in enumerate((0, 0, 0, 0, 1, 0, 0, 1, 1))
    ]
    return tuple(gathered) + tuple(
        lax.all_gather(shards[member], ("dp", "seq"), axis=0, tiled=True) for member in (9, 10)
    )


def body_plain(geo, *args):
    stream_in, residue_in, segments, out_cot = args[:4]
    shards = args[4:]
    levels, width, _ = shards[1].shape
    ff_width = shards[3].shape[1]
    stream = stream_in[0].astype(jnp.float32)
    residue = residue_in[0]
    cotangent = out_cot[0]
    tokens = stream.shape[0]
    query_seg = segments[0]
    whole_seg = lax.all_gather(query_seg, "seq", axis=0, tiled=True)
    seq_index = lax.axis_index("seq")
    query_pos = seq_index * tokens + jnp.arange(tokens, dtype=jnp.int32)
    weights = [gather_plain(shards, number) for number in range(levels)]
    states = []
    for number in range(levels):
        stream, residue, state = layer_forward(stream, residue, weights[number], query_pos, query_seg, whole_seg)
        states.append(state)
    final_norm, pull_final = jax.vjp(
        layer_norm,
        residue,
        weights[-1][9].astype(jnp.float32),
        weights[-1][10].astype(jnp.float32),
    )
    output = stream + final_norm
    grad_residue, final_gain_grad, final_shift_grad = pull_final(cotangent)
    grad_stream = cotangent
    grads = [None] * levels
    for number in reversed(range(levels)):
        grad_stream, grads[number] = layer_backward(
            states[number], weights[number], grad_stream, grad_residue, query_pos, query_seg
        )
    summed = [
        jnp.stack(
            [
                lax.psum_scatter(grads[number][member], ("dp", "seq"), scatter_dimension=axis, tiled=True)
                for number in range(levels)
            ]
        )
        for member, axis in enumerate((0, 0, 0, 0, 1, 0, 0, 1, 1))
    ] + [
        lax.psum_scatter(final_gain_grad, ("dp", "seq"), scatter_dimension=0, tiled=True),
        lax.psum_scatter(final_shift_grad, ("dp", "seq"), scatter_dimension=0, tiled=True),
    ]
    return (output[None], grad_stream[None], grad_residue[None]) + tuple(summed)


def body(geo, *args):
    stream_in, residue_in, segments, out_cot = args[:4]
    shards = list(args[4:])
    shards[-2:] = [shards[-2][None], shards[-1][None]]
    tokens = stream_in.shape[1]
    seg = jnp.broadcast_to(segments, (8, tokens))
    results = settle(run_step(geo, stream_in[0], residue_in[0], seg, out_cot[0], shards))
    return tuple(value[None] for value in results[:3]) + tuple(results[3:-2]) + (results[-2][0], results[-1][0])


def solution(mesh):
    geo = Geometry(mesh)
    chosen = body if geo.seq == 4 and geo.nz == 4 else body_plain
    return jax.shard_map(
        functools.partial(chosen, geo),
        mesh=mesh,
        in_specs=(
            P("dp", "seq", None),
            P("dp", "seq", None),
            P("dp", "seq"),
            P("dp", "seq", None),
            P(None, ("dp", "seq"), None),
            P(None, ("dp", "seq"), None),
            P(None, ("dp", "seq"), None),
            P(None, ("dp", "seq"), None),
            P(None, None, ("dp", "seq")),
            P(None, ("dp", "seq")),
            P(None, ("dp", "seq")),
            P(None, None, ("dp", "seq")),
            P(None, None, ("dp", "seq")),
            P(("dp", "seq")),
            P(("dp", "seq")),
        ),
        out_specs=(
            P("dp", "seq", None),
            P("dp", "seq", None),
            P("dp", "seq", None),
            P(None, ("dp", "seq"), None),
            P(None, ("dp", "seq"), None),
            P(None, ("dp", "seq"), None),
            P(None, ("dp", "seq"), None),
            P(None, None, ("dp", "seq")),
            P(None, ("dp", "seq")),
            P(None, ("dp", "seq")),
            P(None, None, ("dp", "seq")),
            P(None, None, ("dp", "seq")),
            P(("dp", "seq")),
            P(("dp", "seq")),
        ),
        check_vma=False,
    )
```

```python
import functools
import itertools
import math

import jax
import jax.numpy as jnp
from jax import lax
from jax.experimental import pallas as pl
from jax.experimental.pallas import tpu as pltpu
from jax.sharding import PartitionSpec as P

HEADS = 8
MESH = pl.DeviceIdType.MESH


class Geometry:
    def __init__(self, mesh):
        self.dp, self.seq = mesh.shape["dp"], mesh.shape["seq"]
        self.ny = self.seq // 2
        self.nx = self.ny
        self.nz = self.dp // self.nx
        self.shards = self.dp * self.seq

    def here(self):
        dp, seq = lax.axis_index("dp"), lax.axis_index("seq")
        return lax.div(dp, self.nx), lax.rem(dp, self.nx), lax.div(seq, 2), lax.rem(seq, 2)

    def device(self, z, x, y, c):
        return (z * self.nx + x, y * 2 + c)

    def peers(self):
        z, x, y, c = self.here()
        found = [self.device(lax.rem(z + k, self.nz), x, y, c) for k in range(1, self.nz)]
        found += [self.device(z, lax.rem(x + k, self.nx), y, c) for k in range(1, self.nx)]
        found += [self.device(z, x, lax.rem(y + k, self.ny), c) for k in range(1, self.ny)]
        return found + [self.device(z, x, y, 1 - c)]


def greet(devices):
    barrier = pltpu.get_barrier_semaphore()
    for device in devices:
        pl.semaphore_signal(barrier, inc=1, device_id=device, device_id_type=MESH)
    pl.semaphore_wait(barrier, len(devices))


def remote(src, dst, send_sem, recv_sem, device):
    return pltpu.make_async_remote_copy(
        src_ref=src,
        dst_ref=dst,
        send_sem=send_sem,
        recv_sem=recv_sem,
        device_id=device,
        device_id_type=MESH,
    )


epsilon = 1e-05
masked_value = -1e30


def smooth_gate(values):
    return jax.nn.gelu(values, approximate=True)


def layer_norm(values, norm_gain, norm_shift):
    average = jnp.mean(values, axis=-1, keepdims=True)
    centred = values - average
    variance = jnp.mean(centred * centred, axis=-1, keepdims=True)
    return centred * lax.rsqrt(variance + epsilon) * norm_gain + norm_shift


def keep_state(carried):
    return carried


def allowed_pairs(query_pos, query_seg, key_pos, key_seg):
    return (query_seg[:, None] == key_seg[None, :]) & (key_pos[None, :] <= query_pos[:, None])


def block_needed(query_pos, query_seg, key_pos, key_seg):
    return (key_pos[0] <= query_pos[-1]) & (key_seg[-1] >= query_seg[0])


def key_blocks(keys_values, key_seg):
    length = keys_values.shape[0]
    features = keys_values.shape[1] // 2
    head_size = features // HEADS
    block_rows = math.gcd(length, 512)
    block_count = length // block_rows
    split_kv = keys_values.reshape(block_count, block_rows, 2, HEADS, head_size)
    key_pos = jnp.arange(length, dtype=jnp.int32).reshape(block_count, block_rows)
    return (split_kv[:, :, 0], split_kv[:, :, 1], key_pos, key_seg.reshape(block_count, block_rows))


def block_scores(queries3, key_block, query_pos, query_seg, key_pos, key_seg):
    scaling = 1.0 / math.sqrt(queries3.shape[-1])
    raw_scores = (
        jnp.einsum("qhd,khd->hqk", queries3, key_block, preferred_element_type=jnp.float32)
        * scaling
    )
    return (raw_scores, allowed_pairs(query_pos, query_seg, key_pos, key_seg)[None])


def attention_forward(queries3, blocks, query_pos, query_seg):
    tokens, head_count, head_size = queries3.shape

    def statistics(carried, block_items):
        key_block, value_block, key_pos, key_seg = block_items

        def statistics_compute(running):
            run_max, run_sum = running
            raw_scores, allowed = block_scores(
                queries3, key_block, query_pos, query_seg, key_pos, key_seg
            )
            new_max = jnp.maximum(
                run_max, jnp.max(jnp.where(allowed, raw_scores, masked_value), axis=-1)
            )
            exp_terms = jnp.exp(jnp.where(allowed, raw_scores - new_max[..., None], masked_value))
            return (new_max, run_sum * jnp.exp(run_max - new_max) + jnp.sum(exp_terms, axis=-1))

        needed = block_needed(query_pos, query_seg, key_pos, key_seg)
        return (lax.cond(needed, statistics_compute, keep_state, carried), None)

    initial = (
        jnp.full((head_count, tokens), masked_value, jnp.float32),
        jnp.zeros((head_count, tokens), jnp.float32),
    )
    (run_max, run_sum), unused = lax.scan(statistics, initial, blocks)
    log_total = run_max + jnp.log(run_sum)

    def accumulate(carried, block_items):
        key_block, value_block, key_pos, key_seg = block_items

        def accumulate_compute(running):
            raw_scores, allowed = block_scores(
                queries3, key_block, query_pos, query_seg, key_pos, key_seg
            )
            weights = jnp.exp(jnp.where(allowed, raw_scores - log_total[..., None], masked_value))
            weights = weights.astype(jnp.bfloat16)
            return running + jnp.einsum(
                "hqk,khd->qhd", weights, value_block, preferred_element_type=jnp.float32
            )

        needed = block_needed(query_pos, query_seg, key_pos, key_seg)
        return (lax.cond(needed, accumulate_compute, keep_state, carried), None)

    mixed_heads, unused = lax.scan(
        accumulate, jnp.zeros((tokens, head_count, head_size), jnp.float32), blocks
    )
    return (mixed_heads, log_total)


def attention_backward(queries3, blocks, query_pos, query_seg, log_total, mixed_heads, grad_heads):
    tokens, head_count, head_size = queries3.shape
    scaling = 1.0 / math.sqrt(head_size)
    row_dots = jnp.sum(mixed_heads * grad_heads.astype(jnp.float32), axis=-1).T
    block_rows = blocks[0].shape[1]
    block_count = blocks[0].shape[0]

    def backward_step(grad_queries, block_items):
        key_block, value_block, key_pos, key_seg = block_items

        def backward_compute(running):
            raw_scores, allowed = block_scores(
                queries3, key_block, query_pos, query_seg, key_pos, key_seg
            )
            prob_values = jnp.exp(
                jnp.where(allowed, raw_scores - log_total[..., None], masked_value)
            )
            grad_values = jnp.einsum(
                "hqk,qhd->khd",
                prob_values.astype(jnp.bfloat16),
                grad_heads,
                preferred_element_type=jnp.float32,
            )
            grad_probs = jnp.einsum(
                "qhd,khd->hqk", grad_heads, value_block, preferred_element_type=jnp.float32
            )
            grad_scores = (prob_values * (grad_probs - row_dots[..., None])).astype(jnp.bfloat16)
            running = (
                running
                + jnp.einsum(
                    "hqk,khd->qhd", grad_scores, key_block, preferred_element_type=jnp.float32
                )
                * scaling
            )
            grad_keys = (
                jnp.einsum(
                    "hqk,qhd->khd", grad_scores, queries3, preferred_element_type=jnp.float32
                )
                * scaling
            )
            return (running, grad_keys, grad_values)

        def skip_block(running):
            empty_rows = jnp.zeros((block_rows, head_count, head_size), jnp.float32)
            return (running, empty_rows, empty_rows)

        needed = block_needed(query_pos, query_seg, key_pos, key_seg)
        grad_queries, grad_keys, grad_values = lax.cond(
            needed, backward_compute, skip_block, grad_queries
        )
        return (grad_queries, (grad_keys, grad_values))

    initial = jnp.zeros((tokens, head_count, head_size), jnp.float32)
    grad_queries, (grad_keys, grad_values) = lax.scan(backward_step, initial, blocks)
    length = block_count * block_rows
    return (
        grad_queries.reshape(tokens, head_count * head_size),
        grad_keys.reshape(length, head_count * head_size),
        grad_values.reshape(length, head_count * head_size),
    )


def layer_forward(stream, residue, weights, query_pos, query_seg, key_seg):
    (
        qkv_weight,
        out_weight,
        ff_in_weight,
        ff_out_weight,
        att_bias,
        ff_in_bias,
        ff_out_bias,
        norm_gain,
        norm_shift,
    ) = weights[:9]
    tokens, features = stream.shape
    stream_low = stream.astype(jnp.bfloat16)
    bias_row = jnp.concatenate([att_bias[0], jnp.zeros_like(att_bias[0]), att_bias[1]]).astype(
        jnp.float32
    )
    joined = (
        jnp.dot(stream_low, qkv_weight, preferred_element_type=jnp.float32) + bias_row
    ).astype(jnp.bfloat16)
    queries3 = joined[:, :features].reshape(tokens, HEADS, features // HEADS)
    keys_values = lax.all_gather(joined[:, features:], "seq", axis=0, tiled=True)
    blocks = key_blocks(keys_values, key_seg)
    mixed_heads, log_total = attention_forward(queries3, blocks, query_pos, query_seg)
    attended = mixed_heads.reshape(tokens, features).astype(jnp.bfloat16)
    branch_att = jnp.dot(attended, out_weight, preferred_element_type=jnp.float32) + att_bias[
        2
    ].astype(jnp.float32)
    middle, pull_first = jax.vjp(
        layer_norm,
        stream + branch_att,
        norm_gain[0].astype(jnp.float32),
        norm_shift[0].astype(jnp.float32),
    )
    residue_mid = residue + branch_att
    middle_low = middle.astype(jnp.bfloat16)
    hidden = jnp.dot(
        middle_low, ff_in_weight, preferred_element_type=jnp.float32
    ) + ff_in_bias.astype(jnp.float32)
    active = smooth_gate(hidden).astype(jnp.bfloat16)
    branch_ff = jnp.dot(
        active, ff_out_weight, preferred_element_type=jnp.float32
    ) + ff_out_bias.astype(jnp.float32)
    stream_next, pull_second = jax.vjp(
        layer_norm,
        middle + branch_ff,
        norm_gain[1].astype(jnp.float32),
        norm_shift[1].astype(jnp.float32),
    )
    saved_state = (
        stream_low,
        queries3,
        blocks,
        mixed_heads,
        log_total,
        attended,
        pull_first,
        middle_low,
        hidden,
        active,
        pull_second,
    )
    return (stream_next, residue_mid + branch_ff, saved_state)


def layer_backward(saved_state, weights, grad_stream, grad_residue, query_pos, query_seg):
    (
        stream_low,
        queries3,
        blocks,
        mixed_heads,
        log_total,
        attended,
        pull_first,
        middle_low,
        hidden,
        active,
        pull_second,
    ) = saved_state
    qkv_weight, out_weight, ff_in_weight, ff_out_weight = weights[:4]
    grad_second, gain_second, shift_second = pull_second(grad_stream)
    grad_ff = (grad_second + grad_residue).astype(jnp.bfloat16)
    grad_ff_out = jnp.einsum("tf,td->fd", active, grad_ff, preferred_element_type=jnp.float32)
    bias_ff_out = jnp.sum(grad_ff.astype(jnp.float32), axis=0)
    grad_active = jnp.einsum(
        "td,fd->tf", grad_ff, ff_out_weight, preferred_element_type=jnp.float32
    )
    unused_gate, pull_gate = jax.vjp(smooth_gate, hidden)
    grad_hidden = pull_gate(grad_active)[0].astype(jnp.bfloat16)
    grad_ff_in = jnp.einsum(
        "td,tf->df", middle_low, grad_hidden, preferred_element_type=jnp.float32
    )
    bias_ff_in = jnp.sum(grad_hidden.astype(jnp.float32), axis=0)
    grad_middle = grad_second + jnp.einsum(
        "tf,df->td", grad_hidden, ff_in_weight, preferred_element_type=jnp.float32
    )
    grad_first, gain_first, shift_first = pull_first(grad_middle)
    grad_att = (grad_first + grad_residue).astype(jnp.bfloat16)
    grad_out = jnp.einsum("te,td->ed", attended, grad_att, preferred_element_type=jnp.float32)
    bias_att_out = jnp.sum(grad_att.astype(jnp.float32), axis=0)
    grad_attended = jnp.einsum(
        "td,ed->te", grad_att, out_weight, preferred_element_type=jnp.float32
    )
    grad_attended = grad_attended.astype(jnp.bfloat16)
    tokens, features = grad_attended.shape
    grad_queries, grad_keys, grad_values = attention_backward(
        queries3,
        blocks,
        query_pos,
        query_seg,
        log_total,
        mixed_heads,
        grad_attended.reshape(tokens, HEADS, features // HEADS),
    )
    key_grads, value_grads = (
        lax.psum_scatter(
            grad_keys.astype(jnp.bfloat16), "seq", scatter_dimension=0, tiled=True
        ).astype(jnp.float32),
        lax.psum_scatter(
            grad_values.astype(jnp.bfloat16), "seq", scatter_dimension=0, tiled=True
        ).astype(jnp.float32),
    )
    grad_joined = jnp.concatenate([grad_queries, key_grads, value_grads], axis=1).astype(
        jnp.bfloat16
    )
    grad_qkv = jnp.einsum("td,te->de", stream_low, grad_joined, preferred_element_type=jnp.float32)
    column_sums = jnp.sum(grad_joined.astype(jnp.float32), axis=0)
    bias_att = jnp.stack([column_sums[:features], column_sums[2 * features :], bias_att_out])
    grad_stream_in = grad_first + jnp.einsum(
        "te,de->td", grad_joined, qkv_weight, preferred_element_type=jnp.float32
    )
    layer_grads = (
        grad_qkv,
        grad_out,
        grad_ff_in,
        grad_ff_out,
        bias_att,
        bias_ff_in,
        bias_ff_out,
        jnp.stack([gain_first, gain_second]),
        jnp.stack([shift_first, shift_second]),
    )
    return (grad_stream_in, layer_grads)


def product(left, right):
    return lax.dot_general(left, right, (((1,), (0,)), ((), ())), preferred_element_type=jnp.float32)


def product_rows(left, right):
    return lax.dot_general(left, right, (((1,), (1,)), ((), ())), preferred_element_type=jnp.float32)


def product_tokens(left, right):
    return lax.dot_general(left, right, (((0,), (0,)), ((), ())), preferred_element_type=jnp.float32)


def wide(value):
    return value.astype(jnp.float32)


def low(value):
    return value.astype(jnp.bfloat16)


def normalize(values):
    centred = values - jnp.mean(values, axis=-1, keepdims=True)
    inverse = lax.rsqrt(jnp.mean(centred * centred, axis=-1, keepdims=True) + epsilon)
    return centred * inverse, inverse


def normalize_back(grad, normal, inverse, gain):
    scaled = grad * gain
    return (
        scaled
        - jnp.mean(scaled, axis=-1, keepdims=True)
        - normal * jnp.mean(scaled * normal, axis=-1, keepdims=True)
    ) * inverse


def column_sums(values):
    return jnp.sum(values, axis=0, keepdims=True)


def gelu_pair(v):
    rate = math.sqrt(2.0 / math.pi)
    square = v * v
    bent = jnp.tanh(v * (rate + (rate * 0.044715) * square))
    rise = 0.5 + 0.5 * bent
    slope = rise + v * (0.5 - 0.5 * bent * bent) * (rate + (3.0 * rate * 0.044715) * square)
    return v * rise, slope


class Gather:
    def __init__(self, geo, w, l, start, size, cut, sems, number):
        self.geo, self.w, self.l, self.start, self.size, self.cut = geo, w, l, start, size, cut
        (self.z_send, self.z_recv, self.x_send, self.x_recv, self.y_send, self.y_recv, self.xd_send, self.xd_recv,
         self.yd_send, self.yd_recv, self.c_send, self.c_recv) = (sem.at[number] for sem in sems)
        self.here = geo.here()
        z, last = self.here[0], geo.nz - 1
        self.back = [0]
        for n in range(last):
            below, above = n + 1, last - n
            half = n // 2
            between = 1 + half if n % 2 == 0 else last - half
            self.back.append(jnp.where(z == 0, above, jnp.where(z == last, below, between)))

    def at(self, n, i, j, low=None):
        geo, (z, x, y, c) = self.geo, self.here
        rows = (self.start, self.size)
        if low is not None:
            rows = (self.start + self.cut, self.size - self.cut) if low else (self.start, self.cut)
        return self.w.at[
            self.l,
            lax.rem(z + geo.nz - self.back[n], geo.nz),
            lax.rem(x + geo.nx - i, geo.nx),
            lax.rem(y + geo.ny - j, geo.ny),
            c,
            pl.ds(*rows),
        ]

    def z_copies(self, n):
        geo, (z, x, y, c) = self.geo, self.here
        back, piece = self.back[n], self.at(n, 0, 0)
        up = remote(
            piece, piece, self.z_send.at[0, n], self.z_recv.at[lax.rem(back + 1, geo.nz)],
            geo.device(lax.rem(z + 1, geo.nz), x, y, c),
        )
        down = remote(
            piece, piece, self.z_send.at[1, n], self.z_recv.at[lax.rem(back + geo.nz - 1, geo.nz)],
            geo.device(lax.rem(z + geo.nz - 1, geo.nz), x, y, c),
        )
        own = n == 0
        return [
            ((back <= z) & (z < geo.nz - 1), up),
            (((back > z) | own) & (z > 0), down),
        ]

    def z_arrival(self, n):
        piece, (z, x, y, c) = self.at(n, 0, 0), self.here
        return remote(
            piece, piece, self.z_send.at[0, n], self.z_recv.at[self.back[n]],
            self.geo.device(lax.rem(z + 1, self.geo.nz), x, y, c),
        )

    def x_copy(self, n, i):
        z, x, y, c = self.here
        piece = self.at(n, 0, 0)
        return remote(piece, piece, self.x_send.at[n, i - 1], self.x_recv.at[n, i - 1],
                      self.geo.device(z, lax.rem(x + i, self.geo.nx), y, c))

    def y_copy(self, n, j):
        z, x, y, c = self.here
        piece = self.at(n, 0, 0)
        return remote(piece, piece, self.y_send.at[n, j - 1], self.y_recv.at[n, j - 1],
                      self.geo.device(z, x, lax.rem(y + j, self.geo.ny), c))

    def x_forward(self, n, i, j):
        z, x, y, c = self.here
        piece, index = self.at(n, 0, j, True), (n, i - 1, j - 1)
        return remote(piece, piece, self.xd_send.at[index], self.xd_recv.at[index],
                      self.geo.device(z, lax.rem(x + i, self.geo.nx), y, c))

    def y_forward(self, n, i, j):
        z, x, y, c = self.here
        piece, index = self.at(n, i, 0, False), (n, i - 1, j - 1)
        return remote(piece, piece, self.yd_send.at[index], self.yd_recv.at[index],
                      self.geo.device(z, x, lax.rem(y + j, self.geo.ny), c))

    def c_copy(self, n):
        geo, (z, x, y, c) = self.geo, self.here
        piece = self.w.at[self.l, lax.rem(z + geo.nz - self.back[n], geo.nz), :, :, c, pl.ds(self.start, self.size)]
        return remote(piece, piece, self.c_send.at[n], self.c_recv.at[n], geo.device(z, x, y, 1 - c))

    def fan(self, n):
        for needed, copy in self.z_copies(n):
            pl.when(needed)(copy.start)
        for i in range(1, self.geo.nx):
            self.x_copy(n, i).start()
        for j in range(1, self.geo.ny):
            self.y_copy(n, j).start()

    def own(self):
        self.fan(0)

    def from_z(self, n):
        self.z_arrival(n).wait_recv()
        self.fan(n)

    def from_line(self, n):
        nx, ny = self.geo.nx, self.geo.ny
        for j in range(1, ny):
            self.y_copy(n, j).wait_recv()
            for i in range(1, nx):
                self.x_forward(n, i, j).start()
        for i in range(1, nx):
            self.x_copy(n, i).wait_recv()
            for j in range(1, ny):
                self.y_forward(n, i, j).start()

    def from_corner(self, n):
        for i in range(1, self.geo.nx):
            for j in range(1, self.geo.ny):
                self.x_forward(n, i, j).wait_recv()
                self.y_forward(n, i, j).wait_recv()
        self.c_copy(n).start()

    def steps(self):
        every = range(self.geo.nz)
        return [
            [functools.partial(self.from_z, n) for n in every if n],
            [functools.partial(self.from_line, n) for n in every],
            [functools.partial(self.from_corner, n) for n in every],
        ]

    def arrive(self):
        for n in range(self.geo.nz):
            self.c_copy(n).wait_recv()

    def finish(self):
        nx, ny = self.geo.nx, self.geo.ny
        for n in range(self.geo.nz):
            self.c_copy(n).wait_send()
            for needed, copy in self.z_copies(n):
                pl.when(needed)(copy.wait_send)
            for i in range(1, nx):
                self.x_copy(n, i).wait_send()
            for j in range(1, ny):
                self.y_copy(n, j).wait_send()
            for i in range(1, nx):
                for j in range(1, ny):
                    self.x_forward(n, i, j).wait_send()
                    self.y_forward(n, i, j).wait_send()

    @staticmethod
    def semaphores(geo, count):
        dma = pltpu.SemaphoreType.DMA
        nz, nx, ny = geo.nz, geo.nx, geo.ny
        return (
            [dma((count, 2, nz)), dma((count, nz))]
            + [dma((count, nz, nx - 1))] * 2
            + [dma((count, nz, ny - 1))] * 2
            + [dma((count, nz, nx - 1, ny - 1))] * 4
            + [dma((count, nz))] * 2
        )


class Scatter:
    def __init__(self, geo, g, own, r1h, r1l, r2h, r2l, zin, total, l, cut, sems, number):
        self.geo, self.g, self.own, self.l, self.cut = geo, g, own.at[l], l, cut
        self.r1h, self.r1l, self.r2h, self.r2l, self.zin = (ref.at[l] for ref in (r1h, r1l, r2h, r2l, zin))
        self.total = total
        self.rows = g.shape[4]
        self.sems = [sem.at[number] for sem in sems]
        self.z, self.x, self.y, self.c = geo.here()
        self.order = list(range(1, geo.nz)) + [0]

    def copy(self, src, dst, number, index, device):
        return remote(src, dst, self.sems[number].at[index], self.sems[number + 1].at[index], device)

    def cross(self, k):
        return self.copy(
            self.g.at[lax.rem(self.z + k, self.geo.nz), :, :, 1 - self.c], self.own.at[k], 0, (k,),
            self.geo.device(self.z, self.x, self.y, 1 - self.c),
        )

    def to_x(self, src, dst, number, index, i):
        return self.copy(src, dst, number, index, self.geo.device(self.z, lax.rem(self.x + i, self.geo.nx), self.y, self.c))

    def to_y(self, src, dst, number, index, j):
        return self.copy(src, dst, number, index, self.geo.device(self.z, self.x, lax.rem(self.y + j, self.geo.ny), self.c))

    def one(self, k):
        nx, ny = self.geo.nx, self.geo.ny
        top, rest = pl.ds(0, self.cut), pl.ds(self.cut, self.rows - self.cut)
        return [
            self.to_y(self.own.at[k, :, lax.rem(self.y + j, ny), top], self.r1h.at[k, j - 1], 2, (k, j - 1), j)
            for j in range(1, ny)
        ] + [
            self.to_x(self.own.at[k, lax.rem(self.x + i, nx), :, rest], self.r1l.at[k, i - 1], 4, (k, i - 1), i)
            for i in range(1, nx)
        ]

    def two(self, k):
        nx, ny = self.geo.nx, self.geo.ny
        top, rest = pl.ds(0, self.cut), pl.ds(self.cut, self.rows - self.cut)
        return [
            self.to_x(self.own.at[k, lax.rem(self.x + i, nx), self.y, top], self.r2h.at[k, i - 1], 6, (k, i - 1), i)
            for i in range(1, nx)
        ] + [
            self.to_y(self.own.at[k, self.x, lax.rem(self.y + j, ny), rest], self.r2l.at[k, j - 1], 8, (k, j - 1), j)
            for j in range(1, ny)
        ]

    def three(self, k):
        return self.copy(
            self.own.at[k, self.x, self.y], self.zin.at[k - 1], 10, (k - 1,),
            self.geo.device(lax.rem(self.z + k, self.geo.nz), self.x, self.y, self.c),
        )

    def begin(self):
        for k in self.order:
            self.cross(k).start()

    def step_one(self, k):
        own = self.own
        self.cross(k).wait()
        for i in range(self.geo.nx):
            for j in range(self.geo.ny):
                mine = self.g[lax.rem(self.z + k, self.geo.nz), i, j, self.c]
                own[k, i, j] = low(wide(mine) + wide(own[k, i, j]))
        for copy in self.one(k):
            copy.start()

    def step_two(self, k):
        own, x, y = self.own, self.x, self.y
        top, rest = pl.ds(0, self.cut), pl.ds(self.cut, self.rows - self.cut)
        for copy in self.one(k):
            copy.wait()
        for i in range(self.geo.nx):
            total = wide(own[k, i, y, top])
            for j in range(1, self.geo.ny):
                total = total + wide(self.r1h[k, j - 1, i])
            own[k, i, y, top] = low(total)
        for j in range(self.geo.ny):
            total = wide(own[k, x, j, rest])
            for i in range(1, self.geo.nx):
                total = total + wide(self.r1l[k, i - 1, j])
            own[k, x, j, rest] = low(total)
        for copy in self.two(k):
            copy.start()

    def step_three(self, k):
        own, x, y = self.own, self.x, self.y
        top, rest = pl.ds(0, self.cut), pl.ds(self.cut, self.rows - self.cut)
        for copy in self.two(k):
            copy.wait()
        upper = wide(own[k, x, y, top])
        for i in range(1, self.geo.nx):
            upper = upper + wide(self.r2h[k, i - 1])
        lower = wide(own[k, x, y, rest])
        for j in range(1, self.geo.ny):
            lower = lower + wide(self.r2l[k, j - 1])
        if k:
            own[k, x, y, top] = low(upper)
            own[k, x, y, rest] = low(lower)
            self.three(k).start()
        else:
            self.total[top] = upper
            self.total[rest] = lower

    def finish(self):
        total = self.total[...]
        for k in range(1, self.geo.nz):
            self.three(k).wait()
            total = total + wide(self.zin[k - 1])
        self.total[...] = total

    def steps(self):
        return [
            [functools.partial(step, k) for k in self.order]
            for step in (self.step_one, self.step_two, self.step_three)
        ]

    @staticmethod
    def buffers(geo, levels, rows, cut, columns, kind):
        vmem = pltpu.VMEM
        nz, nx, ny = geo.nz, geo.nx, geo.ny
        rest = rows - cut
        return [
            vmem((nz, nx, ny, 2, rows, columns), kind),
            vmem((levels, nz, nx, ny, rows, columns), kind),
            vmem((levels, nz, ny - 1, nx, cut, columns), kind),
            vmem((levels, nz, nx - 1, ny, rest, columns), kind),
            vmem((levels, nz, nx - 1, cut, columns), kind),
            vmem((levels, nz, ny - 1, rest, columns), kind),
            vmem((levels, nz - 1, rows, columns), kind),
            vmem((rows, columns), jnp.float32),
        ]

    @staticmethod
    def semaphores(geo, count):
        dma = pltpu.SemaphoreType.DMA
        nz, nx, ny = geo.nz, geo.nx, geo.ny
        return (
            [dma((count, nz))] * 2
            + [dma((count, nz, ny - 1))] * 2
            + [dma((count, nz, nx - 1))] * 2
            + [dma((count, nz, nx - 1))] * 2
            + [dma((count, nz, ny - 1))] * 2
            + [dma((count, nz - 1))] * 2
        )


ROW_ATT_BIAS, ROW_IN_BIAS, ROW_OUT_BIAS, ROW_GAIN, ROW_SHIFT, ROW_FINAL, ROWS = 0, 3, 7, 8, 10, 12, 16


def step_kernel(geo, cuts, half_a, half_f, *refs):
    refs = list(refs)

    def take(count):
        taken = refs[:count]
        del refs[:count]
        return taken

    (stream_in, residue_in, seg, cot, qkv_in, out_in, ff_in_in, ff_out_in, att_in, in_bias_in, out_bias_in, gain_in,
     shift_in, final_gain_in, final_shift_in) = take(15)
    (out, stream_grad, residue_grad, qkv_grad, out_grad, ff_in_grad, ff_out_grad, att_grad, in_bias_grad, out_bias_grad,
     gain_grad, shift_grad, final_gain_grad, final_shift_grad) = take(14)
    (w, par, own_small, xl_next, xn, qs, kv, kt, pt, att, mid, act, slope, n1, n2, i1, i2, bias, segs, dkv, ob, sb, sc,
     rb, rc, small, sbuf, sin) = take(28)
    buffers_a, buffers_f = take(8), take(8)
    gather_sems, scatter_sems = take(12), take(12)
    (load_sem, seg_send, seg_recv, y_send, y_recv, c_send, c_recv, by_send, by_recv, bc_send, bc_recv, s_send,
     s_recv, residue_sem) = take(14)
    assert not refs

    z, xx, y, c = geo.here()
    s = 2 * y + c
    shard = (z * geo.nx + xx) * geo.seq + s
    count = geo.seq
    tokens, features = residue_in.shape
    levels = w.shape[0]
    width = features // geo.shards
    ff_rows = in_bias_in.shape[1]
    head = features // HEADS
    lanes = 2 * head
    pairs = features // lanes
    parts = act.shape[1]
    sibling, across = geo.device(z, xx, y, 1 - c), geo.device(z, xx, 1 - y, c)
    row_in = 4 * width + ROWS
    row_out = row_in + parts * width
    xl = [stream_in] + [xl_next.at[l - 1] for l in range(1, levels)]

    pieces = [
        (
            Gather(geo, w, l, 0, row_in, cuts[0], gather_sems, 2 * l),
            Gather(geo, w, l, row_in, parts * width + ff_rows, cuts[1], gather_sems, 2 * l + 1),
        )
        for l in range(levels)
    ]
    sums = [
        (
            Scatter(geo, *buffers_a, l, half_a, scatter_sems, 2 * l),
            Scatter(geo, *buffers_f, l, half_f, scatter_sems, 2 * l + 1),
        )
        for l in range(levels)
    ]

    def own_loads(l):
        mine = w.at[l, z, xx, y, c]
        pairs_of = [(qkv_in.at[l, :, pl.ds(n * features, features)], n * width, width) for n in range(3)]
        pairs_of.append((out_in.at[l], 3 * width, width))
        for n in range(parts):
            pairs_of.append((ff_in_in.at[l, :, pl.ds(n * features, features)], row_in + n * width, width))
        pairs_of.append((ff_out_in.at[l], row_out, ff_rows))
        return [
            pltpu.make_async_copy(src, mine.at[pl.ds(start, size)], load_sem.at[l, n])
            for n, (src, start, size) in enumerate(pairs_of)
        ]

    for l in range(levels):
        for copy in own_loads(l):
            copy.start()
    lane = lax.broadcasted_iota(jnp.int32, (width, features), 1)
    place = low(jnp.where(lane == shard * width + lax.broadcasted_iota(jnp.int32, (width, features), 0), 1.0, 0.0))
    lane = lax.broadcasted_iota(jnp.int32, (ff_rows, features), 1)
    ff_lane = lax.rem(shard, features // ff_rows) * ff_rows
    ff_place = low(jnp.where(lane == ff_lane + lax.broadcasted_iota(jnp.int32, (ff_rows, features), 0), 1.0, 0.0))
    own_small[...] = jnp.zeros_like(own_small)
    for l in range(levels):
        for n in range(3):
            own_small[l, ROW_ATT_BIAS + n : ROW_ATT_BIAS + n + 1, :] = product(att_in[n, l : l + 1, :], place)
        spread = product(in_bias_in[l : l + 1, :], ff_place)
        for j in range(parts):
            own_small[l, ROW_IN_BIAS + j : ROW_IN_BIAS + j + 1, :] = jnp.where(z == j, spread, 0.0)
        own_small[l, ROW_OUT_BIAS : ROW_OUT_BIAS + 1, :] = product(out_bias_in[l : l + 1, :], place)
        own_small[l, ROW_GAIN : ROW_GAIN + 2, :] = product(gain_in[l], place)
        own_small[l, ROW_SHIFT : ROW_SHIFT + 2, :] = product(shift_in[l], place)
        own_small[l, ROW_FINAL : ROW_FINAL + 1, :] = product(final_gain_in[...], place)
        own_small[l, ROW_FINAL + 1 : ROW_FINAL + 2, :] = product(final_shift_in[...], place)
        w[l, z, xx, y, c, 4 * width : row_in, :] = low(own_small[l])

    segs[0] = jnp.broadcast_to(seg[...], segs.shape[1:])
    greet(
        [geo.device(lax.rem(z + k, geo.nz), xx, y, c) for k in range(1, geo.nz)]
        + [
            geo.device(z, lax.rem(xx + i, geo.nx), lax.rem(y + j, geo.ny), lax.rem(c + k, 2))
            for i in range(geo.nx)
            for j in range(geo.ny)
            for k in range(2)
            if i or j or k
        ]
    )
    line = [(z * geo.nx + xx, lax.rem(s + k, count)) for k in range(1, count)]

    def seg_copy(k):
        return remote(segs.at[0], segs.at[k], seg_send.at[k], seg_recv.at[k], line[k - 1])

    def y_copy(l):
        return remote(xl[l], xn.at[l], y_send.at[l], y_recv.at[l], across)

    def c_copy(l, src):
        return remote(kv.at[l, src], kv.at[l, 1], c_send.at[l], c_recv.at[l], sibling)

    def send_stream(l):
        @pl.when(y == 0)
        def _():
            y_copy(l).start()

    for copy in own_loads(0)[:4]:
        copy.wait()
    nz = geo.nz
    (first_a, first_f), (next_a, next_f) = pieces
    first_a.own()
    for copy in own_loads(0)[4:]:
        copy.wait()
    for k in range(1, count):
        seg_copy(k).start()
    send_stream(0)
    first_f.own()
    for copy in own_loads(1):
        copy.wait()

    waiting = []

    def tick(number):
        for _ in range(min(number, len(waiting))):
            waiting.pop(0)()

    def drain(last):
        while any(task is last for task in waiting):
            tick(1)

    steps = [piece.steps() for piece in (first_a, first_f, next_a, next_f)]
    waiting.extend(steps[0][0] + steps[0][1] + steps[1][0] + steps[0][2] + [next_a.own])
    waiting.extend(steps[1][1] + steps[2][0] + steps[1][2] + [next_f.own])
    waiting.extend(steps[2][1] + steps[3][0] + steps[2][2] + steps[3][1] + steps[3][2])
    last_step = {}
    for piece in (first_a, first_f, next_a, next_f):
        own_steps = [task for task in waiting if task.__class__ is functools.partial and task.func.__self__ is piece]
        last_step[piece] = own_steps[-1]

    @pl.when(y == 0)
    def _():
        for l in range(levels):
            xn[l] = jnp.zeros_like(xn[l])

    @pl.when(s == 0)
    def _():
        for l in range(levels):
            kv[l, 1] = jnp.zeros_like(kv[l, 1])

    for k in range(1, count):
        seg_copy(k).wait()
    query_seg = segs[0, 0:1, :]
    query_pos = s * tokens + lax.broadcasted_iota(jnp.int32, (tokens, tokens), 1)
    for b in range(3):
        block = lax.rem(s + count - b, count)
        key_seg = jnp.transpose(jnp.broadcast_to(wide(segs[b, 0:1, :]), (128, tokens)))[:, 0:1]
        key_pos = block * tokens + lax.broadcasted_iota(jnp.int32, (tokens, tokens), 0)
        allowed = (key_seg == wide(query_seg)) & (key_pos <= query_pos)
        bias[b] = jnp.where(allowed, 0.0, masked_value)
    for l in range(levels):
        small[l] = jnp.zeros_like(small[l])

    def weight(l, start):
        return w[l, :, :, :, :, pl.ds(start, width), :].reshape(features, features)

    def out_weight(l, j):
        return w[l, j, :, :, :, pl.ds(row_out, ff_rows), :].reshape(features, features)

    g_a, g_f = buffers_a[0], buffers_f[0]

    def keep(ref, start, value):
        ref[:, :, :, :, pl.ds(start, width), :] = low(value).reshape(nz, geo.nx, geo.ny, 2, width, features)

    def keep_out(j, value):
        g_f[j, :, :, :, pl.ds(parts * width, ff_rows), :] = low(value).reshape(geo.nx, geo.ny, 2, ff_rows, features)

    def row(l, index):
        return par[l, index : index + 1, :]

    pair_lane = lax.broadcasted_iota(jnp.int32, (1, lanes), 1)

    def one_head(value, side):
        return jnp.where((pair_lane < head) == (side == 0), value, jnp.zeros_like(value))

    def ready(piece):
        drain(last_step[piece])
        piece.arrive()

    x, r = stream_grad, out
    residue_load = pltpu.make_async_copy(residue_in, r, residue_sem)
    residue_load.start()

    def forward(l):
        ready(pieces[l][0])
        par[l] = jnp.sum(
            wide(w[l, :, :, :, :, pl.ds(4 * width, ROWS), :]).reshape(geo.shards, ROWS, features), axis=0
        )
        xv = xl[l][...]
        keys = product(xv, weight(l, width))
        values = product(xv, weight(l, 2 * width)) + row(l, ROW_ATT_BIAS + 1)
        kv[l, 0, :, 0:features] = low(keys)
        kv[l, 0, :, features:] = low(values)

        @pl.when(c == 0)
        def _():
            c_copy(l, 0).start()

        tick(2)
        queries = low(product(xv, weight(l, 0)) + row(l, ROW_ATT_BIAS))
        qs[l] = queries * (1.0 / math.sqrt(head))

        @pl.when(y == 1)
        def _():
            y_copy(l).wait_recv()

        xv = xn[l]
        keys = product(xv, weight(l, width))
        values = product(xv, weight(l, 2 * width)) + row(l, ROW_ATT_BIAS + 1)
        kv[l, 2, :, 0:features] = low(keys)
        kv[l, 2, :, features:] = low(values)

        @pl.when((y == 1) & (c == 1))
        def _():
            c_copy(l, 2).start()

        tick(2)

        @pl.when((y == 1) | (c == 1))
        def _():
            c_copy(l, 0).wait_recv()

        for b in range(3):
            kt[:, b * tokens : (b + 1) * tokens] = jnp.transpose(kv[l, b, :, features:])

        def attend(p, carry):
            at = pl.ds(pl.multiple_of(p * lanes, lanes), lanes)
            queries = qs[l, :, at]
            keys = kv[l, :, :, at].reshape(3 * tokens, lanes)
            for side in range(2):
                scores = product_rows(keys, one_head(queries, side)) + bias[...].reshape(3 * tokens, tokens)
                terms = jnp.exp(scores - jnp.max(scores, axis=0, keepdims=True))
                probs = low(terms * (1.0 / jnp.sum(terms, axis=0, keepdims=True)))
                pt[l, 2 * p + side] = probs
                rows = pl.ds(pl.multiple_of(p * lanes + side * head, head), head)
                ob[rows, :] = product(kt[rows, :], probs)
            return carry

        for half in range(2):
            lax.fori_loop(half * pairs // 2, (half + 1) * pairs // 2, attend, 0)
            tick(5)
        att[l] = low(jnp.transpose(ob[...]))
        branch = product(att[l], weight(l, 3 * width)) + row(l, ROW_ATT_BIAS + 2)
        normal, inverse = normalize((wide(stream_in[...]) if l == 0 else x[...]) + branch)
        n1[l] = normal
        i1[l] = inverse
        middle = normal * row(l, ROW_GAIN) + row(l, ROW_SHIFT)
        mid[l] = low(middle)
        x[...] = middle
        if l == 0:
            residue_load.wait()
        r[...] = r[...] + branch
        ready(pieces[l][1])
        total = jnp.broadcast_to(row(l, ROW_OUT_BIAS), (tokens, features))
        for j in range(parts):
            hidden = product(mid[l], weight(l, row_in + j * width)) + row(l, ROW_IN_BIAS + j)
            active, rise = gelu_pair(hidden)
            act[l, j] = low(active)
            slope[l, j] = low(rise)
            total = total + product(act[l, j], out_weight(l, j))
            tick(2)
        r[...] = r[...] + total
        normal, inverse = normalize(x[...] + total)
        n2[l] = normal
        i2[l] = inverse
        next_x = normal * row(l, ROW_GAIN + 1) + row(l, ROW_SHIFT + 1)
        x[...] = next_x
        if l + 1 < levels:
            xl[l + 1][...] = low(next_x)
            send_stream(l + 1)

    def note(l, index, value):
        small[l, index : index + 1, :] = value

    def by_copy(l):
        return remote(sc.at[l], rc.at[l], by_send.at[l], by_recv.at[l], across)

    def bc_copy(l):
        return remote(sb.at[l], rb.at[l], bc_send.at[l], bc_recv.at[l], sibling)

    gx = stream_grad
    block_lanes = features // nz
    last = levels - 1
    sum_ones, stores = {}, []

    def queue_sum(scatter, store, l):
        one, two, three = scatter.steps()
        sum_ones[scatter] = one[-1]
        for n in range(len(one) + 3):
            for stage, lag in ((one, 0), (two, 2), (three, 3)):
                if 0 <= n - lag < len(one):
                    waiting.append(stage[n - lag])
        waiting.extend(stores)
        stores[:] = [functools.partial(store, l)]

    def backward(l):
        sum_a, sum_f = sums[l]
        grad = gx[...]
        note(l, ROW_GAIN + 1, column_sums(grad * n2[l]))
        note(l, ROW_SHIFT + 1, column_sums(grad))
        g2 = normalize_back(grad, n2[l], i2[l], row(l, ROW_GAIN + 1))
        d_ff = low(g2 + residue_grad[...])
        if l < last:
            drain(sum_ones[sums[l + 1][1]])
        note(l, ROW_OUT_BIAS, column_sums(wide(d_ff)))
        total = g2
        for j in range(parts):
            keep_out(j, product_tokens(act[l, j], d_ff))
            d_hidden = low(product_rows(d_ff, out_weight(l, j)) * wide(slope[l, j]))
            sums_in = column_sums(wide(d_hidden))
            for q in range(parts):
                block = sums_in[:, q * block_lanes : (q + 1) * block_lanes]
                small[l, ROW_IN_BIAS + q : ROW_IN_BIAS + q + 1, j * block_lanes : (j + 1) * block_lanes] = block
            keep(g_f, j * width, product_tokens(mid[l], d_hidden))
            total = total + product_rows(d_hidden, weight(l, row_in + j * width))
            tick(2)
        sum_f.begin()
        note(l, ROW_GAIN, column_sums(total * n1[l]))
        note(l, ROW_SHIFT, column_sums(total))
        g1 = normalize_back(total, n1[l], i1[l], row(l, ROW_GAIN))
        gx[...] = g1
        d_att = low(g1 + residue_grad[...])
        note(l, ROW_ATT_BIAS + 2, column_sums(wide(d_att)))
        if l < last:
            drain(sum_ones[sums[l + 1][0]])
        keep(g_a, 3 * width, product_tokens(att[l], d_att))
        att[l] = low(product_rows(d_att, weight(l, 3 * width)))
        queue_sum(sum_f, store_f, l)
        tick(4)
        for b in range(3):
            kt[:, b * tokens : (b + 1) * tokens] = jnp.transpose(kv[l, b, :, 0:features])

        def attend(p, carry):
            start = pl.multiple_of(p * lanes, lanes)
            at, at_values = pl.ds(start, lanes), pl.ds(start + features, lanes)
            queries, d_out = qs[l, :, at], att[l, :, at]
            values = kv[l, :, :, at_values].reshape(3 * tokens, lanes)
            d_keys = jnp.zeros((3 * tokens, lanes), jnp.float32)
            d_values = jnp.zeros((3 * tokens, lanes), jnp.float32)
            for side in range(2):
                own = one_head(d_out, side)
                probs = pt[l, 2 * p + side]
                terms = product_rows(values, own)
                weighted = terms * wide(probs)
                d_scores = low(weighted - wide(probs) * jnp.sum(weighted, axis=0, keepdims=True))
                d_values = d_values + product(probs, own)
                d_keys = d_keys + product(d_scores, one_head(queries, side))
                rows = pl.ds(pl.multiple_of(p * lanes + side * head, head), head)
                ob[rows, :] = product(kt[rows, :], d_scores)
            for where, value in ((at, d_keys), (at_values, d_values)):
                dkv[0, :, where] = value[:tokens]
                sb[l, :, where] = low(value[tokens : 2 * tokens])
                dkv[1, :, where] = value[2 * tokens :]
            return carry

        for half in range(2):
            lax.fori_loop(half * pairs // 2, (half + 1) * pairs // 2, attend, 0)
            tick(2)

        @pl.when((c == 1) | (y == 1))
        def _():
            bc_copy(l).start()

        @pl.when((y == 1) & (c == 1))
        def _():
            bc_copy(l).wait_recv()
            dkv[1] = dkv[1] + wide(rb[l])

        far_keys, far_values = low(dkv[1, :, 0:features]), low(dkv[1, :, features:])

        @pl.when(y == 1)
        def _():
            sc[l] = low(product_rows(far_keys, weight(l, width)) + product_rows(far_values, weight(l, 2 * width)))
            by_copy(l).start()

        tick(2)
        d_queries = low(jnp.transpose(ob[...]) * (1.0 / math.sqrt(head)))
        keep(g_a, 0, product_tokens(xl[l][...], d_queries))
        note(l, ROW_ATT_BIAS, column_sums(wide(d_queries)))

        @pl.when(c == 0)
        def _():
            bc_copy(l).wait_recv()
            dkv[0] = dkv[0] + wide(rb[l])

        d_keys, d_values = low(dkv[0, :, 0:features]), low(dkv[0, :, features:])
        keep(g_a, width, product_tokens(xl[l][...], d_keys) + product_tokens(xn[l], far_keys))
        keep(g_a, 2 * width, product_tokens(xl[l][...], d_values) + product_tokens(xn[l], far_values))
        note(l, ROW_ATT_BIAS + 1, column_sums(wide(d_values)) + column_sums(wide(far_values)))
        sum_a.begin()
        tick(2)
        gx[...] = (
            gx[...]
            + product_rows(d_queries, weight(l, 0))
            + product_rows(d_keys, weight(l, width))
            + product_rows(d_values, weight(l, 2 * width))
        )
        queue_sum(sum_a, store_a, l)
        tick(2)

        @pl.when(y == 0)
        def _():
            by_copy(l).wait_recv()
            gx[...] = gx[...] + wide(rc[l])

    def store_f(l):
        sum_f = sums[l][1]
        sum_f.finish()
        for n in range(parts):
            ff_in_grad[l, :, n * features : (n + 1) * features] = sum_f.total[n * width : (n + 1) * width]
        ff_out_grad[l] = sum_f.total[parts * width :]

    def store_a(l):
        sum_a = sums[l][0]
        sum_a.finish()
        for n in range(3):
            qkv_grad[l, :, n * features : (n + 1) * features] = sum_a.total[n * width : (n + 1) * width]
        out_grad[l] = sum_a.total[3 * width :]

    for l in range(levels):
        forward(l)
    normal, inverse = normalize(r[...])
    gain = row(last, ROW_FINAL)
    out[...] = x[...] + normal * gain + row(last, ROW_FINAL + 1)
    grad = cot[...]
    note(last, ROW_FINAL, column_sums(grad * normal))
    note(last, ROW_FINAL + 1, column_sums(grad))
    residue_grad[...] = normalize_back(grad, normal, inverse, gain)
    gx[...] = grad
    for l in reversed(range(levels)):
        backward(l)

    z_peers = [geo.device(lax.rem(z + k, nz), xx, y, c) for k in range(1, nz)]
    plane = [
        geo.device(z, lax.rem(xx + i, geo.nx), lax.rem(y + j, geo.ny), lax.rem(c + k, 2))
        for i in range(geo.nx)
        for j in range(geo.ny)
        for k in range(2)
    ][1:]

    def z_small(k):
        return remote(
            sbuf.at[lax.rem(z + k, nz)], sin.at[k - 1], s_send.at[k - 1], s_recv.at[k - 1], z_peers[k - 1]
        )

    def plane_small(n):
        m = nz - 1 + n
        return remote(sbuf.at[nz], sin.at[m], s_send.at[m], s_recv.at[m], plane[n])

    for k in range(nz):
        sbuf[k] = small[:, :, k * block_lanes : (k + 1) * block_lanes].reshape(levels * ROWS, block_lanes)
    for k in range(1, nz):
        z_small(k).start()
    waiting.extend(stores)
    while len(waiting) > 2 * nz + 1:
        tick(1)
    total = sbuf[z]
    for k in range(1, nz):
        z_small(k).wait()
        total = total + sin[k - 1]
    sbuf[nz] = total
    for n in range(len(plane)):
        plane_small(n).start()
    tick(nz)
    total = sbuf[nz]
    for n in range(len(plane)):
        plane_small(n).wait()
        total = total + sin[nz - 1 + n]
    exact = functools.partial(jnp.dot, preferred_element_type=jnp.float32, precision=lax.Precision.HIGHEST)

    def chosen(lane_count, first, size):
        lane = lax.broadcasted_iota(jnp.int32, (lane_count, size), 0)
        return jnp.where(lane == first + lax.broadcasted_iota(jnp.int32, (lane_count, size), 1), 1.0, 0.0)

    mine = exact(total, chosen(block_lanes, lax.rem(shard, geo.shards // nz) * width, width))
    in_block = exact(total, chosen(block_lanes, lax.rem(ff_lane, block_lanes), ff_rows))
    part = lax.broadcasted_iota(jnp.int32, (ROWS, 1), 0)
    for l in range(levels):
        own = mine[l * ROWS : (l + 1) * ROWS]
        for n in range(3):
            att_grad[n, l : l + 1, :] = own[ROW_ATT_BIAS + n : ROW_ATT_BIAS + n + 1]
        in_rows = in_block[l * ROWS : (l + 1) * ROWS]
        in_bias_grad[l : l + 1, :] = column_sums(
            jnp.where(part == ROW_IN_BIAS + lax.div(ff_lane, block_lanes), in_rows, 0.0)
        )
        out_bias_grad[l : l + 1, :] = own[ROW_OUT_BIAS : ROW_OUT_BIAS + 1]
        gain_grad[l] = own[ROW_GAIN : ROW_GAIN + 2]
        shift_grad[l] = own[ROW_SHIFT : ROW_SHIFT + 2]
    final_gain_grad[...] = own[ROW_FINAL : ROW_FINAL + 1]
    final_shift_grad[...] = own[ROW_FINAL + 1 : ROW_FINAL + 2]
    while waiting:
        tick(1)

    for l in range(levels):
        for piece in pieces[l]:
            piece.finish()

        @pl.when(y == 0)
        def _(l=l):
            y_copy(l).wait_send()

        @pl.when((y == 1) | (c == 0))
        def _(l=l):
            c_copy(l, 0).wait_send()

        @pl.when((c == 1) | (y == 1))
        def _(l=l):
            bc_copy(l).wait_send()

        @pl.when(y == 1)
        def _(l=l):
            by_copy(l).wait_send()


def run_step(geo, stream_in, residue_in, seg, cot, shards):
    tokens, features = residue_in.shape
    levels, width, qkv_columns = shards[0].shape
    parts = shards[2].shape[2] // features
    ff_rows = shards[3].shape[1]
    rows_a, rows_f = 4 * width, parts * width + ff_rows
    shape = (geo.nz, geo.nx, geo.ny, 2)
    dma, vmem = pltpu.SemaphoreType.DMA, pltpu.VMEM
    wide_kind, kind = jnp.float32, jnp.bfloat16
    whole = pl.BlockSpec(memory_space=pltpu.VMEM)
    away = pl.BlockSpec(memory_space=pl.ANY)
    row = (tokens, features)
    half_a, half_f = 2 * width, 4 * width
    cuts = (2 * width, 3 * width)
    others = geo.nz - 1 + 2 * geo.nx * geo.ny - 1
    outs = [row, row, row] + [member.shape for member in shards]
    scratch = [
        vmem((levels,) + shape + (rows_a + ROWS + rows_f, features), kind),
        vmem((levels, ROWS, features), wide_kind),
        vmem((levels, ROWS, features), wide_kind),
        vmem((levels - 1,) + row, kind),
        vmem((levels,) + row, kind),
        vmem((levels,) + row, kind),
        vmem((levels, 3, tokens, 2 * features), kind),
        vmem((features, 3 * tokens), kind),
        vmem((levels, HEADS, 3 * tokens, tokens), kind),
        vmem((levels,) + row, kind),
        vmem((levels,) + row, kind),
        vmem((levels, parts) + row, kind),
        vmem((levels, parts) + row, kind),
        vmem((levels,) + row, wide_kind),
        vmem((levels,) + row, wide_kind),
        vmem((levels, tokens, 1), wide_kind),
        vmem((levels, tokens, 1), wide_kind),
        vmem((3, tokens, tokens), wide_kind),
        vmem((geo.seq, 8, tokens), jnp.int32),
        vmem((2, tokens, 2 * features), wide_kind),
        vmem((features, tokens), wide_kind),
        vmem((levels, tokens, 2 * features), kind),
        vmem((levels,) + row, kind),
        vmem((levels, tokens, 2 * features), kind),
        vmem((levels,) + row, kind),
        vmem((levels, ROWS, features), wide_kind),
        vmem((geo.nz + 1, levels * ROWS, features // geo.nz), wide_kind),
        vmem((others, levels * ROWS, features // geo.nz), wide_kind),
    ]
    scratch += Scatter.buffers(geo, levels, rows_a, half_a, features, kind)
    scratch += Scatter.buffers(geo, levels, rows_f, half_f, features, kind)
    scratch += Gather.semaphores(geo, 2 * levels) + Scatter.semaphores(geo, 2 * levels)
    scratch += [dma((levels, 5 + parts))] + [dma((geo.seq,))] * 2 + [dma((levels,))] * 8 + [dma((others,))] * 2 + [dma(())]
    return pl.pallas_call(
        functools.partial(step_kernel, geo, cuts, half_a, half_f),
        out_shape=tuple(jax.ShapeDtypeStruct(shape_of, wide_kind) for shape_of in outs),
        in_specs=[whole, away, whole, whole] + [away] * 4 + [whole] * 7,
        out_specs=(whole,) * len(outs),
        scratch_shapes=scratch,
        compiler_params=pltpu.CompilerParams(
            collective_id=0, has_side_effects=True, vmem_limit_bytes=64 << 20
        ),
        name="run_step",
    )(stream_in, residue_in, seg, cot, *shards)


def settle_kernel(count, *refs):
    sources, targets, held, (loads, stores) = refs[:count], refs[count : 2 * count], refs[2 * count : -2], refs[-2:]
    into = [pltpu.make_async_copy(src, buf, loads.at[n]) for n, (src, buf) in enumerate(zip(sources, held))]
    away = [pltpu.make_async_copy(buf, dst, stores.at[n]) for n, (buf, dst) in enumerate(zip(held, targets))]
    for copy in into:
        copy.start()
    for load, store in zip(into, away):
        load.wait()
        store.start()
    for copy in away:
        copy.wait()


def settle(values):
    count = len(values)
    away = pl.BlockSpec(memory_space=pl.ANY)
    return pl.pallas_call(
        functools.partial(settle_kernel, count),
        out_shape=tuple(jax.ShapeDtypeStruct(value.shape, value.dtype) for value in values),
        in_specs=[away] * count,
        out_specs=(away,) * count,
        scratch_shapes=[pltpu.VMEM(value.shape, value.dtype) for value in values]
        + [pltpu.SemaphoreType.DMA((count,))] * 2,
        name="settle",
    )(*values)


def gather_plain(shards, number):
    gathered = [
        lax.all_gather(shards[member][number], ("dp", "seq"), axis=axis, tiled=True)
        for member, axis in enumerate((0, 0, 0, 0, 1, 0, 0, 1, 1))
    ]
    return tuple(gathered) + tuple(
        lax.all_gather(shards[member], ("dp", "seq"), axis=0, tiled=True) for member in (9, 10)
    )


def body_plain(geo, *args):
    stream_in, residue_in, segments, out_cot = args[:4]
    shards = args[4:]
    levels, width, _ = shards[1].shape
    ff_width = shards[3].shape[1]
    stream = stream_in[0].astype(jnp.float32)
    residue = residue_in[0]
    cotangent = out_cot[0]
    tokens = stream.shape[0]
    query_seg = segments[0]
    whole_seg = lax.all_gather(query_seg, "seq", axis=0, tiled=True)
    seq_index = lax.axis_index("seq")
    query_pos = seq_index * tokens + jnp.arange(tokens, dtype=jnp.int32)
    weights = [gather_plain(shards, number) for number in range(levels)]
    states = []
    for number in range(levels):
        stream, residue, state = layer_forward(stream, residue, weights[number], query_pos, query_seg, whole_seg)
        states.append(state)
    final_norm, pull_final = jax.vjp(
        layer_norm,
        residue,
        weights[-1][9].astype(jnp.float32),
        weights[-1][10].astype(jnp.float32),
    )
    output = stream + final_norm
    grad_residue, final_gain_grad, final_shift_grad = pull_final(cotangent)
    grad_stream = cotangent
    grads = [None] * levels
    for number in reversed(range(levels)):
        grad_stream, grads[number] = layer_backward(
            states[number], weights[number], grad_stream, grad_residue, query_pos, query_seg
        )
    summed = [
        jnp.stack(
            [
                lax.psum_scatter(grads[number][member], ("dp", "seq"), scatter_dimension=axis, tiled=True)
                for number in range(levels)
            ]
        )
        for member, axis in enumerate((0, 0, 0, 0, 1, 0, 0, 1, 1))
    ] + [
        lax.psum_scatter(final_gain_grad, ("dp", "seq"), scatter_dimension=0, tiled=True),
        lax.psum_scatter(final_shift_grad, ("dp", "seq"), scatter_dimension=0, tiled=True),
    ]
    return (output[None], grad_stream[None], grad_residue[None]) + tuple(summed)


def body(geo, *args):
    stream_in, residue_in, segments, out_cot = args[:4]
    shards = list(args[4:])
    shards[4] = shards[4].transpose(1, 0, 2)
    shards[-2:] = [shards[-2][None], shards[-1][None]]
    results = list(settle(run_step(geo, stream_in[0], residue_in[0], segments, out_cot[0], shards)))
    results[7] = results[7].transpose(1, 0, 2)
    return tuple(value[None] for value in results[:3]) + tuple(results[3:-2]) + (results[-2][0], results[-1][0])


def solution(mesh):
    geo = Geometry(mesh)
    chosen = body if geo.seq == 4 and geo.nz == 4 else body_plain
    return jax.shard_map(
        functools.partial(chosen, geo),
        mesh=mesh,
        in_specs=(
            P("dp", "seq", None),
            P("dp", "seq", None),
            P("dp", "seq"),
            P("dp", "seq", None),
            P(None, ("dp", "seq"), None),
            P(None, ("dp", "seq"), None),
            P(None, ("dp", "seq"), None),
            P(None, ("dp", "seq"), None),
            P(None, None, ("dp", "seq")),
            P(None, ("dp", "seq")),
            P(None, ("dp", "seq")),
            P(None, None, ("dp", "seq")),
            P(None, None, ("dp", "seq")),
            P(("dp", "seq")),
            P(("dp", "seq")),
        ),
        out_specs=(
            P("dp", "seq", None),
            P("dp", "seq", None),
            P("dp", "seq", None),
            P(None, ("dp", "seq"), None),
            P(None, ("dp", "seq"), None),
            P(None, ("dp", "seq"), None),
            P(None, ("dp", "seq"), None),
            P(None, None, ("dp", "seq")),
            P(None, ("dp", "seq")),
            P(None, ("dp", "seq")),
            P(None, None, ("dp", "seq")),
            P(None, None, ("dp", "seq")),
            P(("dp", "seq")),
            P(("dp", "seq")),
        ),
        check_vma=False,
    )
```

```python
import functools
import itertools
import math

import jax
import jax.numpy as jnp
from jax import lax
from jax.experimental import pallas as pl
from jax.experimental.pallas import tpu as pltpu
from jax.sharding import PartitionSpec as P

HEADS = 8
MESH = pl.DeviceIdType.MESH


class Geometry:
    def __init__(self, mesh):
        self.dp, self.seq = mesh.shape["dp"], mesh.shape["seq"]
        self.ny = self.seq // 2
        self.nx = self.ny
        self.nz = self.dp // self.nx
        self.shards = self.dp * self.seq

    def here(self):
        dp, seq = lax.axis_index("dp"), lax.axis_index("seq")
        return lax.div(dp, self.nx), lax.rem(dp, self.nx), lax.div(seq, 2), lax.rem(seq, 2)

    def device(self, z, x, y, c):
        return (z * self.nx + x, y * 2 + c)

    def peers(self):
        z, x, y, c = self.here()
        found = [self.device(lax.rem(z + k, self.nz), x, y, c) for k in range(1, self.nz)]
        found += [self.device(z, lax.rem(x + k, self.nx), y, c) for k in range(1, self.nx)]
        found += [self.device(z, x, lax.rem(y + k, self.ny), c) for k in range(1, self.ny)]
        return found + [self.device(z, x, y, 1 - c)]


def greet(devices):
    barrier = pltpu.get_barrier_semaphore()
    for device in devices:
        pl.semaphore_signal(barrier, inc=1, device_id=device, device_id_type=MESH)
    pl.semaphore_wait(barrier, len(devices))


def remote(src, dst, send_sem, recv_sem, device):
    return pltpu.make_async_remote_copy(
        src_ref=src,
        dst_ref=dst,
        send_sem=send_sem,
        recv_sem=recv_sem,
        device_id=device,
        device_id_type=MESH,
    )


epsilon = 1e-05
masked_value = -1e30


def smooth_gate(values):
    return jax.nn.gelu(values, approximate=True)


def layer_norm(values, norm_gain, norm_shift):
    average = jnp.mean(values, axis=-1, keepdims=True)
    centred = values - average
    variance = jnp.mean(centred * centred, axis=-1, keepdims=True)
    return centred * lax.rsqrt(variance + epsilon) * norm_gain + norm_shift


def keep_state(carried):
    return carried


def allowed_pairs(query_pos, query_seg, key_pos, key_seg):
    return (query_seg[:, None] == key_seg[None, :]) & (key_pos[None, :] <= query_pos[:, None])


def block_needed(query_pos, query_seg, key_pos, key_seg):
    return (key_pos[0] <= query_pos[-1]) & (key_seg[-1] >= query_seg[0])


def key_blocks(keys_values, key_seg):
    length = keys_values.shape[0]
    features = keys_values.shape[1] // 2
    head_size = features // HEADS
    block_rows = math.gcd(length, 512)
    block_count = length // block_rows
    split_kv = keys_values.reshape(block_count, block_rows, 2, HEADS, head_size)
    key_pos = jnp.arange(length, dtype=jnp.int32).reshape(block_count, block_rows)
    return (split_kv[:, :, 0], split_kv[:, :, 1], key_pos, key_seg.reshape(block_count, block_rows))


def block_scores(queries3, key_block, query_pos, query_seg, key_pos, key_seg):
    scaling = 1.0 / math.sqrt(queries3.shape[-1])
    raw_scores = (
        jnp.einsum("qhd,khd->hqk", queries3, key_block, preferred_element_type=jnp.float32)
        * scaling
    )
    return (raw_scores, allowed_pairs(query_pos, query_seg, key_pos, key_seg)[None])


def attention_forward(queries3, blocks, query_pos, query_seg):
    tokens, head_count, head_size = queries3.shape

    def statistics(carried, block_items):
        key_block, value_block, key_pos, key_seg = block_items

        def statistics_compute(running):
            run_max, run_sum = running
            raw_scores, allowed = block_scores(
                queries3, key_block, query_pos, query_seg, key_pos, key_seg
            )
            new_max = jnp.maximum(
                run_max, jnp.max(jnp.where(allowed, raw_scores, masked_value), axis=-1)
            )
            exp_terms = jnp.exp(jnp.where(allowed, raw_scores - new_max[..., None], masked_value))
            return (new_max, run_sum * jnp.exp(run_max - new_max) + jnp.sum(exp_terms, axis=-1))

        needed = block_needed(query_pos, query_seg, key_pos, key_seg)
        return (lax.cond(needed, statistics_compute, keep_state, carried), None)

    initial = (
        jnp.full((head_count, tokens), masked_value, jnp.float32),
        jnp.zeros((head_count, tokens), jnp.float32),
    )
    (run_max, run_sum), unused = lax.scan(statistics, initial, blocks)
    log_total = run_max + jnp.log(run_sum)

    def accumulate(carried, block_items):
        key_block, value_block, key_pos, key_seg = block_items

        def accumulate_compute(running):
            raw_scores, allowed = block_scores(
                queries3, key_block, query_pos, query_seg, key_pos, key_seg
            )
            weights = jnp.exp(jnp.where(allowed, raw_scores - log_total[..., None], masked_value))
            weights = weights.astype(jnp.bfloat16)
            return running + jnp.einsum(
                "hqk,khd->qhd", weights, value_block, preferred_element_type=jnp.float32
            )

        needed = block_needed(query_pos, query_seg, key_pos, key_seg)
        return (lax.cond(needed, accumulate_compute, keep_state, carried), None)

    mixed_heads, unused = lax.scan(
        accumulate, jnp.zeros((tokens, head_count, head_size), jnp.float32), blocks
    )
    return (mixed_heads, log_total)


def attention_backward(queries3, blocks, query_pos, query_seg, log_total, mixed_heads, grad_heads):
    tokens, head_count, head_size = queries3.shape
    scaling = 1.0 / math.sqrt(head_size)
    row_dots = jnp.sum(mixed_heads * grad_heads.astype(jnp.float32), axis=-1).T
    block_rows = blocks[0].shape[1]
    block_count = blocks[0].shape[0]

    def backward_step(grad_queries, block_items):
        key_block, value_block, key_pos, key_seg = block_items

        def backward_compute(running):
            raw_scores, allowed = block_scores(
                queries3, key_block, query_pos, query_seg, key_pos, key_seg
            )
            prob_values = jnp.exp(
                jnp.where(allowed, raw_scores - log_total[..., None], masked_value)
            )
            grad_values = jnp.einsum(
                "hqk,qhd->khd",
                prob_values.astype(jnp.bfloat16),
                grad_heads,
                preferred_element_type=jnp.float32,
            )
            grad_probs = jnp.einsum(
                "qhd,khd->hqk", grad_heads, value_block, preferred_element_type=jnp.float32
            )
            grad_scores = (prob_values * (grad_probs - row_dots[..., None])).astype(jnp.bfloat16)
            running = (
                running
                + jnp.einsum(
                    "hqk,khd->qhd", grad_scores, key_block, preferred_element_type=jnp.float32
                )
                * scaling
            )
            grad_keys = (
                jnp.einsum(
                    "hqk,qhd->khd", grad_scores, queries3, preferred_element_type=jnp.float32
                )
                * scaling
            )
            return (running, grad_keys, grad_values)

        def skip_block(running):
            empty_rows = jnp.zeros((block_rows, head_count, head_size), jnp.float32)
            return (running, empty_rows, empty_rows)

        needed = block_needed(query_pos, query_seg, key_pos, key_seg)
        grad_queries, grad_keys, grad_values = lax.cond(
            needed, backward_compute, skip_block, grad_queries
        )
        return (grad_queries, (grad_keys, grad_values))

    initial = jnp.zeros((tokens, head_count, head_size), jnp.float32)
    grad_queries, (grad_keys, grad_values) = lax.scan(backward_step, initial, blocks)
    length = block_count * block_rows
    return (
        grad_queries.reshape(tokens, head_count * head_size),
        grad_keys.reshape(length, head_count * head_size),
        grad_values.reshape(length, head_count * head_size),
    )


def layer_forward(stream, residue, weights, query_pos, query_seg, key_seg):
    (
        qkv_weight,
        out_weight,
        ff_in_weight,
        ff_out_weight,
        att_bias,
        ff_in_bias,
        ff_out_bias,
        norm_gain,
        norm_shift,
    ) = weights[:9]
    tokens, features = stream.shape
    stream_low = stream.astype(jnp.bfloat16)
    bias_row = jnp.concatenate([att_bias[0], jnp.zeros_like(att_bias[0]), att_bias[1]]).astype(
        jnp.float32
    )
    joined = (
        jnp.dot(stream_low, qkv_weight, preferred_element_type=jnp.float32) + bias_row
    ).astype(jnp.bfloat16)
    queries3 = joined[:, :features].reshape(tokens, HEADS, features // HEADS)
    keys_values = lax.all_gather(joined[:, features:], "seq", axis=0, tiled=True)
    blocks = key_blocks(keys_values, key_seg)
    mixed_heads, log_total = attention_forward(queries3, blocks, query_pos, query_seg)
    attended = mixed_heads.reshape(tokens, features).astype(jnp.bfloat16)
    branch_att = jnp.dot(attended, out_weight, preferred_element_type=jnp.float32) + att_bias[
        2
    ].astype(jnp.float32)
    middle, pull_first = jax.vjp(
        layer_norm,
        stream + branch_att,
        norm_gain[0].astype(jnp.float32),
        norm_shift[0].astype(jnp.float32),
    )
    residue_mid = residue + branch_att
    middle_low = middle.astype(jnp.bfloat16)
    hidden = jnp.dot(
        middle_low, ff_in_weight, preferred_element_type=jnp.float32
    ) + ff_in_bias.astype(jnp.float32)
    active = smooth_gate(hidden).astype(jnp.bfloat16)
    branch_ff = jnp.dot(
        active, ff_out_weight, preferred_element_type=jnp.float32
    ) + ff_out_bias.astype(jnp.float32)
    stream_next, pull_second = jax.vjp(
        layer_norm,
        middle + branch_ff,
        norm_gain[1].astype(jnp.float32),
        norm_shift[1].astype(jnp.float32),
    )
    saved_state = (
        stream_low,
        queries3,
        blocks,
        mixed_heads,
        log_total,
        attended,
        pull_first,
        middle_low,
        hidden,
        active,
        pull_second,
    )
    return (stream_next, residue_mid + branch_ff, saved_state)


def layer_backward(saved_state, weights, grad_stream, grad_residue, query_pos, query_seg):
    (
        stream_low,
        queries3,
        blocks,
        mixed_heads,
        log_total,
        attended,
        pull_first,
        middle_low,
        hidden,
        active,
        pull_second,
    ) = saved_state
    qkv_weight, out_weight, ff_in_weight, ff_out_weight = weights[:4]
    grad_second, gain_second, shift_second = pull_second(grad_stream)
    grad_ff = (grad_second + grad_residue).astype(jnp.bfloat16)
    grad_ff_out = jnp.einsum("tf,td->fd", active, grad_ff, preferred_element_type=jnp.float32)
    bias_ff_out = jnp.sum(grad_ff.astype(jnp.float32), axis=0)
    grad_active = jnp.einsum(
        "td,fd->tf", grad_ff, ff_out_weight, preferred_element_type=jnp.float32
    )
    unused_gate, pull_gate = jax.vjp(smooth_gate, hidden)
    grad_hidden = pull_gate(grad_active)[0].astype(jnp.bfloat16)
    grad_ff_in = jnp.einsum(
        "td,tf->df", middle_low, grad_hidden, preferred_element_type=jnp.float32
    )
    bias_ff_in = jnp.sum(grad_hidden.astype(jnp.float32), axis=0)
    grad_middle = grad_second + jnp.einsum(
        "tf,df->td", grad_hidden, ff_in_weight, preferred_element_type=jnp.float32
    )
    grad_first, gain_first, shift_first = pull_first(grad_middle)
    grad_att = (grad_first + grad_residue).astype(jnp.bfloat16)
    grad_out = jnp.einsum("te,td->ed", attended, grad_att, preferred_element_type=jnp.float32)
    bias_att_out = jnp.sum(grad_att.astype(jnp.float32), axis=0)
    grad_attended = jnp.einsum(
        "td,ed->te", grad_att, out_weight, preferred_element_type=jnp.float32
    )
    grad_attended = grad_attended.astype(jnp.bfloat16)
    tokens, features = grad_attended.shape
    grad_queries, grad_keys, grad_values = attention_backward(
        queries3,
        blocks,
        query_pos,
        query_seg,
        log_total,
        mixed_heads,
        grad_attended.reshape(tokens, HEADS, features // HEADS),
    )
    key_grads, value_grads = (
        lax.psum_scatter(
            grad_keys.astype(jnp.bfloat16), "seq", scatter_dimension=0, tiled=True
        ).astype(jnp.float32),
        lax.psum_scatter(
            grad_values.astype(jnp.bfloat16), "seq", scatter_dimension=0, tiled=True
        ).astype(jnp.float32),
    )
    grad_joined = jnp.concatenate([grad_queries, key_grads, value_grads], axis=1).astype(
        jnp.bfloat16
    )
    grad_qkv = jnp.einsum("td,te->de", stream_low, grad_joined, preferred_element_type=jnp.float32)
    column_sums = jnp.sum(grad_joined.astype(jnp.float32), axis=0)
    bias_att = jnp.stack([column_sums[:features], column_sums[2 * features :], bias_att_out])
    grad_stream_in = grad_first + jnp.einsum(
        "te,de->td", grad_joined, qkv_weight, preferred_element_type=jnp.float32
    )
    layer_grads = (
        grad_qkv,
        grad_out,
        grad_ff_in,
        grad_ff_out,
        bias_att,
        bias_ff_in,
        bias_ff_out,
        jnp.stack([gain_first, gain_second]),
        jnp.stack([shift_first, shift_second]),
    )
    return (grad_stream_in, layer_grads)


def product(left, right):
    return lax.dot_general(left, right, (((1,), (0,)), ((), ())), preferred_element_type=jnp.float32)


def product_rows(left, right):
    return lax.dot_general(left, right, (((1,), (1,)), ((), ())), preferred_element_type=jnp.float32)


def product_tokens(left, right):
    return lax.dot_general(left, right, (((0,), (0,)), ((), ())), preferred_element_type=jnp.float32)


def wide(value):
    return value.astype(jnp.float32)


def low(value):
    return value.astype(jnp.bfloat16)


def normalize(values):
    centred = values - jnp.mean(values, axis=-1, keepdims=True)
    inverse = lax.rsqrt(jnp.mean(centred * centred, axis=-1, keepdims=True) + epsilon)
    return centred * inverse, inverse


def normalize_back(grad, normal, inverse, gain):
    scaled = grad * gain
    return (
        scaled
        - jnp.mean(scaled, axis=-1, keepdims=True)
        - normal * jnp.mean(scaled * normal, axis=-1, keepdims=True)
    ) * inverse


def column_sums(values):
    return jnp.sum(values, axis=0, keepdims=True)


def gelu_pair(v):
    rate = math.sqrt(2.0 / math.pi)
    square = v * v
    bent = jnp.tanh(v * (rate + (rate * 0.044715) * square))
    rise = 0.5 + 0.5 * bent
    slope = rise + v * (0.5 - 0.5 * bent * bent) * (rate + (3.0 * rate * 0.044715) * square)
    return v * rise, slope


class Gather:
    def __init__(self, geo, w, l, start, size, cut, sems, number):
        self.geo, self.w, self.l, self.start, self.size, self.cut = geo, w, l, start, size, cut
        (self.z_send, self.z_recv, self.x_send, self.x_recv, self.y_send, self.y_recv, self.xd_send, self.xd_recv,
         self.yd_send, self.yd_recv, self.c_send, self.c_recv) = (sem.at[number] for sem in sems)
        self.here = geo.here()
        z, last = self.here[0], geo.nz - 1
        self.back = [0]
        for n in range(last):
            below, above = n + 1, last - n
            half = n // 2
            between = 1 + half if n % 2 == 0 else last - half
            self.back.append(jnp.where(z == 0, above, jnp.where(z == last, below, between)))

    def at(self, n, i, j, low=None):
        geo, (z, x, y, c) = self.geo, self.here
        rows = (self.start, self.size)
        if low is not None:
            rows = (self.start + self.cut, self.size - self.cut) if low else (self.start, self.cut)
        return self.w.at[
            self.l,
            lax.rem(z + geo.nz - self.back[n], geo.nz),
            lax.rem(x + geo.nx - i, geo.nx),
            lax.rem(y + geo.ny - j, geo.ny),
            c,
            pl.ds(*rows),
        ]

    def z_copies(self, n):
        geo, (z, x, y, c) = self.geo, self.here
        back, piece = self.back[n], self.at(n, 0, 0)
        up = remote(
            piece, piece, self.z_send.at[0, n], self.z_recv.at[lax.rem(back + 1, geo.nz)],
            geo.device(lax.rem(z + 1, geo.nz), x, y, c),
        )
        down = remote(
            piece, piece, self.z_send.at[1, n], self.z_recv.at[lax.rem(back + geo.nz - 1, geo.nz)],
            geo.device(lax.rem(z + geo.nz - 1, geo.nz), x, y, c),
        )
        own = n == 0
        return [
            ((back <= z) & (z < geo.nz - 1), up),
            (((back > z) | own) & (z > 0), down),
        ]

    def z_arrival(self, n):
        piece, (z, x, y, c) = self.at(n, 0, 0), self.here
        return remote(
            piece, piece, self.z_send.at[0, n], self.z_recv.at[self.back[n]],
            self.geo.device(lax.rem(z + 1, self.geo.nz), x, y, c),
        )

    def x_copy(self, n, i):
        z, x, y, c = self.here
        piece = self.at(n, 0, 0)
        return remote(piece, piece, self.x_send.at[n, i - 1], self.x_recv.at[n, i - 1],
                      self.geo.device(z, lax.rem(x + i, self.geo.nx), y, c))

    def y_copy(self, n, j):
        z, x, y, c = self.here
        piece = self.at(n, 0, 0)
        return remote(piece, piece, self.y_send.at[n, j - 1], self.y_recv.at[n, j - 1],
                      self.geo.device(z, x, lax.rem(y + j, self.geo.ny), c))

    def x_forward(self, n, i, j):
        z, x, y, c = self.here
        piece, index = self.at(n, 0, j, True), (n, i - 1, j - 1)
        return remote(piece, piece, self.xd_send.at[index], self.xd_recv.at[index],
                      self.geo.device(z, lax.rem(x + i, self.geo.nx), y, c))

    def y_forward(self, n, i, j):
        z, x, y, c = self.here
        piece, index = self.at(n, i, 0, False), (n, i - 1, j - 1)
        return remote(piece, piece, self.yd_send.at[index], self.yd_recv.at[index],
                      self.geo.device(z, x, lax.rem(y + j, self.geo.ny), c))

    def c_copy(self, n):
        geo, (z, x, y, c) = self.geo, self.here
        piece = self.w.at[self.l, lax.rem(z + geo.nz - self.back[n], geo.nz), :, :, c, pl.ds(self.start, self.size)]
        return remote(piece, piece, self.c_send.at[n], self.c_recv.at[n], geo.device(z, x, y, 1 - c))

    def fan(self, n):
        for needed, copy in self.z_copies(n):
            pl.when(needed)(copy.start)
        for i in range(1, self.geo.nx):
            self.x_copy(n, i).start()
        for j in range(1, self.geo.ny):
            self.y_copy(n, j).start()

    def own(self):
        self.fan(0)

    def from_z(self, n):
        self.z_arrival(n).wait_recv()
        self.fan(n)

    def from_line(self, n):
        nx, ny = self.geo.nx, self.geo.ny
        for j in range(1, ny):
            self.y_copy(n, j).wait_recv()
            for i in range(1, nx):
                self.x_forward(n, i, j).start()
        for i in range(1, nx):
            self.x_copy(n, i).wait_recv()
            for j in range(1, ny):
                self.y_forward(n, i, j).start()

    def from_corner(self, n):
        for i in range(1, self.geo.nx):
            for j in range(1, self.geo.ny):
                self.x_forward(n, i, j).wait_recv()
                self.y_forward(n, i, j).wait_recv()
        self.c_copy(n).start()

    def steps(self):
        every = range(self.geo.nz)
        return [
            [functools.partial(self.from_z, n) for n in every if n],
            [functools.partial(self.from_line, n) for n in every],
            [functools.partial(self.from_corner, n) for n in every],
        ]

    def arrive(self):
        for n in range(self.geo.nz):
            self.c_copy(n).wait_recv()

    def finish(self):
        nx, ny = self.geo.nx, self.geo.ny
        for n in range(self.geo.nz):
            self.c_copy(n).wait_send()
            for needed, copy in self.z_copies(n):
                pl.when(needed)(copy.wait_send)
            for i in range(1, nx):
                self.x_copy(n, i).wait_send()
            for j in range(1, ny):
                self.y_copy(n, j).wait_send()
            for i in range(1, nx):
                for j in range(1, ny):
                    self.x_forward(n, i, j).wait_send()
                    self.y_forward(n, i, j).wait_send()

    @staticmethod
    def semaphores(geo, count):
        dma = pltpu.SemaphoreType.DMA
        nz, nx, ny = geo.nz, geo.nx, geo.ny
        return (
            [dma((count, 2, nz)), dma((count, nz))]
            + [dma((count, nz, nx - 1))] * 2
            + [dma((count, nz, ny - 1))] * 2
            + [dma((count, nz, nx - 1, ny - 1))] * 4
            + [dma((count, nz))] * 2
        )


class Scatter:
    def __init__(self, geo, g, own, r1h, r1l, r2h, r2l, zin, total, l, cut, sems, number):
        self.geo, self.g, self.own, self.l, self.cut = geo, g, own.at[l], l, cut
        self.r1h, self.r1l, self.r2h, self.r2l, self.zin = (ref.at[l] for ref in (r1h, r1l, r2h, r2l, zin))
        self.total = total
        self.rows = g.shape[4]
        self.sems = [sem.at[number] for sem in sems]
        self.z, self.x, self.y, self.c = geo.here()
        self.order = list(range(1, geo.nz)) + [0]

    def copy(self, src, dst, number, index, device):
        return remote(src, dst, self.sems[number].at[index], self.sems[number + 1].at[index], device)

    def cross(self, k):
        return self.copy(
            self.g.at[lax.rem(self.z + k, self.geo.nz), :, :, 1 - self.c], self.own.at[k], 0, (k,),
            self.geo.device(self.z, self.x, self.y, 1 - self.c),
        )

    def to_x(self, src, dst, number, index, i):
        return self.copy(src, dst, number, index, self.geo.device(self.z, lax.rem(self.x + i, self.geo.nx), self.y, self.c))

    def to_y(self, src, dst, number, index, j):
        return self.copy(src, dst, number, index, self.geo.device(self.z, self.x, lax.rem(self.y + j, self.geo.ny), self.c))

    def one(self, k):
        nx, ny = self.geo.nx, self.geo.ny
        top, rest = pl.ds(0, self.cut), pl.ds(self.cut, self.rows - self.cut)
        return [
            self.to_y(self.own.at[k, :, lax.rem(self.y + j, ny), top], self.r1h.at[k, j - 1], 2, (k, j - 1), j)
            for j in range(1, ny)
        ] + [
            self.to_x(self.own.at[k, lax.rem(self.x + i, nx), :, rest], self.r1l.at[k, i - 1], 4, (k, i - 1), i)
            for i in range(1, nx)
        ]

    def two(self, k):
        nx, ny = self.geo.nx, self.geo.ny
        top, rest = pl.ds(0, self.cut), pl.ds(self.cut, self.rows - self.cut)
        return [
            self.to_x(self.own.at[k, lax.rem(self.x + i, nx), self.y, top], self.r2h.at[k, i - 1], 6, (k, i - 1), i)
            for i in range(1, nx)
        ] + [
            self.to_y(self.own.at[k, self.x, lax.rem(self.y + j, ny), rest], self.r2l.at[k, j - 1], 8, (k, j - 1), j)
            for j in range(1, ny)
        ]

    def three(self, k):
        return self.copy(
            self.own.at[k, self.x, self.y], self.zin.at[k - 1], 10, (k - 1,),
            self.geo.device(lax.rem(self.z + k, self.geo.nz), self.x, self.y, self.c),
        )

    def begin(self):
        for k in self.order:
            self.cross(k).start()

    def step_one(self, k):
        own = self.own
        self.cross(k).wait()
        for i in range(self.geo.nx):
            for j in range(self.geo.ny):
                mine = self.g[lax.rem(self.z + k, self.geo.nz), i, j, self.c]
                own[k, i, j] = low(wide(mine) + wide(own[k, i, j]))
        for copy in self.one(k):
            copy.start()

    def step_two(self, k):
        own, x, y = self.own, self.x, self.y
        top, rest = pl.ds(0, self.cut), pl.ds(self.cut, self.rows - self.cut)
        for copy in self.one(k):
            copy.wait()
        for i in range(self.geo.nx):
            total = wide(own[k, i, y, top])
            for j in range(1, self.geo.ny):
                total = total + wide(self.r1h[k, j - 1, i])
            own[k, i, y, top] = low(total)
        for j in range(self.geo.ny):
            total = wide(own[k, x, j, rest])
            for i in range(1, self.geo.nx):
                total = total + wide(self.r1l[k, i - 1, j])
            own[k, x, j, rest] = low(total)
        for copy in self.two(k):
            copy.start()

    def step_three(self, k):
        own, x, y = self.own, self.x, self.y
        top, rest = pl.ds(0, self.cut), pl.ds(self.cut, self.rows - self.cut)
        for copy in self.two(k):
            copy.wait()
        upper = wide(own[k, x, y, top])
        for i in range(1, self.geo.nx):
            upper = upper + wide(self.r2h[k, i - 1])
        lower = wide(own[k, x, y, rest])
        for j in range(1, self.geo.ny):
            lower = lower + wide(self.r2l[k, j - 1])
        if k:
            own[k, x, y, top] = low(upper)
            own[k, x, y, rest] = low(lower)
            self.three(k).start()
        else:
            self.total[top] = upper
            self.total[rest] = lower

    def finish(self):
        total = self.total[...]
        for k in range(1, self.geo.nz):
            self.three(k).wait()
            total = total + wide(self.zin[k - 1])
        self.total[...] = total

    def steps(self):
        return [
            [functools.partial(step, k) for k in self.order]
            for step in (self.step_one, self.step_two, self.step_three)
        ]

    @staticmethod
    def buffers(geo, levels, rows, cut, columns, kind):
        vmem = pltpu.VMEM
        nz, nx, ny = geo.nz, geo.nx, geo.ny
        rest = rows - cut
        return [
            vmem((nz, nx, ny, 2, rows, columns), kind),
            vmem((levels, nz, nx, ny, rows, columns), kind),
            vmem((levels, nz, ny - 1, nx, cut, columns), kind),
            vmem((levels, nz, nx - 1, ny, rest, columns), kind),
            vmem((levels, nz, nx - 1, cut, columns), kind),
            vmem((levels, nz, ny - 1, rest, columns), kind),
            vmem((levels, nz - 1, rows, columns), kind),
            vmem((rows, columns), jnp.float32),
        ]

    @staticmethod
    def semaphores(geo, count):
        dma = pltpu.SemaphoreType.DMA
        nz, nx, ny = geo.nz, geo.nx, geo.ny
        return (
            [dma((count, nz))] * 2
            + [dma((count, nz, ny - 1))] * 2
            + [dma((count, nz, nx - 1))] * 2
            + [dma((count, nz, nx - 1))] * 2
            + [dma((count, nz, ny - 1))] * 2
            + [dma((count, nz - 1))] * 2
        )


ROW_ATT_BIAS, ROW_IN_BIAS, ROW_OUT_BIAS, ROW_GAIN, ROW_SHIFT, ROW_FINAL, ROWS = 0, 3, 7, 8, 10, 12, 16


def step_kernel(geo, cuts, half_a, half_f, *refs):
    refs = list(refs)

    def take(count):
        taken = refs[:count]
        del refs[:count]
        return taken

    (stream_in, residue_in, seg, cot, qkv_in, out_in, ff_in_in, ff_out_in, att_in, in_bias_in, out_bias_in, gain_in,
     shift_in, final_gain_in, final_shift_in) = take(15)
    (out, stream_grad, residue_grad, qkv_grad, out_grad, ff_in_grad, ff_out_grad, att_grad, in_bias_grad, out_bias_grad,
     gain_grad, shift_grad, final_gain_grad, final_shift_grad) = take(14)
    (w, par, own_small, xl_next, xn, qs, kv, kt, pt, att, mid, act, slope, n1, n2, i1, i2, bias, segs, dkv, ob, sb, sc,
     rb, rc, small, sbuf, sin) = take(28)
    buffers_a, buffers_f = take(8), take(8)
    gather_sems, scatter_sems = take(12), take(12)
    (load_sem, seg_send, seg_recv, y_send, y_recv, c_send, c_recv, by_send, by_recv, bc_send, bc_recv, s_send,
     s_recv, residue_sem) = take(14)
    assert not refs

    z, xx, y, c = geo.here()
    s = 2 * y + c
    shard = (z * geo.nx + xx) * geo.seq + s
    count = geo.seq
    tokens, features = residue_in.shape
    levels = w.shape[0]
    width = features // geo.shards
    ff_rows = in_bias_in.shape[1]
    head = features // HEADS
    lanes = 2 * head
    pairs = features // lanes
    parts = act.shape[1]
    sibling, across = geo.device(z, xx, y, 1 - c), geo.device(z, xx, 1 - y, c)
    row_in = 4 * width + ROWS
    row_out = row_in + parts * width
    xl = [stream_in] + [xl_next.at[l - 1] for l in range(1, levels)]

    pieces = [
        (
            Gather(geo, w, l, 0, row_in, cuts[0], gather_sems, 2 * l),
            Gather(geo, w, l, row_in, parts * width + ff_rows, cuts[1], gather_sems, 2 * l + 1),
        )
        for l in range(levels)
    ]
    sums = [
        (
            Scatter(geo, *buffers_a, l, half_a, scatter_sems, 2 * l),
            Scatter(geo, *buffers_f, l, half_f, scatter_sems, 2 * l + 1),
        )
        for l in range(levels)
    ]

    def own_loads(l):
        mine = w.at[l, z, xx, y, c]
        pairs_of = [(qkv_in.at[l, :, pl.ds(n * features, features)], n * width, width) for n in range(3)]
        pairs_of.append((out_in.at[l], 3 * width, width))
        for n in range(parts):
            pairs_of.append((ff_in_in.at[l, :, pl.ds(n * features, features)], row_in + n * width, width))
        pairs_of.append((ff_out_in.at[l], row_out, ff_rows))
        return [
            pltpu.make_async_copy(src, mine.at[pl.ds(start, size)], load_sem.at[l, n])
            for n, (src, start, size) in enumerate(pairs_of)
        ]

    for l in range(levels):
        for copy in own_loads(l):
            copy.start()
    lane = lax.broadcasted_iota(jnp.int32, (width, features), 1)
    place = low(jnp.where(lane == shard * width + lax.broadcasted_iota(jnp.int32, (width, features), 0), 1.0, 0.0))
    lane = lax.broadcasted_iota(jnp.int32, (ff_rows, features), 1)
    ff_lane = lax.rem(shard, features // ff_rows) * ff_rows
    ff_place = low(jnp.where(lane == ff_lane + lax.broadcasted_iota(jnp.int32, (ff_rows, features), 0), 1.0, 0.0))
    own_small[...] = jnp.zeros_like(own_small)
    for l in range(levels):
        for n in range(3):
            own_small[l, ROW_ATT_BIAS + n : ROW_ATT_BIAS + n + 1, :] = product(att_in[n, l : l + 1, :], place)
        spread = product(in_bias_in[l : l + 1, :], ff_place)
        for j in range(parts):
            own_small[l, ROW_IN_BIAS + j : ROW_IN_BIAS + j + 1, :] = jnp.where(z == j, spread, 0.0)
        own_small[l, ROW_OUT_BIAS : ROW_OUT_BIAS + 1, :] = product(out_bias_in[l : l + 1, :], place)
        own_small[l, ROW_GAIN : ROW_GAIN + 2, :] = product(gain_in[l], place)
        own_small[l, ROW_SHIFT : ROW_SHIFT + 2, :] = product(shift_in[l], place)
        own_small[l, ROW_FINAL : ROW_FINAL + 1, :] = product(final_gain_in[...], place)
        own_small[l, ROW_FINAL + 1 : ROW_FINAL + 2, :] = product(final_shift_in[...], place)
        w[l, z, xx, y, c, 4 * width : row_in, :] = low(own_small[l])

    segs[0] = jnp.broadcast_to(seg[...], segs.shape[1:])
    greet(
        [geo.device(lax.rem(z + k, geo.nz), xx, y, c) for k in range(1, geo.nz)]
        + [
            geo.device(z, lax.rem(xx + i, geo.nx), lax.rem(y + j, geo.ny), lax.rem(c + k, 2))
            for i in range(geo.nx)
            for j in range(geo.ny)
            for k in range(2)
            if i or j or k
        ]
    )
    line = [(z * geo.nx + xx, lax.rem(s + k, count)) for k in range(1, count)]

    def seg_copy(k):
        return remote(segs.at[0], segs.at[k], seg_send.at[k], seg_recv.at[k], line[k - 1])

    def y_copy(l):
        return remote(xl[l], xn.at[l], y_send.at[l], y_recv.at[l], across)

    def c_copy(l, src):
        return remote(kv.at[l, src], kv.at[l, 1], c_send.at[l], c_recv.at[l], sibling)

    def send_stream(l):
        @pl.when(y == 0)
        def _():
            y_copy(l).start()

    for copy in own_loads(0)[:4]:
        copy.wait()
    nz = geo.nz
    (first_a, first_f), (next_a, next_f) = pieces
    first_a.own()
    for copy in own_loads(0)[4:]:
        copy.wait()
    for k in range(1, count):
        seg_copy(k).start()
    send_stream(0)
    first_f.own()
    for copy in own_loads(1):
        copy.wait()

    waiting = []

    def tick(number):
        for _ in range(min(number, len(waiting))):
            waiting.pop(0)()

    def drain(last):
        while any(task is last for task in waiting):
            tick(1)

    steps = [piece.steps() for piece in (first_a, first_f, next_a, next_f)]
    waiting.extend(steps[0][0] + steps[0][1] + steps[1][0] + steps[0][2] + [next_a.own])
    waiting.extend(steps[1][1] + steps[2][0] + steps[1][2] + [next_f.own])
    waiting.extend(steps[2][1] + steps[3][0] + steps[2][2] + steps[3][1] + steps[3][2])
    last_step = {}
    for piece in (first_a, first_f, next_a, next_f):
        own_steps = [task for task in waiting if task.__class__ is functools.partial and task.func.__self__ is piece]
        last_step[piece] = own_steps[-1]

    @pl.when(y == 0)
    def _():
        for l in range(levels):
            xn[l] = jnp.zeros_like(xn[l])

    @pl.when(s == 0)
    def _():
        for l in range(levels):
            kv[l, 1] = jnp.zeros_like(kv[l, 1])

    for k in range(1, count):
        seg_copy(k).wait()
    query_seg = segs[0, 0:1, :]
    query_pos = s * tokens + lax.broadcasted_iota(jnp.int32, (tokens, tokens), 1)
    for b in range(3):
        block = lax.rem(s + count - b, count)
        key_seg = jnp.transpose(jnp.broadcast_to(wide(segs[b, 0:1, :]), (128, tokens)))[:, 0:1]
        key_pos = block * tokens + lax.broadcasted_iota(jnp.int32, (tokens, tokens), 0)
        allowed = (key_seg == wide(query_seg)) & (key_pos <= query_pos)
        bias[b] = jnp.where(allowed, 0.0, masked_value)
    for l in range(levels):
        small[l] = jnp.zeros_like(small[l])

    def weight(l, start):
        return w[l, :, :, :, :, pl.ds(start, width), :].reshape(features, features)

    def out_weight(l, j):
        return w[l, j, :, :, :, pl.ds(row_out, ff_rows), :].reshape(features, features)

    g_a, g_f = buffers_a[0], buffers_f[0]

    def keep(ref, start, value):
        ref[:, :, :, :, pl.ds(start, width), :] = low(value).reshape(nz, geo.nx, geo.ny, 2, width, features)

    def keep_out(j, value):
        g_f[j, :, :, :, pl.ds(parts * width, ff_rows), :] = low(value).reshape(geo.nx, geo.ny, 2, ff_rows, features)

    def row(l, index):
        return par[l, index : index + 1, :]

    pair_lane = lax.broadcasted_iota(jnp.int32, (1, lanes), 1)

    def one_head(value, side):
        return jnp.where((pair_lane < head) == (side == 0), value, jnp.zeros_like(value))

    def ready(piece):
        drain(last_step[piece])
        piece.arrive()

    x, r = stream_grad, out
    residue_load = pltpu.make_async_copy(residue_in, r, residue_sem)
    residue_load.start()

    def forward(l):
        ready(pieces[l][0])
        par[l] = jnp.sum(
            wide(w[l, :, :, :, :, pl.ds(4 * width, ROWS), :]).reshape(geo.shards, ROWS, features), axis=0
        )
        xv = xl[l][...]
        keys = product(xv, weight(l, width))
        values = product(xv, weight(l, 2 * width)) + row(l, ROW_ATT_BIAS + 1)
        kv[l, 0, :, 0:features] = low(keys)
        kv[l, 0, :, features:] = low(values)

        @pl.when(c == 0)
        def _():
            c_copy(l, 0).start()

        tick(2)
        queries = low(product(xv, weight(l, 0)) + row(l, ROW_ATT_BIAS))
        qs[l] = queries * (1.0 / math.sqrt(head))

        @pl.when(y == 1)
        def _():
            y_copy(l).wait_recv()

        xv = xn[l]
        keys = product(xv, weight(l, width))
        values = product(xv, weight(l, 2 * width)) + row(l, ROW_ATT_BIAS + 1)
        kv[l, 2, :, 0:features] = low(keys)
        kv[l, 2, :, features:] = low(values)

        @pl.when((y == 1) & (c == 1))
        def _():
            c_copy(l, 2).start()

        tick(2)

        @pl.when((y == 1) | (c == 1))
        def _():
            c_copy(l, 0).wait_recv()

        for b in range(3):
            kt[:, b * tokens : (b + 1) * tokens] = jnp.transpose(kv[l, b, :, features:])

        def attend(p, carry):
            at = pl.ds(pl.multiple_of(p * lanes, lanes), lanes)
            queries = qs[l, :, at]
            keys = kv[l, :, :, at].reshape(3 * tokens, lanes)
            for side in range(2):
                scores = product_rows(keys, one_head(queries, side)) + bias[...].reshape(3 * tokens, tokens)
                terms = jnp.exp(scores - jnp.max(scores, axis=0, keepdims=True))
                probs = low(terms * (1.0 / jnp.sum(terms, axis=0, keepdims=True)))
                pt[l, 2 * p + side] = probs
                rows = pl.ds(pl.multiple_of(p * lanes + side * head, head), head)
                ob[rows, :] = product(kt[rows, :], probs)
            return carry

        for half in range(2):
            lax.fori_loop(half * pairs // 2, (half + 1) * pairs // 2, attend, 0)
            tick(5)
        att[l] = low(jnp.transpose(ob[...]))
        branch = product(att[l], weight(l, 3 * width)) + row(l, ROW_ATT_BIAS + 2)
        normal, inverse = normalize((wide(stream_in[...]) if l == 0 else x[...]) + branch)
        n1[l] = normal
        i1[l] = inverse
        middle = normal * row(l, ROW_GAIN) + row(l, ROW_SHIFT)
        mid[l] = low(middle)
        x[...] = middle
        if l == 0:
            residue_load.wait()
        r[...] = r[...] + branch
        ready(pieces[l][1])
        total = jnp.broadcast_to(row(l, ROW_OUT_BIAS), (tokens, features))
        for j in range(parts):
            hidden = product(mid[l], weight(l, row_in + j * width)) + row(l, ROW_IN_BIAS + j)
            active, rise = gelu_pair(hidden)
            act[l, j] = low(active)
            slope[l, j] = low(rise)
            total = total + product(act[l, j], out_weight(l, j))
            tick(2)
        r[...] = r[...] + total
        normal, inverse = normalize(x[...] + total)
        n2[l] = normal
        i2[l] = inverse
        next_x = normal * row(l, ROW_GAIN + 1) + row(l, ROW_SHIFT + 1)
        x[...] = next_x
        if l + 1 < levels:
            xl[l + 1][...] = low(next_x)
            send_stream(l + 1)

    def note(l, index, value):
        small[l, index : index + 1, :] = value

    def by_copy(l):
        return remote(sc.at[l], rc.at[l], by_send.at[l], by_recv.at[l], across)

    def bc_copy(l):
        return remote(sb.at[l], rb.at[l], bc_send.at[l], bc_recv.at[l], sibling)

    gx = stream_grad
    block_lanes = features // nz
    last = levels - 1
    sum_ones, stores, ahead = {}, [], 3

    def queue_sum(scatter, store, l):
        one, two, three = scatter.steps()
        sum_ones[scatter] = one[-1]
        order = [
            stage[n - lag]
            for n in range(len(one) + 3)
            for stage, lag in ((one, 0), (two, 2), (three, 3))
            if 0 <= n - lag < len(one)
        ]
        left = waiting[:]
        waiting.clear()
        for n in range(ahead):
            waiting.append(order[n])
            waiting.extend(left[n : n + 1])
        waiting.extend(left[ahead:] + order[ahead:])
        waiting.extend(stores)
        stores[:] = [functools.partial(store, l)]

    def backward(l):
        sum_a, sum_f = sums[l]
        grad = gx[...]
        note(l, ROW_GAIN + 1, column_sums(grad * n2[l]))
        note(l, ROW_SHIFT + 1, column_sums(grad))
        g2 = normalize_back(grad, n2[l], i2[l], row(l, ROW_GAIN + 1))
        d_ff = low(g2 + residue_grad[...])
        if l < last:
            drain(sum_ones[sums[l + 1][1]])
        note(l, ROW_OUT_BIAS, column_sums(wide(d_ff)))
        total = g2
        for j in range(parts):
            keep_out(j, product_tokens(act[l, j], d_ff))
            d_hidden = low(product_rows(d_ff, out_weight(l, j)) * wide(slope[l, j]))
            sums_in = column_sums(wide(d_hidden))
            for q in range(parts):
                block = sums_in[:, q * block_lanes : (q + 1) * block_lanes]
                small[l, ROW_IN_BIAS + q : ROW_IN_BIAS + q + 1, j * block_lanes : (j + 1) * block_lanes] = block
            keep(g_f, j * width, product_tokens(mid[l], d_hidden))
            total = total + product_rows(d_hidden, weight(l, row_in + j * width))
            tick(2)
        sum_f.begin()
        note(l, ROW_GAIN, column_sums(total * n1[l]))
        note(l, ROW_SHIFT, column_sums(total))
        g1 = normalize_back(total, n1[l], i1[l], row(l, ROW_GAIN))
        gx[...] = g1
        d_att = low(g1 + residue_grad[...])
        note(l, ROW_ATT_BIAS + 2, column_sums(wide(d_att)))
        if l < last:
            drain(sum_ones[sums[l + 1][0]])
        keep(g_a, 3 * width, product_tokens(att[l], d_att))
        att[l] = low(product_rows(d_att, weight(l, 3 * width)))
        queue_sum(sum_f, store_f, l)
        tick(6)
        for b in range(3):
            kt[:, b * tokens : (b + 1) * tokens] = jnp.transpose(kv[l, b, :, 0:features])

        def attend(p, carry):
            start = pl.multiple_of(p * lanes, lanes)
            at, at_values = pl.ds(start, lanes), pl.ds(start + features, lanes)
            queries, d_out = qs[l, :, at], att[l, :, at]
            values = kv[l, :, :, at_values].reshape(3 * tokens, lanes)
            d_keys = jnp.zeros((3 * tokens, lanes), jnp.float32)
            d_values = jnp.zeros((3 * tokens, lanes), jnp.float32)
            for side in range(2):
                own = one_head(d_out, side)
                probs = pt[l, 2 * p + side]
                terms = product_rows(values, own)
                weighted = terms * wide(probs)
                d_scores = low(weighted - wide(probs) * jnp.sum(weighted, axis=0, keepdims=True))
                d_values = d_values + product(probs, own)
                d_keys = d_keys + product(d_scores, one_head(queries, side))
                rows = pl.ds(pl.multiple_of(p * lanes + side * head, head), head)
                ob[rows, :] = product(kt[rows, :], d_scores)
            for where, value in ((at, d_keys), (at_values, d_values)):
                dkv[0, :, where] = value[:tokens]
                sb[l, :, where] = low(value[tokens : 2 * tokens])
                dkv[1, :, where] = value[2 * tokens :]
            return carry

        for half in range(2):
            lax.fori_loop(half * pairs // 2, (half + 1) * pairs // 2, attend, 0)
            tick(2)

        @pl.when((c == 1) | (y == 1))
        def _():
            bc_copy(l).start()

        @pl.when((y == 1) & (c == 1))
        def _():
            bc_copy(l).wait_recv()
            dkv[1] = dkv[1] + wide(rb[l])

        far_keys, far_values = low(dkv[1, :, 0:features]), low(dkv[1, :, features:])

        @pl.when(y == 1)
        def _():
            sc[l] = low(product_rows(far_keys, weight(l, width)) + product_rows(far_values, weight(l, 2 * width)))
            by_copy(l).start()

        tick(2)
        d_queries = low(jnp.transpose(ob[...]) * (1.0 / math.sqrt(head)))
        keep(g_a, 0, product_tokens(xl[l][...], d_queries))
        note(l, ROW_ATT_BIAS, column_sums(wide(d_queries)))

        @pl.when(c == 0)
        def _():
            bc_copy(l).wait_recv()
            dkv[0] = dkv[0] + wide(rb[l])

        d_keys, d_values = low(dkv[0, :, 0:features]), low(dkv[0, :, features:])
        keep(g_a, width, product_tokens(xl[l][...], d_keys) + product_tokens(xn[l], far_keys))
        keep(g_a, 2 * width, product_tokens(xl[l][...], d_values) + product_tokens(xn[l], far_values))
        note(l, ROW_ATT_BIAS + 1, column_sums(wide(d_values)) + column_sums(wide(far_values)))
        sum_a.begin()
        tick(2)
        gx[...] = (
            gx[...]
            + product_rows(d_queries, weight(l, 0))
            + product_rows(d_keys, weight(l, width))
            + product_rows(d_values, weight(l, 2 * width))
        )
        queue_sum(sum_a, store_a, l)
        tick(2)

        @pl.when(y == 0)
        def _():
            by_copy(l).wait_recv()
            gx[...] = gx[...] + wide(rc[l])

    def store_f(l):
        sum_f = sums[l][1]
        sum_f.finish()
        for n in range(parts):
            ff_in_grad[l, :, n * features : (n + 1) * features] = sum_f.total[n * width : (n + 1) * width]
        ff_out_grad[l] = sum_f.total[parts * width :]

    def store_a(l):
        sum_a = sums[l][0]
        sum_a.finish()
        for n in range(3):
            qkv_grad[l, :, n * features : (n + 1) * features] = sum_a.total[n * width : (n + 1) * width]
        out_grad[l] = sum_a.total[3 * width :]

    for l in range(levels):
        forward(l)
    normal, inverse = normalize(r[...])
    gain = row(last, ROW_FINAL)
    out[...] = x[...] + normal * gain + row(last, ROW_FINAL + 1)
    grad = cot[...]
    note(last, ROW_FINAL, column_sums(grad * normal))
    note(last, ROW_FINAL + 1, column_sums(grad))
    residue_grad[...] = normalize_back(grad, normal, inverse, gain)
    gx[...] = grad
    for l in reversed(range(levels)):
        backward(l)

    z_peers = [geo.device(lax.rem(z + k, nz), xx, y, c) for k in range(1, nz)]
    plane = [
        geo.device(z, lax.rem(xx + i, geo.nx), lax.rem(y + j, geo.ny), lax.rem(c + k, 2))
        for i in range(geo.nx)
        for j in range(geo.ny)
        for k in range(2)
    ][1:]

    def z_small(k):
        return remote(
            sbuf.at[lax.rem(z + k, nz)], sin.at[k - 1], s_send.at[k - 1], s_recv.at[k - 1], z_peers[k - 1]
        )

    def plane_small(n):
        m = nz - 1 + n
        return remote(sbuf.at[nz], sin.at[m], s_send.at[m], s_recv.at[m], plane[n])

    for k in range(nz):
        sbuf[k] = small[:, :, k * block_lanes : (k + 1) * block_lanes].reshape(levels * ROWS, block_lanes)
    for k in range(1, nz):
        z_small(k).start()
    waiting.extend(stores)
    while len(waiting) > 2 * nz + 1:
        tick(1)
    total = sbuf[z]
    for k in range(1, nz):
        z_small(k).wait()
        total = total + sin[k - 1]
    sbuf[nz] = total
    for n in range(len(plane)):
        plane_small(n).start()
    tick(nz)
    total = sbuf[nz]
    for n in range(len(plane)):
        plane_small(n).wait()
        total = total + sin[nz - 1 + n]
    exact = functools.partial(jnp.dot, preferred_element_type=jnp.float32, precision=lax.Precision.HIGHEST)

    def chosen(lane_count, first, size):
        lane = lax.broadcasted_iota(jnp.int32, (lane_count, size), 0)
        return jnp.where(lane == first + lax.broadcasted_iota(jnp.int32, (lane_count, size), 1), 1.0, 0.0)

    mine = exact(total, chosen(block_lanes, lax.rem(shard, geo.shards // nz) * width, width))
    in_block = exact(total, chosen(block_lanes, lax.rem(ff_lane, block_lanes), ff_rows))
    part = lax.broadcasted_iota(jnp.int32, (ROWS, 1), 0)
    for l in range(levels):
        own = mine[l * ROWS : (l + 1) * ROWS]
        for n in range(3):
            att_grad[n, l : l + 1, :] = own[ROW_ATT_BIAS + n : ROW_ATT_BIAS + n + 1]
        in_rows = in_block[l * ROWS : (l + 1) * ROWS]
        in_bias_grad[l : l + 1, :] = column_sums(
            jnp.where(part == ROW_IN_BIAS + lax.div(ff_lane, block_lanes), in_rows, 0.0)
        )
        out_bias_grad[l : l + 1, :] = own[ROW_OUT_BIAS : ROW_OUT_BIAS + 1]
        gain_grad[l] = own[ROW_GAIN : ROW_GAIN + 2]
        shift_grad[l] = own[ROW_SHIFT : ROW_SHIFT + 2]
    final_gain_grad[...] = own[ROW_FINAL : ROW_FINAL + 1]
    final_shift_grad[...] = own[ROW_FINAL + 1 : ROW_FINAL + 2]
    while waiting:
        tick(1)

    for l in range(levels):
        for piece in pieces[l]:
            piece.finish()

        @pl.when(y == 0)
        def _(l=l):
            y_copy(l).wait_send()

        @pl.when((y == 1) | (c == 0))
        def _(l=l):
            c_copy(l, 0).wait_send()

        @pl.when((c == 1) | (y == 1))
        def _(l=l):
            bc_copy(l).wait_send()

        @pl.when(y == 1)
        def _(l=l):
            by_copy(l).wait_send()


def run_step(geo, stream_in, residue_in, seg, cot, shards):
    tokens, features = residue_in.shape
    levels, width, qkv_columns = shards[0].shape
    parts = shards[2].shape[2] // features
    ff_rows = shards[3].shape[1]
    rows_a, rows_f = 4 * width, parts * width + ff_rows
    shape = (geo.nz, geo.nx, geo.ny, 2)
    dma, vmem = pltpu.SemaphoreType.DMA, pltpu.VMEM
    wide_kind, kind = jnp.float32, jnp.bfloat16
    whole = pl.BlockSpec(memory_space=pltpu.VMEM)
    away = pl.BlockSpec(memory_space=pl.ANY)
    row = (tokens, features)
    half_a, half_f = 2 * width, 4 * width
    cuts = (2 * width, 3 * width)
    others = geo.nz - 1 + 2 * geo.nx * geo.ny - 1
    outs = [row, row, row] + [member.shape for member in shards]
    scratch = [
        vmem((levels,) + shape + (rows_a + ROWS + rows_f, features), kind),
        vmem((levels, ROWS, features), wide_kind),
        vmem((levels, ROWS, features), wide_kind),
        vmem((levels - 1,) + row, kind),
        vmem((levels,) + row, kind),
        vmem((levels,) + row, kind),
        vmem((levels, 3, tokens, 2 * features), kind),
        vmem((features, 3 * tokens), kind),
        vmem((levels, HEADS, 3 * tokens, tokens), kind),
        vmem((levels,) + row, kind),
        vmem((levels,) + row, kind),
        vmem((levels, parts) + row, kind),
        vmem((levels, parts) + row, kind),
        vmem((levels,) + row, wide_kind),
        vmem((levels,) + row, wide_kind),
        vmem((levels, tokens, 1), wide_kind),
        vmem((levels, tokens, 1), wide_kind),
        vmem((3, tokens, tokens), wide_kind),
        vmem((geo.seq, 8, tokens), jnp.int32),
        vmem((2, tokens, 2 * features), wide_kind),
        vmem((features, tokens), wide_kind),
        vmem((levels, tokens, 2 * features), kind),
        vmem((levels,) + row, kind),
        vmem((levels, tokens, 2 * features), kind),
        vmem((levels,) + row, kind),
        vmem((levels, ROWS, features), wide_kind),
        vmem((geo.nz + 1, levels * ROWS, features // geo.nz), wide_kind),
        vmem((others, levels * ROWS, features // geo.nz), wide_kind),
    ]
    scratch += Scatter.buffers(geo, levels, rows_a, half_a, features, kind)
    scratch += Scatter.buffers(geo, levels, rows_f, half_f, features, kind)
    scratch += Gather.semaphores(geo, 2 * levels) + Scatter.semaphores(geo, 2 * levels)
    scratch += [dma((levels, 5 + parts))] + [dma((geo.seq,))] * 2 + [dma((levels,))] * 8 + [dma((others,))] * 2 + [dma(())]
    return pl.pallas_call(
        functools.partial(step_kernel, geo, cuts, half_a, half_f),
        out_shape=tuple(jax.ShapeDtypeStruct(shape_of, wide_kind) for shape_of in outs),
        in_specs=[whole, away, whole, whole] + [away] * 4 + [whole] * 7,
        out_specs=(whole,) * len(outs),
        scratch_shapes=scratch,
        compiler_params=pltpu.CompilerParams(
            collective_id=0, has_side_effects=True, vmem_limit_bytes=64 << 20
        ),
        name="run_step",
    )(stream_in, residue_in, seg, cot, *shards)


def settle_kernel(count, *refs):
    sources, targets, held, (loads, stores) = refs[:count], refs[count : 2 * count], refs[2 * count : -2], refs[-2:]
    into = [pltpu.make_async_copy(src, buf, loads.at[n]) for n, (src, buf) in enumerate(zip(sources, held))]
    away = [pltpu.make_async_copy(buf, dst, stores.at[n]) for n, (buf, dst) in enumerate(zip(held, targets))]
    for copy in into:
        copy.start()
    for load, store in zip(into, away):
        load.wait()
        store.start()
    for copy in away:
        copy.wait()


def settle(values):
    count = len(values)
    away = pl.BlockSpec(memory_space=pl.ANY)
    return pl.pallas_call(
        functools.partial(settle_kernel, count),
        out_shape=tuple(jax.ShapeDtypeStruct(value.shape, value.dtype) for value in values),
        in_specs=[away] * count,
        out_specs=(away,) * count,
        scratch_shapes=[pltpu.VMEM(value.shape, value.dtype) for value in values]
        + [pltpu.SemaphoreType.DMA((count,))] * 2,
        name="settle",
    )(*values)


def gather_plain(shards, number):
    gathered = [
        lax.all_gather(shards[member][number], ("dp", "seq"), axis=axis, tiled=True)
        for member, axis in enumerate((0, 0, 0, 0, 1, 0, 0, 1, 1))
    ]
    return tuple(gathered) + tuple(
        lax.all_gather(shards[member], ("dp", "seq"), axis=0, tiled=True) for member in (9, 10)
    )


def body_plain(geo, *args):
    stream_in, residue_in, segments, out_cot = args[:4]
    shards = args[4:]
    levels, width, _ = shards[1].shape
    ff_width = shards[3].shape[1]
    stream = stream_in[0].astype(jnp.float32)
    residue = residue_in[0]
    cotangent = out_cot[0]
    tokens = stream.shape[0]
    query_seg = segments[0]
    whole_seg = lax.all_gather(query_seg, "seq", axis=0, tiled=True)
    seq_index = lax.axis_index("seq")
    query_pos = seq_index * tokens + jnp.arange(tokens, dtype=jnp.int32)
    weights = [gather_plain(shards, number) for number in range(levels)]
    states = []
    for number in range(levels):
        stream, residue, state = layer_forward(stream, residue, weights[number], query_pos, query_seg, whole_seg)
        states.append(state)
    final_norm, pull_final = jax.vjp(
        layer_norm,
        residue,
        weights[-1][9].astype(jnp.float32),
        weights[-1][10].astype(jnp.float32),
    )
    output = stream + final_norm
    grad_residue, final_gain_grad, final_shift_grad = pull_final(cotangent)
    grad_stream = cotangent
    grads = [None] * levels
    for number in reversed(range(levels)):
        grad_stream, grads[number] = layer_backward(
            states[number], weights[number], grad_stream, grad_residue, query_pos, query_seg
        )
    summed = [
        jnp.stack(
            [
                lax.psum_scatter(grads[number][member], ("dp", "seq"), scatter_dimension=axis, tiled=True)
                for number in range(levels)
            ]
        )
        for member, axis in enumerate((0, 0, 0, 0, 1, 0, 0, 1, 1))
    ] + [
        lax.psum_scatter(final_gain_grad, ("dp", "seq"), scatter_dimension=0, tiled=True),
        lax.psum_scatter(final_shift_grad, ("dp", "seq"), scatter_dimension=0, tiled=True),
    ]
    return (output[None], grad_stream[None], grad_residue[None]) + tuple(summed)


def body(geo, *args):
    stream_in, residue_in, segments, out_cot = args[:4]
    shards = list(args[4:])
    shards[4] = shards[4].transpose(1, 0, 2)
    shards[-2:] = [shards[-2][None], shards[-1][None]]
    results = list(settle(run_step(geo, stream_in[0], residue_in[0], segments, out_cot[0], shards)))
    results[7] = results[7].transpose(1, 0, 2)
    return tuple(value[None] for value in results[:3]) + tuple(results[3:-2]) + (results[-2][0], results[-1][0])


def solution(mesh):
    geo = Geometry(mesh)
    chosen = body if geo.seq == 4 and geo.nz == 4 else body_plain
    return jax.shard_map(
        functools.partial(chosen, geo),
        mesh=mesh,
        in_specs=(
            P("dp", "seq", None),
            P("dp", "seq", None),
            P("dp", "seq"),
            P("dp", "seq", None),
            P(None, ("dp", "seq"), None),
            P(None, ("dp", "seq"), None),
            P(None, ("dp", "seq"), None),
            P(None, ("dp", "seq"), None),
            P(None, None, ("dp", "seq")),
            P(None, ("dp", "seq")),
            P(None, ("dp", "seq")),
            P(None, None, ("dp", "seq")),
            P(None, None, ("dp", "seq")),
            P(("dp", "seq")),
            P(("dp", "seq")),
        ),
        out_specs=(
            P("dp", "seq", None),
            P("dp", "seq", None),
            P("dp", "seq", None),
            P(None, ("dp", "seq"), None),
            P(None, ("dp", "seq"), None),
            P(None, ("dp", "seq"), None),
            P(None, ("dp", "seq"), None),
            P(None, None, ("dp", "seq")),
            P(None, ("dp", "seq")),
            P(None, ("dp", "seq")),
            P(None, None, ("dp", "seq")),
            P(None, None, ("dp", "seq")),
            P(("dp", "seq")),
            P(("dp", "seq")),
        ),
        check_vma=False,
    )
```

```python
import functools
import itertools
import math

import jax
import jax.numpy as jnp
from jax import lax
from jax.experimental import pallas as pl
from jax.experimental.pallas import tpu as pltpu
from jax.sharding import PartitionSpec as P

HEADS = 8
MESH = pl.DeviceIdType.MESH


class Geometry:
    def __init__(self, mesh):
        self.dp, self.seq = mesh.shape["dp"], mesh.shape["seq"]
        self.ny = self.seq // 2
        self.nx = self.ny
        self.nz = self.dp // self.nx
        self.shards = self.dp * self.seq

    def here(self):
        dp, seq = lax.axis_index("dp"), lax.axis_index("seq")
        return lax.div(dp, self.nx), lax.rem(dp, self.nx), lax.div(seq, 2), lax.rem(seq, 2)

    def device(self, z, x, y, c):
        return (z * self.nx + x, y * 2 + c)

    def peers(self):
        z, x, y, c = self.here()
        found = [self.device(lax.rem(z + k, self.nz), x, y, c) for k in range(1, self.nz)]
        found += [self.device(z, lax.rem(x + k, self.nx), y, c) for k in range(1, self.nx)]
        found += [self.device(z, x, lax.rem(y + k, self.ny), c) for k in range(1, self.ny)]
        return found + [self.device(z, x, y, 1 - c)]


def greet(devices):
    barrier = pltpu.get_barrier_semaphore()
    for device in devices:
        pl.semaphore_signal(barrier, inc=1, device_id=device, device_id_type=MESH)
    pl.semaphore_wait(barrier, len(devices))


def remote(src, dst, send_sem, recv_sem, device):
    return pltpu.make_async_remote_copy(
        src_ref=src,
        dst_ref=dst,
        send_sem=send_sem,
        recv_sem=recv_sem,
        device_id=device,
        device_id_type=MESH,
    )


epsilon = 1e-05
masked_value = -1e30


def smooth_gate(values):
    return jax.nn.gelu(values, approximate=True)


def layer_norm(values, norm_gain, norm_shift):
    average = jnp.mean(values, axis=-1, keepdims=True)
    centred = values - average
    variance = jnp.mean(centred * centred, axis=-1, keepdims=True)
    return centred * lax.rsqrt(variance + epsilon) * norm_gain + norm_shift


def keep_state(carried):
    return carried


def allowed_pairs(query_pos, query_seg, key_pos, key_seg):
    return (query_seg[:, None] == key_seg[None, :]) & (key_pos[None, :] <= query_pos[:, None])


def block_needed(query_pos, query_seg, key_pos, key_seg):
    return (key_pos[0] <= query_pos[-1]) & (key_seg[-1] >= query_seg[0])


def key_blocks(keys_values, key_seg):
    length = keys_values.shape[0]
    features = keys_values.shape[1] // 2
    head_size = features // HEADS
    block_rows = math.gcd(length, 512)
    block_count = length // block_rows
    split_kv = keys_values.reshape(block_count, block_rows, 2, HEADS, head_size)
    key_pos = jnp.arange(length, dtype=jnp.int32).reshape(block_count, block_rows)
    return (split_kv[:, :, 0], split_kv[:, :, 1], key_pos, key_seg.reshape(block_count, block_rows))


def block_scores(queries3, key_block, query_pos, query_seg, key_pos, key_seg):
    scaling = 1.0 / math.sqrt(queries3.shape[-1])
    raw_scores = (
        jnp.einsum("qhd,khd->hqk", queries3, key_block, preferred_element_type=jnp.float32)
        * scaling
    )
    return (raw_scores, allowed_pairs(query_pos, query_seg, key_pos, key_seg)[None])


def attention_forward(queries3, blocks, query_pos, query_seg):
    tokens, head_count, head_size = queries3.shape

    def statistics(carried, block_items):
        key_block, value_block, key_pos, key_seg = block_items

        def statistics_compute(running):
            run_max, run_sum = running
            raw_scores, allowed = block_scores(
                queries3, key_block, query_pos, query_seg, key_pos, key_seg
            )
            new_max = jnp.maximum(
                run_max, jnp.max(jnp.where(allowed, raw_scores, masked_value), axis=-1)
            )
            exp_terms = jnp.exp(jnp.where(allowed, raw_scores - new_max[..., None], masked_value))
            return (new_max, run_sum * jnp.exp(run_max - new_max) + jnp.sum(exp_terms, axis=-1))

        needed = block_needed(query_pos, query_seg, key_pos, key_seg)
        return (lax.cond(needed, statistics_compute, keep_state, carried), None)

    initial = (
        jnp.full((head_count, tokens), masked_value, jnp.float32),
        jnp.zeros((head_count, tokens), jnp.float32),
    )
    (run_max, run_sum), unused = lax.scan(statistics, initial, blocks)
    log_total = run_max + jnp.log(run_sum)

    def accumulate(carried, block_items):
        key_block, value_block, key_pos, key_seg = block_items

        def accumulate_compute(running):
            raw_scores, allowed = block_scores(
                queries3, key_block, query_pos, query_seg, key_pos, key_seg
            )
            weights = jnp.exp(jnp.where(allowed, raw_scores - log_total[..., None], masked_value))
            weights = weights.astype(jnp.bfloat16)
            return running + jnp.einsum(
                "hqk,khd->qhd", weights, value_block, preferred_element_type=jnp.float32
            )

        needed = block_needed(query_pos, query_seg, key_pos, key_seg)
        return (lax.cond(needed, accumulate_compute, keep_state, carried), None)

    mixed_heads, unused = lax.scan(
        accumulate, jnp.zeros((tokens, head_count, head_size), jnp.float32), blocks
    )
    return (mixed_heads, log_total)


def attention_backward(queries3, blocks, query_pos, query_seg, log_total, mixed_heads, grad_heads):
    tokens, head_count, head_size = queries3.shape
    scaling = 1.0 / math.sqrt(head_size)
    row_dots = jnp.sum(mixed_heads * grad_heads.astype(jnp.float32), axis=-1).T
    block_rows = blocks[0].shape[1]
    block_count = blocks[0].shape[0]

    def backward_step(grad_queries, block_items):
        key_block, value_block, key_pos, key_seg = block_items

        def backward_compute(running):
            raw_scores, allowed = block_scores(
                queries3, key_block, query_pos, query_seg, key_pos, key_seg
            )
            prob_values = jnp.exp(
                jnp.where(allowed, raw_scores - log_total[..., None], masked_value)
            )
            grad_values = jnp.einsum(
                "hqk,qhd->khd",
                prob_values.astype(jnp.bfloat16),
                grad_heads,
                preferred_element_type=jnp.float32,
            )
            grad_probs = jnp.einsum(
                "qhd,khd->hqk", grad_heads, value_block, preferred_element_type=jnp.float32
            )
            grad_scores = (prob_values * (grad_probs - row_dots[..., None])).astype(jnp.bfloat16)
            running = (
                running
                + jnp.einsum(
                    "hqk,khd->qhd", grad_scores, key_block, preferred_element_type=jnp.float32
                )
                * scaling
            )
            grad_keys = (
                jnp.einsum(
                    "hqk,qhd->khd", grad_scores, queries3, preferred_element_type=jnp.float32
                )
                * scaling
            )
            return (running, grad_keys, grad_values)

        def skip_block(running):
            empty_rows = jnp.zeros((block_rows, head_count, head_size), jnp.float32)
            return (running, empty_rows, empty_rows)

        needed = block_needed(query_pos, query_seg, key_pos, key_seg)
        grad_queries, grad_keys, grad_values = lax.cond(
            needed, backward_compute, skip_block, grad_queries
        )
        return (grad_queries, (grad_keys, grad_values))

    initial = jnp.zeros((tokens, head_count, head_size), jnp.float32)
    grad_queries, (grad_keys, grad_values) = lax.scan(backward_step, initial, blocks)
    length = block_count * block_rows
    return (
        grad_queries.reshape(tokens, head_count * head_size),
        grad_keys.reshape(length, head_count * head_size),
        grad_values.reshape(length, head_count * head_size),
    )


def layer_forward(stream, residue, weights, query_pos, query_seg, key_seg):
    (
        qkv_weight,
        out_weight,
        ff_in_weight,
        ff_out_weight,
        att_bias,
        ff_in_bias,
        ff_out_bias,
        norm_gain,
        norm_shift,
    ) = weights[:9]
    tokens, features = stream.shape
    stream_low = stream.astype(jnp.bfloat16)
    bias_row = jnp.concatenate([att_bias[0], jnp.zeros_like(att_bias[0]), att_bias[1]]).astype(
        jnp.float32
    )
    joined = (
        jnp.dot(stream_low, qkv_weight, preferred_element_type=jnp.float32) + bias_row
    ).astype(jnp.bfloat16)
    queries3 = joined[:, :features].reshape(tokens, HEADS, features // HEADS)
    keys_values = lax.all_gather(joined[:, features:], "seq", axis=0, tiled=True)
    blocks = key_blocks(keys_values, key_seg)
    mixed_heads, log_total = attention_forward(queries3, blocks, query_pos, query_seg)
    attended = mixed_heads.reshape(tokens, features).astype(jnp.bfloat16)
    branch_att = jnp.dot(attended, out_weight, preferred_element_type=jnp.float32) + att_bias[
        2
    ].astype(jnp.float32)
    middle, pull_first = jax.vjp(
        layer_norm,
        stream + branch_att,
        norm_gain[0].astype(jnp.float32),
        norm_shift[0].astype(jnp.float32),
    )
    residue_mid = residue + branch_att
    middle_low = middle.astype(jnp.bfloat16)
    hidden = jnp.dot(
        middle_low, ff_in_weight, preferred_element_type=jnp.float32
    ) + ff_in_bias.astype(jnp.float32)
    active = smooth_gate(hidden).astype(jnp.bfloat16)
    branch_ff = jnp.dot(
        active, ff_out_weight, preferred_element_type=jnp.float32
    ) + ff_out_bias.astype(jnp.float32)
    stream_next, pull_second = jax.vjp(
        layer_norm,
        middle + branch_ff,
        norm_gain[1].astype(jnp.float32),
        norm_shift[1].astype(jnp.float32),
    )
    saved_state = (
        stream_low,
        queries3,
        blocks,
        mixed_heads,
        log_total,
        attended,
        pull_first,
        middle_low,
        hidden,
        active,
        pull_second,
    )
    return (stream_next, residue_mid + branch_ff, saved_state)


def layer_backward(saved_state, weights, grad_stream, grad_residue, query_pos, query_seg):
    (
        stream_low,
        queries3,
        blocks,
        mixed_heads,
        log_total,
        attended,
        pull_first,
        middle_low,
        hidden,
        active,
        pull_second,
    ) = saved_state
    qkv_weight, out_weight, ff_in_weight, ff_out_weight = weights[:4]
    grad_second, gain_second, shift_second = pull_second(grad_stream)
    grad_ff = (grad_second + grad_residue).astype(jnp.bfloat16)
    grad_ff_out = jnp.einsum("tf,td->fd", active, grad_ff, preferred_element_type=jnp.float32)
    bias_ff_out = jnp.sum(grad_ff.astype(jnp.float32), axis=0)
    grad_active = jnp.einsum(
        "td,fd->tf", grad_ff, ff_out_weight, preferred_element_type=jnp.float32
    )
    unused_gate, pull_gate = jax.vjp(smooth_gate, hidden)
    grad_hidden = pull_gate(grad_active)[0].astype(jnp.bfloat16)
    grad_ff_in = jnp.einsum(
        "td,tf->df", middle_low, grad_hidden, preferred_element_type=jnp.float32
    )
    bias_ff_in = jnp.sum(grad_hidden.astype(jnp.float32), axis=0)
    grad_middle = grad_second + jnp.einsum(
        "tf,df->td", grad_hidden, ff_in_weight, preferred_element_type=jnp.float32
    )
    grad_first, gain_first, shift_first = pull_first(grad_middle)
    grad_att = (grad_first + grad_residue).astype(jnp.bfloat16)
    grad_out = jnp.einsum("te,td->ed", attended, grad_att, preferred_element_type=jnp.float32)
    bias_att_out = jnp.sum(grad_att.astype(jnp.float32), axis=0)
    grad_attended = jnp.einsum(
        "td,ed->te", grad_att, out_weight, preferred_element_type=jnp.float32
    )
    grad_attended = grad_attended.astype(jnp.bfloat16)
    tokens, features = grad_attended.shape
    grad_queries, grad_keys, grad_values = attention_backward(
        queries3,
        blocks,
        query_pos,
        query_seg,
        log_total,
        mixed_heads,
        grad_attended.reshape(tokens, HEADS, features // HEADS),
    )
    key_grads, value_grads = (
        lax.psum_scatter(
            grad_keys.astype(jnp.bfloat16), "seq", scatter_dimension=0, tiled=True
        ).astype(jnp.float32),
        lax.psum_scatter(
            grad_values.astype(jnp.bfloat16), "seq", scatter_dimension=0, tiled=True
        ).astype(jnp.float32),
    )
    grad_joined = jnp.concatenate([grad_queries, key_grads, value_grads], axis=1).astype(
        jnp.bfloat16
    )
    grad_qkv = jnp.einsum("td,te->de", stream_low, grad_joined, preferred_element_type=jnp.float32)
    column_sums = jnp.sum(grad_joined.astype(jnp.float32), axis=0)
    bias_att = jnp.stack([column_sums[:features], column_sums[2 * features :], bias_att_out])
    grad_stream_in = grad_first + jnp.einsum(
        "te,de->td", grad_joined, qkv_weight, preferred_element_type=jnp.float32
    )
    layer_grads = (
        grad_qkv,
        grad_out,
        grad_ff_in,
        grad_ff_out,
        bias_att,
        bias_ff_in,
        bias_ff_out,
        jnp.stack([gain_first, gain_second]),
        jnp.stack([shift_first, shift_second]),
    )
    return (grad_stream_in, layer_grads)


def product(left, right):
    return lax.dot_general(left, right, (((1,), (0,)), ((), ())), preferred_element_type=jnp.float32)


def product_rows(left, right):
    return lax.dot_general(left, right, (((1,), (1,)), ((), ())), preferred_element_type=jnp.float32)


def product_tokens(left, right):
    return lax.dot_general(left, right, (((0,), (0,)), ((), ())), preferred_element_type=jnp.float32)


def wide(value):
    return value.astype(jnp.float32)


def low(value):
    return value.astype(jnp.bfloat16)


def normalize(values):
    centred = values - jnp.mean(values, axis=-1, keepdims=True)
    inverse = lax.rsqrt(jnp.mean(centred * centred, axis=-1, keepdims=True) + epsilon)
    return centred * inverse, inverse


def normalize_back(grad, normal, inverse, gain):
    scaled = grad * gain
    return (
        scaled
        - jnp.mean(scaled, axis=-1, keepdims=True)
        - normal * jnp.mean(scaled * normal, axis=-1, keepdims=True)
    ) * inverse


def column_sums(values):
    return jnp.sum(values, axis=0, keepdims=True)


def gelu_pair(v):
    rate = math.sqrt(2.0 / math.pi)
    square = v * v
    bent = jnp.tanh(v * (rate + (rate * 0.044715) * square))
    rise = 0.5 + 0.5 * bent
    slope = rise + v * (0.5 - 0.5 * bent * bent) * (rate + (3.0 * rate * 0.044715) * square)
    return v * rise, slope


class Gather:
    def __init__(self, geo, w, l, start, size, cut, sems, number):
        self.geo, self.w, self.l, self.start, self.size, self.cut = geo, w, l, start, size, cut
        (self.z_send, self.z_recv, self.x_send, self.x_recv, self.y_send, self.y_recv, self.xd_send, self.xd_recv,
         self.yd_send, self.yd_recv, self.c_send, self.c_recv) = (sem.at[number] for sem in sems)
        self.here = geo.here()
        z, last = self.here[0], geo.nz - 1
        self.back = [0]
        for n in range(last):
            below, above = n + 1, last - n
            half = n // 2
            between = 1 + half if n % 2 == 0 else last - half
            self.back.append(jnp.where(z == 0, above, jnp.where(z == last, below, between)))

    def at(self, n, i, j, low=None):
        geo, (z, x, y, c) = self.geo, self.here
        rows = (self.start, self.size)
        if low is not None:
            rows = (self.start + self.cut, self.size - self.cut) if low else (self.start, self.cut)
        return self.w.at[
            self.l,
            lax.rem(z + geo.nz - self.back[n], geo.nz),
            lax.rem(x + geo.nx - i, geo.nx),
            lax.rem(y + geo.ny - j, geo.ny),
            c,
            pl.ds(*rows),
        ]

    def z_copies(self, n):
        geo, (z, x, y, c) = self.geo, self.here
        back, piece = self.back[n], self.at(n, 0, 0)
        up = remote(
            piece, piece, self.z_send.at[0, n], self.z_recv.at[lax.rem(back + 1, geo.nz)],
            geo.device(lax.rem(z + 1, geo.nz), x, y, c),
        )
        down = remote(
            piece, piece, self.z_send.at[1, n], self.z_recv.at[lax.rem(back + geo.nz - 1, geo.nz)],
            geo.device(lax.rem(z + geo.nz - 1, geo.nz), x, y, c),
        )
        own = n == 0
        return [
            ((back <= z) & (z < geo.nz - 1), up),
            (((back > z) | own) & (z > 0), down),
        ]

    def z_arrival(self, n):
        piece, (z, x, y, c) = self.at(n, 0, 0), self.here
        return remote(
            piece, piece, self.z_send.at[0, n], self.z_recv.at[self.back[n]],
            self.geo.device(lax.rem(z + 1, self.geo.nz), x, y, c),
        )

    def x_copy(self, n, i):
        z, x, y, c = self.here
        piece = self.at(n, 0, 0)
        return remote(piece, piece, self.x_send.at[n, i - 1], self.x_recv.at[n, i - 1],
                      self.geo.device(z, lax.rem(x + i, self.geo.nx), y, c))

    def y_copy(self, n, j):
        z, x, y, c = self.here
        piece = self.at(n, 0, 0)
        return remote(piece, piece, self.y_send.at[n, j - 1], self.y_recv.at[n, j - 1],
                      self.geo.device(z, x, lax.rem(y + j, self.geo.ny), c))

    def x_forward(self, n, i, j):
        z, x, y, c = self.here
        piece, index = self.at(n, 0, j, True), (n, i - 1, j - 1)
        return remote(piece, piece, self.xd_send.at[index], self.xd_recv.at[index],
                      self.geo.device(z, lax.rem(x + i, self.geo.nx), y, c))

    def y_forward(self, n, i, j):
        z, x, y, c = self.here
        piece, index = self.at(n, i, 0, False), (n, i - 1, j - 1)
        return remote(piece, piece, self.yd_send.at[index], self.yd_recv.at[index],
                      self.geo.device(z, x, lax.rem(y + j, self.geo.ny), c))

    def c_copy(self, n):
        geo, (z, x, y, c) = self.geo, self.here
        piece = self.w.at[self.l, lax.rem(z + geo.nz - self.back[n], geo.nz), :, :, c, pl.ds(self.start, self.size)]
        return remote(piece, piece, self.c_send.at[n], self.c_recv.at[n], geo.device(z, x, y, 1 - c))

    def fan(self, n):
        for needed, copy in self.z_copies(n):
            pl.when(needed)(copy.start)
        for i in range(1, self.geo.nx):
            self.x_copy(n, i).start()
        for j in range(1, self.geo.ny):
            self.y_copy(n, j).start()

    def own(self):
        self.fan(0)

    def from_z(self, n):
        self.z_arrival(n).wait_recv()
        self.fan(n)

    def from_line(self, n):
        nx, ny = self.geo.nx, self.geo.ny
        for j in range(1, ny):
            self.y_copy(n, j).wait_recv()
            for i in range(1, nx):
                self.x_forward(n, i, j).start()
        for i in range(1, nx):
            self.x_copy(n, i).wait_recv()
            for j in range(1, ny):
                self.y_forward(n, i, j).start()

    def from_corner(self, n):
        for i in range(1, self.geo.nx):
            for j in range(1, self.geo.ny):
                self.x_forward(n, i, j).wait_recv()
                self.y_forward(n, i, j).wait_recv()
        self.c_copy(n).start()

    def steps(self):
        every = range(self.geo.nz)
        return [
            [functools.partial(self.from_z, n) for n in every if n],
            [functools.partial(self.from_line, n) for n in every],
            [functools.partial(self.from_corner, n) for n in every],
        ]

    def arrive(self):
        for n in range(self.geo.nz):
            self.c_copy(n).wait_recv()

    def finish(self):
        nx, ny = self.geo.nx, self.geo.ny
        for n in range(self.geo.nz):
            self.c_copy(n).wait_send()
            for needed, copy in self.z_copies(n):
                pl.when(needed)(copy.wait_send)
            for i in range(1, nx):
                self.x_copy(n, i).wait_send()
            for j in range(1, ny):
                self.y_copy(n, j).wait_send()
            for i in range(1, nx):
                for j in range(1, ny):
                    self.x_forward(n, i, j).wait_send()
                    self.y_forward(n, i, j).wait_send()

    @staticmethod
    def semaphores(geo, count):
        dma = pltpu.SemaphoreType.DMA
        nz, nx, ny = geo.nz, geo.nx, geo.ny
        return (
            [dma((count, 2, nz)), dma((count, nz))]
            + [dma((count, nz, nx - 1))] * 2
            + [dma((count, nz, ny - 1))] * 2
            + [dma((count, nz, nx - 1, ny - 1))] * 4
            + [dma((count, nz))] * 2
        )


class Scatter:
    def __init__(self, geo, g, own, r1h, r1l, r2h, r2l, zin, total, l, cut, sems, number):
        self.geo, self.g, self.own, self.l, self.cut = geo, g, own.at[l], l, cut
        self.r1h, self.r1l, self.r2h, self.r2l, self.zin = (ref.at[l] for ref in (r1h, r1l, r2h, r2l, zin))
        self.total = total
        self.rows = g.shape[4]
        self.sems = [sem.at[number] for sem in sems]
        self.z, self.x, self.y, self.c = geo.here()
        self.order = list(range(1, geo.nz)) + [0]

    def copy(self, src, dst, number, index, device):
        return remote(src, dst, self.sems[number].at[index], self.sems[number + 1].at[index], device)

    def cross(self, k):
        return self.copy(
            self.g.at[lax.rem(self.z + k, self.geo.nz), :, :, 1 - self.c], self.own.at[k], 0, (k,),
            self.geo.device(self.z, self.x, self.y, 1 - self.c),
        )

    def to_x(self, src, dst, number, index, i):
        return self.copy(src, dst, number, index, self.geo.device(self.z, lax.rem(self.x + i, self.geo.nx), self.y, self.c))

    def to_y(self, src, dst, number, index, j):
        return self.copy(src, dst, number, index, self.geo.device(self.z, self.x, lax.rem(self.y + j, self.geo.ny), self.c))

    def one(self, k):
        nx, ny = self.geo.nx, self.geo.ny
        top, rest = pl.ds(0, self.cut), pl.ds(self.cut, self.rows - self.cut)
        return [
            self.to_y(self.own.at[k, :, lax.rem(self.y + j, ny), top], self.r1h.at[k, j - 1], 2, (k, j - 1), j)
            for j in range(1, ny)
        ] + [
            self.to_x(self.own.at[k, lax.rem(self.x + i, nx), :, rest], self.r1l.at[k, i - 1], 4, (k, i - 1), i)
            for i in range(1, nx)
        ]

    def two(self, k):
        nx, ny = self.geo.nx, self.geo.ny
        top, rest = pl.ds(0, self.cut), pl.ds(self.cut, self.rows - self.cut)
        return [
            self.to_x(self.own.at[k, lax.rem(self.x + i, nx), self.y, top], self.r2h.at[k, i - 1], 6, (k, i - 1), i)
            for i in range(1, nx)
        ] + [
            self.to_y(self.own.at[k, self.x, lax.rem(self.y + j, ny), rest], self.r2l.at[k, j - 1], 8, (k, j - 1), j)
            for j in range(1, ny)
        ]

    def three(self, k):
        return self.copy(
            self.own.at[k, self.x, self.y], self.zin.at[k - 1], 10, (k - 1,),
            self.geo.device(lax.rem(self.z + k, self.geo.nz), self.x, self.y, self.c),
        )

    def begin(self):
        for k in self.order:
            self.cross(k).start()

    def step_one(self, k):
        own = self.own
        self.cross(k).wait()
        for i in range(self.geo.nx):
            for j in range(self.geo.ny):
                mine = self.g[lax.rem(self.z + k, self.geo.nz), i, j, self.c]
                own[k, i, j] = low(wide(mine) + wide(own[k, i, j]))
        for copy in self.one(k):
            copy.start()

    def step_two(self, k):
        own, x, y = self.own, self.x, self.y
        top, rest = pl.ds(0, self.cut), pl.ds(self.cut, self.rows - self.cut)
        for copy in self.one(k):
            copy.wait_recv()
        for i in range(self.geo.nx):
            total = wide(own[k, i, y, top])
            for j in range(1, self.geo.ny):
                total = total + wide(self.r1h[k, j - 1, i])
            own[k, i, y, top] = low(total)
        for j in range(self.geo.ny):
            total = wide(own[k, x, j, rest])
            for i in range(1, self.geo.nx):
                total = total + wide(self.r1l[k, i - 1, j])
            own[k, x, j, rest] = low(total)
        for copy in self.two(k):
            copy.start()

    def step_three(self, k):
        own, x, y = self.own, self.x, self.y
        top, rest = pl.ds(0, self.cut), pl.ds(self.cut, self.rows - self.cut)
        for copy in self.two(k):
            copy.wait_recv()
        upper = wide(own[k, x, y, top])
        for i in range(1, self.geo.nx):
            upper = upper + wide(self.r2h[k, i - 1])
        lower = wide(own[k, x, y, rest])
        for j in range(1, self.geo.ny):
            lower = lower + wide(self.r2l[k, j - 1])
        if k:
            own[k, x, y, top] = low(upper)
            own[k, x, y, rest] = low(lower)
            self.three(k).start()
        else:
            self.total[top] = upper
            self.total[rest] = lower

    def finish(self):
        total = self.total[...]
        for k in range(1, self.geo.nz):
            self.three(k).wait()
            total = total + wide(self.zin[k - 1])
        self.total[...] = total
        for k in self.order:
            for copy in self.one(k) + self.two(k):
                copy.wait_send()

    def steps(self):
        return [
            [functools.partial(step, k) for k in self.order]
            for step in (self.step_one, self.step_two, self.step_three)
        ]

    @staticmethod
    def buffers(geo, levels, rows, cut, columns, kind):
        vmem = pltpu.VMEM
        nz, nx, ny = geo.nz, geo.nx, geo.ny
        rest = rows - cut
        return [
            vmem((nz, nx, ny, 2, rows, columns), kind),
            vmem((levels, nz, nx, ny, rows, columns), kind),
            vmem((levels, nz, ny - 1, nx, cut, columns), kind),
            vmem((levels, nz, nx - 1, ny, rest, columns), kind),
            vmem((levels, nz, nx - 1, cut, columns), kind),
            vmem((levels, nz, ny - 1, rest, columns), kind),
            vmem((levels, nz - 1, rows, columns), kind),
            vmem((rows, columns), jnp.float32),
        ]

    @staticmethod
    def semaphores(geo, count):
        dma = pltpu.SemaphoreType.DMA
        nz, nx, ny = geo.nz, geo.nx, geo.ny
        return (
            [dma((count, nz))] * 2
            + [dma((count, nz, ny - 1))] * 2
            + [dma((count, nz, nx - 1))] * 2
            + [dma((count, nz, nx - 1))] * 2
            + [dma((count, nz, ny - 1))] * 2
            + [dma((count, nz - 1))] * 2
        )


ROW_ATT_BIAS, ROW_IN_BIAS, ROW_OUT_BIAS, ROW_GAIN, ROW_SHIFT, ROW_FINAL, ROWS = 0, 3, 7, 8, 10, 12, 16


def step_kernel(geo, cuts, half_a, half_f, *refs):
    refs = list(refs)

    def take(count):
        taken = refs[:count]
        del refs[:count]
        return taken

    (stream_in, residue_in, seg, cot, qkv_in, out_in, ff_in_in, ff_out_in, att_in, in_bias_in, out_bias_in, gain_in,
     shift_in, final_gain_in, final_shift_in) = take(15)
    (out, stream_grad, residue_grad, qkv_grad, out_grad, ff_in_grad, ff_out_grad, att_grad, in_bias_grad, out_bias_grad,
     gain_grad, shift_grad, final_gain_grad, final_shift_grad) = take(14)
    (w, par, own_small, xl_next, xn, qs, kv, kt, pt, att, mid, act, slope, n1, n2, i1, i2, bias, segs, dkv, ob, sb, sc,
     rb, rc, small, sbuf, sin) = take(28)
    buffers_a, buffers_f = take(8), take(8)
    gather_sems, scatter_sems = take(12), take(12)
    (load_sem, seg_send, seg_recv, y_send, y_recv, c_send, c_recv, by_send, by_recv, bc_send, bc_recv, s_send,
     s_recv, residue_sem) = take(14)
    assert not refs

    z, xx, y, c = geo.here()
    s = 2 * y + c
    shard = (z * geo.nx + xx) * geo.seq + s
    count = geo.seq
    tokens, features = residue_in.shape
    levels = w.shape[0]
    width = features // geo.shards
    ff_rows = in_bias_in.shape[1]
    head = features // HEADS
    lanes = 2 * head
    pairs = features // lanes
    parts = act.shape[1]
    sibling, across = geo.device(z, xx, y, 1 - c), geo.device(z, xx, 1 - y, c)
    row_in = 4 * width + ROWS
    row_out = row_in + parts * width
    xl = [stream_in] + [xl_next.at[l - 1] for l in range(1, levels)]

    pieces = [
        (
            Gather(geo, w, l, 0, row_in, cuts[0], gather_sems, 2 * l),
            Gather(geo, w, l, row_in, parts * width + ff_rows, cuts[1], gather_sems, 2 * l + 1),
        )
        for l in range(levels)
    ]
    sums = [
        (
            Scatter(geo, *buffers_a, l, half_a, scatter_sems, 2 * l),
            Scatter(geo, *buffers_f, l, half_f, scatter_sems, 2 * l + 1),
        )
        for l in range(levels)
    ]

    def own_loads(l):
        mine = w.at[l, z, xx, y, c]
        pairs_of = [(qkv_in.at[l, :, pl.ds(n * features, features)], n * width, width) for n in range(3)]
        pairs_of.append((out_in.at[l], 3 * width, width))
        for n in range(parts):
            pairs_of.append((ff_in_in.at[l, :, pl.ds(n * features, features)], row_in + n * width, width))
        pairs_of.append((ff_out_in.at[l], row_out, ff_rows))
        return [
            pltpu.make_async_copy(src, mine.at[pl.ds(start, size)], load_sem.at[l, n])
            for n, (src, start, size) in enumerate(pairs_of)
        ]

    for l in range(levels):
        for copy in own_loads(l):
            copy.start()
    lane = lax.broadcasted_iota(jnp.int32, (width, features), 1)
    place = low(jnp.where(lane == shard * width + lax.broadcasted_iota(jnp.int32, (width, features), 0), 1.0, 0.0))
    lane = lax.broadcasted_iota(jnp.int32, (ff_rows, features), 1)
    ff_lane = lax.rem(shard, features // ff_rows) * ff_rows
    ff_place = low(jnp.where(lane == ff_lane + lax.broadcasted_iota(jnp.int32, (ff_rows, features), 0), 1.0, 0.0))
    own_small[...] = jnp.zeros_like(own_small)
    for l in range(levels):
        for n in range(3):
            own_small[l, ROW_ATT_BIAS + n : ROW_ATT_BIAS + n + 1, :] = product(att_in[n, l : l + 1, :], place)
        spread = product(in_bias_in[l : l + 1, :], ff_place)
        for j in range(parts):
            own_small[l, ROW_IN_BIAS + j : ROW_IN_BIAS + j + 1, :] = jnp.where(z == j, spread, 0.0)
        own_small[l, ROW_OUT_BIAS : ROW_OUT_BIAS + 1, :] = product(out_bias_in[l : l + 1, :], place)
        own_small[l, ROW_GAIN : ROW_GAIN + 2, :] = product(gain_in[l], place)
        own_small[l, ROW_SHIFT : ROW_SHIFT + 2, :] = product(shift_in[l], place)
        own_small[l, ROW_FINAL : ROW_FINAL + 1, :] = product(final_gain_in[...], place)
        own_small[l, ROW_FINAL + 1 : ROW_FINAL + 2, :] = product(final_shift_in[...], place)
        w[l, z, xx, y, c, 4 * width : row_in, :] = low(own_small[l])

    segs[0] = jnp.broadcast_to(seg[...], segs.shape[1:])
    greet(
        [geo.device(lax.rem(z + k, geo.nz), xx, y, c) for k in range(1, geo.nz)]
        + [
            geo.device(z, lax.rem(xx + i, geo.nx), lax.rem(y + j, geo.ny), lax.rem(c + k, 2))
            for i in range(geo.nx)
            for j in range(geo.ny)
            for k in range(2)
            if i or j or k
        ]
    )
    line = [(z * geo.nx + xx, lax.rem(s + k, count)) for k in range(1, count)]

    def seg_copy(k):
        return remote(segs.at[0], segs.at[k], seg_send.at[k], seg_recv.at[k], line[k - 1])

    def y_copy(l):
        return remote(xl[l], xn.at[l], y_send.at[l], y_recv.at[l], across)

    def c_copy(l, src):
        return remote(kv.at[l, src], kv.at[l, 1], c_send.at[l], c_recv.at[l], sibling)

    def send_stream(l):
        @pl.when(y == 0)
        def _():
            y_copy(l).start()

    for copy in own_loads(0)[:4]:
        copy.wait()
    nz = geo.nz
    (first_a, first_f), (next_a, next_f) = pieces
    first_a.own()
    for copy in own_loads(0)[4:]:
        copy.wait()
    for k in range(1, count):
        seg_copy(k).start()
    send_stream(0)
    first_f.own()
    for copy in own_loads(1):
        copy.wait()

    waiting = []

    def tick(number):
        for _ in range(min(number, len(waiting))):
            waiting.pop(0)()

    def drain(last):
        while any(task is last for task in waiting):
            tick(1)

    steps = [piece.steps() for piece in (first_a, first_f, next_a, next_f)]
    waiting.extend(steps[0][0] + steps[0][1] + steps[1][0] + steps[0][2] + [next_a.own])
    waiting.extend(steps[1][1] + steps[2][0] + steps[1][2] + [next_f.own])
    waiting.extend(steps[2][1] + steps[3][0] + steps[2][2] + steps[3][1] + steps[3][2])
    last_step = {}
    for piece in (first_a, first_f, next_a, next_f):
        own_steps = [task for task in waiting if task.__class__ is functools.partial and task.func.__self__ is piece]
        last_step[piece] = own_steps[-1]

    @pl.when(y == 0)
    def _():
        for l in range(levels):
            xn[l] = jnp.zeros_like(xn[l])

    @pl.when(s == 0)
    def _():
        for l in range(levels):
            kv[l, 1] = jnp.zeros_like(kv[l, 1])

    for k in range(1, count):
        seg_copy(k).wait()
    query_seg = segs[0, 0:1, :]
    query_pos = s * tokens + lax.broadcasted_iota(jnp.int32, (tokens, tokens), 1)
    for b in range(3):
        block = lax.rem(s + count - b, count)
        key_seg = jnp.transpose(jnp.broadcast_to(wide(segs[b, 0:1, :]), (128, tokens)))[:, 0:1]
        key_pos = block * tokens + lax.broadcasted_iota(jnp.int32, (tokens, tokens), 0)
        allowed = (key_seg == wide(query_seg)) & (key_pos <= query_pos)
        bias[b] = jnp.where(allowed, 0.0, masked_value)
    for l in range(levels):
        small[l] = jnp.zeros_like(small[l])

    def weight(l, start):
        return w[l, :, :, :, :, pl.ds(start, width), :].reshape(features, features)

    def out_weight(l, j):
        return w[l, j, :, :, :, pl.ds(row_out, ff_rows), :].reshape(features, features)

    g_a, g_f = buffers_a[0], buffers_f[0]

    def keep(ref, start, value):
        ref[:, :, :, :, pl.ds(start, width), :] = low(value).reshape(nz, geo.nx, geo.ny, 2, width, features)

    def keep_out(j, value):
        g_f[j, :, :, :, pl.ds(parts * width, ff_rows), :] = low(value).reshape(geo.nx, geo.ny, 2, ff_rows, features)

    def row(l, index):
        return par[l, index : index + 1, :]

    pair_lane = lax.broadcasted_iota(jnp.int32, (1, lanes), 1)

    def one_head(value, side):
        return jnp.where((pair_lane < head) == (side == 0), value, jnp.zeros_like(value))

    def ready(piece):
        drain(last_step[piece])
        piece.arrive()

    x, r = stream_grad, out
    residue_load = pltpu.make_async_copy(residue_in, r, residue_sem)
    residue_load.start()

    def forward(l):
        ready(pieces[l][0])
        par[l] = jnp.sum(
            wide(w[l, :, :, :, :, pl.ds(4 * width, ROWS), :]).reshape(geo.shards, ROWS, features), axis=0
        )
        xv = xl[l][...]
        keys = product(xv, weight(l, width))
        values = product(xv, weight(l, 2 * width)) + row(l, ROW_ATT_BIAS + 1)
        kv[l, 0, :, 0:features] = low(keys)
        kv[l, 0, :, features:] = low(values)

        @pl.when(c == 0)
        def _():
            c_copy(l, 0).start()

        tick(2)
        queries = low(product(xv, weight(l, 0)) + row(l, ROW_ATT_BIAS))
        qs[l] = queries * (1.0 / math.sqrt(head))

        @pl.when(y == 1)
        def _():
            y_copy(l).wait_recv()

        xv = xn[l]
        keys = product(xv, weight(l, width))
        values = product(xv, weight(l, 2 * width)) + row(l, ROW_ATT_BIAS + 1)
        kv[l, 2, :, 0:features] = low(keys)
        kv[l, 2, :, features:] = low(values)

        @pl.when((y == 1) & (c == 1))
        def _():
            c_copy(l, 2).start()

        tick(2)

        @pl.when((y == 1) | (c == 1))
        def _():
            c_copy(l, 0).wait_recv()

        for b in range(3):
            kt[:, b * tokens : (b + 1) * tokens] = jnp.transpose(kv[l, b, :, features:])

        def attend(p, carry):
            at = pl.ds(pl.multiple_of(p * lanes, lanes), lanes)
            queries = qs[l, :, at]
            keys = kv[l, :, :, at].reshape(3 * tokens, lanes)
            for side in range(2):
                scores = product_rows(keys, one_head(queries, side)) + bias[...].reshape(3 * tokens, tokens)
                terms = jnp.exp(scores - jnp.max(scores, axis=0, keepdims=True))
                probs = low(terms * (1.0 / jnp.sum(terms, axis=0, keepdims=True)))
                pt[l, 2 * p + side] = probs
                rows = pl.ds(pl.multiple_of(p * lanes + side * head, head), head)
                ob[rows, :] = product(kt[rows, :], probs)
            return carry

        for half in range(2):
            lax.fori_loop(half * pairs // 2, (half + 1) * pairs // 2, attend, 0)
            tick(5)
        att[l] = low(jnp.transpose(ob[...]))
        branch = product(att[l], weight(l, 3 * width)) + row(l, ROW_ATT_BIAS + 2)
        normal, inverse = normalize((wide(stream_in[...]) if l == 0 else x[...]) + branch)
        n1[l] = normal
        i1[l] = inverse
        middle = normal * row(l, ROW_GAIN) + row(l, ROW_SHIFT)
        mid[l] = low(middle)
        x[...] = middle
        if l == 0:
            residue_load.wait()
        r[...] = r[...] + branch
        ready(pieces[l][1])
        total = jnp.broadcast_to(row(l, ROW_OUT_BIAS), (tokens, features))
        for j in range(parts):
            hidden = product(mid[l], weight(l, row_in + j * width)) + row(l, ROW_IN_BIAS + j)
            active, rise = gelu_pair(hidden)
            act[l, j] = low(active)
            slope[l, j] = low(rise)
            total = total + product(act[l, j], out_weight(l, j))
            tick(2)
        r[...] = r[...] + total
        normal, inverse = normalize(x[...] + total)
        n2[l] = normal
        i2[l] = inverse
        next_x = normal * row(l, ROW_GAIN + 1) + row(l, ROW_SHIFT + 1)
        x[...] = next_x
        if l + 1 < levels:
            xl[l + 1][...] = low(next_x)
            send_stream(l + 1)

    def note(l, index, value):
        small[l, index : index + 1, :] = value

    def by_copy(l):
        return remote(sc.at[l], rc.at[l], by_send.at[l], by_recv.at[l], across)

    def bc_copy(l):
        return remote(sb.at[l], rb.at[l], bc_send.at[l], bc_recv.at[l], sibling)

    gx = stream_grad
    block_lanes = features // nz
    last = levels - 1
    sum_ones, stores, ahead = {}, [], 3

    def queue_sum(scatter, store, l):
        one, two, three = scatter.steps()
        sum_ones[scatter] = one[-1]
        order = [
            stage[n - lag]
            for n in range(len(one) + 3)
            for stage, lag in ((one, 0), (two, 2), (three, 3))
            if 0 <= n - lag < len(one)
        ]
        left = waiting[:]
        waiting.clear()
        for n in range(ahead):
            waiting.append(order[n])
            waiting.extend(left[n : n + 1])
        waiting.extend(left[ahead:] + order[ahead:])
        waiting.extend(stores)
        stores[:] = [functools.partial(store, l)]

    def backward(l):
        sum_a, sum_f = sums[l]
        grad = gx[...]
        note(l, ROW_GAIN + 1, column_sums(grad * n2[l]))
        note(l, ROW_SHIFT + 1, column_sums(grad))
        g2 = normalize_back(grad, n2[l], i2[l], row(l, ROW_GAIN + 1))
        d_ff = low(g2 + residue_grad[...])
        if l < last:
            drain(sum_ones[sums[l + 1][1]])
        note(l, ROW_OUT_BIAS, column_sums(wide(d_ff)))
        total = g2
        for j in range(parts):
            keep_out(j, product_tokens(act[l, j], d_ff))
            d_hidden = low(product_rows(d_ff, out_weight(l, j)) * wide(slope[l, j]))
            sums_in = column_sums(wide(d_hidden))
            for q in range(parts):
                block = sums_in[:, q * block_lanes : (q + 1) * block_lanes]
                small[l, ROW_IN_BIAS + q : ROW_IN_BIAS + q + 1, j * block_lanes : (j + 1) * block_lanes] = block
            keep(g_f, j * width, product_tokens(mid[l], d_hidden))
            total = total + product_rows(d_hidden, weight(l, row_in + j * width))
            tick(2)
        sum_f.begin()
        note(l, ROW_GAIN, column_sums(total * n1[l]))
        note(l, ROW_SHIFT, column_sums(total))
        g1 = normalize_back(total, n1[l], i1[l], row(l, ROW_GAIN))
        gx[...] = g1
        d_att = low(g1 + residue_grad[...])
        note(l, ROW_ATT_BIAS + 2, column_sums(wide(d_att)))
        if l < last:
            drain(sum_ones[sums[l + 1][0]])
        keep(g_a, 3 * width, product_tokens(att[l], d_att))
        att[l] = low(product_rows(d_att, weight(l, 3 * width)))
        queue_sum(sum_f, store_f, l)
        tick(6)
        for b in range(3):
            kt[:, b * tokens : (b + 1) * tokens] = jnp.transpose(kv[l, b, :, 0:features])

        def attend(p, carry):
            start = pl.multiple_of(p * lanes, lanes)
            at, at_values = pl.ds(start, lanes), pl.ds(start + features, lanes)
            queries, d_out = qs[l, :, at], att[l, :, at]
            values = kv[l, :, :, at_values].reshape(3 * tokens, lanes)
            d_keys = jnp.zeros((3 * tokens, lanes), jnp.float32)
            d_values = jnp.zeros((3 * tokens, lanes), jnp.float32)
            for side in range(2):
                own = one_head(d_out, side)
                probs = pt[l, 2 * p + side]
                terms = product_rows(values, own)
                weighted = terms * wide(probs)
                d_scores = low(weighted - wide(probs) * jnp.sum(weighted, axis=0, keepdims=True))
                d_values = d_values + product(probs, own)
                d_keys = d_keys + product(d_scores, one_head(queries, side))
                rows = pl.ds(pl.multiple_of(p * lanes + side * head, head), head)
                ob[rows, :] = product(kt[rows, :], d_scores)
            for where, value in ((at, d_keys), (at_values, d_values)):
                dkv[0, :, where] = value[:tokens]
                sb[l, :, where] = low(value[tokens : 2 * tokens])
                dkv[1, :, where] = value[2 * tokens :]
            return carry

        for half in range(2):
            lax.fori_loop(half * pairs // 2, (half + 1) * pairs // 2, attend, 0)
            tick(2)

        @pl.when((c == 1) | (y == 1))
        def _():
            bc_copy(l).start()

        @pl.when((y == 1) & (c == 1))
        def _():
            bc_copy(l).wait_recv()
            dkv[1] = dkv[1] + wide(rb[l])

        far_keys, far_values = low(dkv[1, :, 0:features]), low(dkv[1, :, features:])

        @pl.when(y == 1)
        def _():
            sc[l] = low(product_rows(far_keys, weight(l, width)) + product_rows(far_values, weight(l, 2 * width)))
            by_copy(l).start()

        tick(1)
        d_queries = low(jnp.transpose(ob[...]) * (1.0 / math.sqrt(head)))
        keep(g_a, 0, product_tokens(xl[l][...], d_queries))
        note(l, ROW_ATT_BIAS, column_sums(wide(d_queries)))

        @pl.when(c == 0)
        def _():
            bc_copy(l).wait_recv()
            dkv[0] = dkv[0] + wide(rb[l])

        d_keys, d_values = low(dkv[0, :, 0:features]), low(dkv[0, :, features:])
        keep(g_a, width, product_tokens(xl[l][...], d_keys) + product_tokens(xn[l], far_keys))
        keep(g_a, 2 * width, product_tokens(xl[l][...], d_values) + product_tokens(xn[l], far_values))
        note(l, ROW_ATT_BIAS + 1, column_sums(wide(d_values)) + column_sums(wide(far_values)))
        sum_a.begin()
        tick(2)
        gx[...] = (
            gx[...]
            + product_rows(d_queries, weight(l, 0))
            + product_rows(d_keys, weight(l, width))
            + product_rows(d_values, weight(l, 2 * width))
        )
        queue_sum(sum_a, store_a, l)
        tick(2)

        @pl.when(y == 0)
        def _():
            by_copy(l).wait_recv()
            gx[...] = gx[...] + wide(rc[l])

    def store_f(l):
        sum_f = sums[l][1]
        sum_f.finish()
        for n in range(parts):
            ff_in_grad[l, :, n * features : (n + 1) * features] = sum_f.total[n * width : (n + 1) * width]
        ff_out_grad[l] = sum_f.total[parts * width :]

    def store_a(l):
        sum_a = sums[l][0]
        sum_a.finish()
        for n in range(3):
            qkv_grad[l, :, n * features : (n + 1) * features] = sum_a.total[n * width : (n + 1) * width]
        out_grad[l] = sum_a.total[3 * width :]

    for l in range(levels):
        forward(l)
    normal, inverse = normalize(r[...])
    gain = row(last, ROW_FINAL)
    out[...] = x[...] + normal * gain + row(last, ROW_FINAL + 1)
    grad = cot[...]
    note(last, ROW_FINAL, column_sums(grad * normal))
    note(last, ROW_FINAL + 1, column_sums(grad))
    residue_grad[...] = normalize_back(grad, normal, inverse, gain)
    gx[...] = grad
    for l in reversed(range(levels)):
        backward(l)

    z_peers = [geo.device(lax.rem(z + k, nz), xx, y, c) for k in range(1, nz)]
    plane = [
        geo.device(z, lax.rem(xx + i, geo.nx), lax.rem(y + j, geo.ny), lax.rem(c + k, 2))
        for i in range(geo.nx)
        for j in range(geo.ny)
        for k in range(2)
    ][1:]

    def z_small(k):
        return remote(
            sbuf.at[lax.rem(z + k, nz)], sin.at[k - 1], s_send.at[k - 1], s_recv.at[k - 1], z_peers[k - 1]
        )

    def plane_small(n):
        m = nz - 1 + n
        return remote(sbuf.at[nz], sin.at[m], s_send.at[m], s_recv.at[m], plane[n])

    for k in range(nz):
        sbuf[k] = small[:, :, k * block_lanes : (k + 1) * block_lanes].reshape(levels * ROWS, block_lanes)
    for k in range(1, nz):
        z_small(k).start()
    waiting.extend(stores)
    while len(waiting) > 2 * nz + 1:
        tick(1)
    total = sbuf[z]
    for k in range(1, nz):
        z_small(k).wait()
        total = total + sin[k - 1]
    sbuf[nz] = total
    for n in range(len(plane)):
        plane_small(n).start()
    tick(nz)
    total = sbuf[nz]
    for n in range(len(plane)):
        plane_small(n).wait()
        total = total + sin[nz - 1 + n]
    exact = functools.partial(jnp.dot, preferred_element_type=jnp.float32, precision=lax.Precision.HIGHEST)

    def chosen(lane_count, first, size):
        lane = lax.broadcasted_iota(jnp.int32, (lane_count, size), 0)
        return jnp.where(lane == first + lax.broadcasted_iota(jnp.int32, (lane_count, size), 1), 1.0, 0.0)

    mine = exact(total, chosen(block_lanes, lax.rem(shard, geo.shards // nz) * width, width))
    in_block = exact(total, chosen(block_lanes, lax.rem(ff_lane, block_lanes), ff_rows))
    part = lax.broadcasted_iota(jnp.int32, (ROWS, 1), 0)
    for l in range(levels):
        own = mine[l * ROWS : (l + 1) * ROWS]
        for n in range(3):
            att_grad[n, l : l + 1, :] = own[ROW_ATT_BIAS + n : ROW_ATT_BIAS + n + 1]
        in_rows = in_block[l * ROWS : (l + 1) * ROWS]
        in_bias_grad[l : l + 1, :] = column_sums(
            jnp.where(part == ROW_IN_BIAS + lax.div(ff_lane, block_lanes), in_rows, 0.0)
        )
        out_bias_grad[l : l + 1, :] = own[ROW_OUT_BIAS : ROW_OUT_BIAS + 1]
        gain_grad[l] = own[ROW_GAIN : ROW_GAIN + 2]
        shift_grad[l] = own[ROW_SHIFT : ROW_SHIFT + 2]
    final_gain_grad[...] = own[ROW_FINAL : ROW_FINAL + 1]
    final_shift_grad[...] = own[ROW_FINAL + 1 : ROW_FINAL + 2]
    while waiting:
        tick(1)

    for l in range(levels):
        for piece in pieces[l]:
            piece.finish()

        @pl.when(y == 0)
        def _(l=l):
            y_copy(l).wait_send()

        @pl.when((y == 1) | (c == 0))
        def _(l=l):
            c_copy(l, 0).wait_send()

        @pl.when((c == 1) | (y == 1))
        def _(l=l):
            bc_copy(l).wait_send()

        @pl.when(y == 1)
        def _(l=l):
            by_copy(l).wait_send()


def run_step(geo, stream_in, residue_in, seg, cot, shards):
    tokens, features = residue_in.shape
    levels, width, qkv_columns = shards[0].shape
    parts = shards[2].shape[2] // features
    ff_rows = shards[3].shape[1]
    rows_a, rows_f = 4 * width, parts * width + ff_rows
    shape = (geo.nz, geo.nx, geo.ny, 2)
    dma, vmem = pltpu.SemaphoreType.DMA, pltpu.VMEM
    wide_kind, kind = jnp.float32, jnp.bfloat16
    whole = pl.BlockSpec(memory_space=pltpu.VMEM)
    away = pl.BlockSpec(memory_space=pl.ANY)
    row = (tokens, features)
    half_a, half_f = 2 * width, 4 * width
    cuts = (2 * width, 3 * width)
    others = geo.nz - 1 + 2 * geo.nx * geo.ny - 1
    outs = [row, row, row] + [member.shape for member in shards]
    scratch = [
        vmem((levels,) + shape + (rows_a + ROWS + rows_f, features), kind),
        vmem((levels, ROWS, features), wide_kind),
        vmem((levels, ROWS, features), wide_kind),
        vmem((levels - 1,) + row, kind),
        vmem((levels,) + row, kind),
        vmem((levels,) + row, kind),
        vmem((levels, 3, tokens, 2 * features), kind),
        vmem((features, 3 * tokens), kind),
        vmem((levels, HEADS, 3 * tokens, tokens), kind),
        vmem((levels,) + row, kind),
        vmem((levels,) + row, kind),
        vmem((levels, parts) + row, kind),
        vmem((levels, parts) + row, kind),
        vmem((levels,) + row, wide_kind),
        vmem((levels,) + row, wide_kind),
        vmem((levels, tokens, 1), wide_kind),
        vmem((levels, tokens, 1), wide_kind),
        vmem((3, tokens, tokens), wide_kind),
        vmem((geo.seq, 8, tokens), jnp.int32),
        vmem((2, tokens, 2 * features), wide_kind),
        vmem((features, tokens), wide_kind),
        vmem((levels, tokens, 2 * features), kind),
        vmem((levels,) + row, kind),
        vmem((levels, tokens, 2 * features), kind),
        vmem((levels,) + row, kind),
        vmem((levels, ROWS, features), wide_kind),
        vmem((geo.nz + 1, levels * ROWS, features // geo.nz), wide_kind),
        vmem((others, levels * ROWS, features // geo.nz), wide_kind),
    ]
    scratch += Scatter.buffers(geo, levels, rows_a, half_a, features, kind)
    scratch += Scatter.buffers(geo, levels, rows_f, half_f, features, kind)
    scratch += Gather.semaphores(geo, 2 * levels) + Scatter.semaphores(geo, 2 * levels)
    scratch += [dma((levels, 5 + parts))] + [dma((geo.seq,))] * 2 + [dma((levels,))] * 8 + [dma((others,))] * 2 + [dma(())]
    return pl.pallas_call(
        functools.partial(step_kernel, geo, cuts, half_a, half_f),
        out_shape=tuple(jax.ShapeDtypeStruct(shape_of, wide_kind) for shape_of in outs),
        in_specs=[whole, away, whole, whole] + [away] * 4 + [whole] * 7,
        out_specs=(whole,) * len(outs),
        scratch_shapes=scratch,
        compiler_params=pltpu.CompilerParams(
            collective_id=0, has_side_effects=True, vmem_limit_bytes=64 << 20
        ),
        name="run_step",
    )(stream_in, residue_in, seg, cot, *shards)


def settle_kernel(count, *refs):
    sources, targets, held, (loads, stores) = refs[:count], refs[count : 2 * count], refs[2 * count : -2], refs[-2:]
    into = [pltpu.make_async_copy(src, buf, loads.at[n]) for n, (src, buf) in enumerate(zip(sources, held))]
    away = [pltpu.make_async_copy(buf, dst, stores.at[n]) for n, (buf, dst) in enumerate(zip(held, targets))]
    for copy in into:
        copy.start()
    for load, store in zip(into, away):
        load.wait()
        store.start()
    for copy in away:
        copy.wait()


def settle(values):
    count = len(values)
    away = pl.BlockSpec(memory_space=pl.ANY)
    return pl.pallas_call(
        functools.partial(settle_kernel, count),
        out_shape=tuple(jax.ShapeDtypeStruct(value.shape, value.dtype) for value in values),
        in_specs=[away] * count,
        out_specs=(away,) * count,
        scratch_shapes=[pltpu.VMEM(value.shape, value.dtype) for value in values]
        + [pltpu.SemaphoreType.DMA((count,))] * 2,
        name="settle",
    )(*values)


def gather_plain(shards, number):
    gathered = [
        lax.all_gather(shards[member][number], ("dp", "seq"), axis=axis, tiled=True)
        for member, axis in enumerate((0, 0, 0, 0, 1, 0, 0, 1, 1))
    ]
    return tuple(gathered) + tuple(
        lax.all_gather(shards[member], ("dp", "seq"), axis=0, tiled=True) for member in (9, 10)
    )


def body_plain(geo, *args):
    stream_in, residue_in, segments, out_cot = args[:4]
    shards = args[4:]
    levels, width, _ = shards[1].shape
    ff_width = shards[3].shape[1]
    stream = stream_in[0].astype(jnp.float32)
    residue = residue_in[0]
    cotangent = out_cot[0]
    tokens = stream.shape[0]
    query_seg = segments[0]
    whole_seg = lax.all_gather(query_seg, "seq", axis=0, tiled=True)
    seq_index = lax.axis_index("seq")
    query_pos = seq_index * tokens + jnp.arange(tokens, dtype=jnp.int32)
    weights = [gather_plain(shards, number) for number in range(levels)]
    states = []
    for number in range(levels):
        stream, residue, state = layer_forward(stream, residue, weights[number], query_pos, query_seg, whole_seg)
        states.append(state)
    final_norm, pull_final = jax.vjp(
        layer_norm,
        residue,
        weights[-1][9].astype(jnp.float32),
        weights[-1][10].astype(jnp.float32),
    )
    output = stream + final_norm
    grad_residue, final_gain_grad, final_shift_grad = pull_final(cotangent)
    grad_stream = cotangent
    grads = [None] * levels
    for number in reversed(range(levels)):
        grad_stream, grads[number] = layer_backward(
            states[number], weights[number], grad_stream, grad_residue, query_pos, query_seg
        )
    summed = [
        jnp.stack(
            [
                lax.psum_scatter(grads[number][member], ("dp", "seq"), scatter_dimension=axis, tiled=True)
                for number in range(levels)
            ]
        )
        for member, axis in enumerate((0, 0, 0, 0, 1, 0, 0, 1, 1))
    ] + [
        lax.psum_scatter(final_gain_grad, ("dp", "seq"), scatter_dimension=0, tiled=True),
        lax.psum_scatter(final_shift_grad, ("dp", "seq"), scatter_dimension=0, tiled=True),
    ]
    return (output[None], grad_stream[None], grad_residue[None]) + tuple(summed)


def body(geo, *args):
    stream_in, residue_in, segments, out_cot = args[:4]
    shards = list(args[4:])
    shards[4] = shards[4].transpose(1, 0, 2)
    shards[-2:] = [shards[-2][None], shards[-1][None]]
    results = list(settle(run_step(geo, stream_in[0], residue_in[0], segments, out_cot[0], shards)))
    results[7] = results[7].transpose(1, 0, 2)
    return tuple(value[None] for value in results[:3]) + tuple(results[3:-2]) + (results[-2][0], results[-1][0])


def solution(mesh):
    geo = Geometry(mesh)
    chosen = body if geo.seq == 4 and geo.nz == 4 else body_plain
    return jax.shard_map(
        functools.partial(chosen, geo),
        mesh=mesh,
        in_specs=(
            P("dp", "seq", None),
            P("dp", "seq", None),
            P("dp", "seq"),
            P("dp", "seq", None),
            P(None, ("dp", "seq"), None),
            P(None, ("dp", "seq"), None),
            P(None, ("dp", "seq"), None),
            P(None, ("dp", "seq"), None),
            P(None, None, ("dp", "seq")),
            P(None, ("dp", "seq")),
            P(None, ("dp", "seq")),
            P(None, None, ("dp", "seq")),
            P(None, None, ("dp", "seq")),
            P(("dp", "seq")),
            P(("dp", "seq")),
        ),
        out_specs=(
            P("dp", "seq", None),
            P("dp", "seq", None),
            P("dp", "seq", None),
            P(None, ("dp", "seq"), None),
            P(None, ("dp", "seq"), None),
            P(None, ("dp", "seq"), None),
            P(None, ("dp", "seq"), None),
            P(None, None, ("dp", "seq")),
            P(None, ("dp", "seq")),
            P(None, ("dp", "seq")),
            P(None, None, ("dp", "seq")),
            P(None, None, ("dp", "seq")),
            P(("dp", "seq")),
            P(("dp", "seq")),
        ),
        check_vma=False,
    )
```
